32 devices in a mesh: seq: 4 (over y, x), fsdp: 8 (over z, core).
Axes of the slice: x: 2, y: 2, z: 4, core: 2. Of those that a mesh axis runs over, the one named last changes fastest.
Arguments:
- tokens: bfloat16 [16, 512, 1024], P('fsdp', 'seq')
- cotangent: bfloat16 [16, 512, 1024], P('fsdp', 'seq'), may hold values from -6 to 6
- prefix: int32 [16], P('fsdp'), may hold values from 51 to 256, as said below
- qkv_weight: bfloat16 [1024, 3072], P('fsdp', 'seq'), may hold values from -0.1875 to 0.1875
- out_weight: bfloat16 [1024, 1024], P('fsdp', 'seq'), may hold values from -0.75 to 0.75
- up_weight: bfloat16 [1024, 4096], P('fsdp', 'seq'), may hold values from -0.1875 to 0.1875
- down_weight: bfloat16 [4096, 1024], P('fsdp', 'seq'), may hold values from -0.09375 to 0.09375
- norm_gains: bfloat16 [4, 1024], P(None, 'fsdp'), may hold values from 0.5 to 1.5
Outputs:
- output: bfloat16 [16, 512, 1024], P('fsdp', 'seq')
- input_grad: bfloat16 [16, 512, 1024], P('fsdp', 'seq')
- qkv_grad: float32 [1024, 3072], P('fsdp', 'seq')
- out_grad: float32 [1024, 1024], P('fsdp', 'seq')
- up_grad: float32 [1024, 4096], P('fsdp', 'seq')
- down_grad: float32 [4096, 1024], P('fsdp', 'seq')
- gains_grad: float32 [4, 1024], P(None, 'fsdp')
- stream_rms: float32 [4], replicated
The draws below stay inside these ranges and needn't reach their ends.
Inputs may be any that keep to these rules, and one draw needn't show every extreme that they name: `prefix`: prefix length of each sequence; some sequence has 256 and another has 51.
All inputs are finite; a program needn't handle non-finite values.
Results may differ from the reference program's by a relative error of at most 0.022.
Values may be sent and summed in bfloat16 or wider, within the bound.
No kernel may reach another device: no remote copies, remote signals or barrier semaphores. Data moves between devices by JAX's collectives and lax.ppermute only.
A program may use at most 192 MiB of HBM per device.

```python
from functools import partial
import jax
import jax.numpy as jnp
from jax import lax

D = 1024
HEADS = 16
HEAD = 64
FF = 4096
L = 512
SEQS = 16


def draw_tokens(key, part):
    seq_place = jnp.arange(SEQS, dtype=jnp.float32)[:, None, None] / max(SEQS - 1, 1)
    row_place = jnp.arange(L, dtype=jnp.float32)[None, :, None] / (L - 1)
    base = jnp.clip(jax.random.normal(key, (SEQS, L, D), jnp.float32), -6.0, 6.0)
    return (base * 0.5 * 3.5 ** (seq_place + row_place)).astype(jnp.bfloat16)


def draw_prefix(key, part):
    first_key, second_key = jax.random.split(jax.random.fold_in(key, 7))
    lengths = jax.random.randint(first_key, (SEQS,), L // 10, L // 2 + 1, dtype=jnp.int32)
    chosen = jax.random.randint(second_key, (), 0, SEQS, dtype=jnp.int32)
    lengths = lengths.at[chosen].set(L // 2)
    return lengths.at[(chosen + 1) % SEQS].set(L // 10)


def level_of(rng, shape, shards, least, high):
    def one(dim, parts):
        draws = jax.random.uniform(jax.random.fold_in(jax.random.fold_in(rng, 6), dim), (parts,), jnp.float32, least / len(shards), high / len(shards))
        return jnp.repeat(jnp.exp(draws), shape[dim] // parts).reshape((-1,) + (1,) * (len(shape) - dim - 1))

    gain = one(*shards[0])
    for cut in shards[1:]:
        gain = gain * one(*cut)
    return gain


def bell_draw(rng, dims, scale, limit, cuts=(), held_as=jnp.bfloat16):
    gain = level_of(rng, dims, cuts, -0.22, 0.18) if cuts else 1.0
    entries = jax.random.normal(rng, dims, jnp.float32) * scale * gain
    return jnp.minimum(jnp.maximum(entries, -limit), limit).astype(held_as)


def setup_inputs(seed: int = 0) -> dict:
    streams_of = jax.random.split(jax.random.key(seed), 9)
    return {
        "tokens": draw_tokens(jax.random.fold_in(streams_of[8], 71), 0),
        "cotangent": bell_draw(streams_of[1], (SEQS, L, D), 1.0, 6.0, ((0, 8), (1, 4))),
        "prefix": draw_prefix(jax.random.fold_in(streams_of[8], 71), 0),
        "qkv_weight": bell_draw(streams_of[3], (D, 3 * D), D ** -0.5, 0.1875, ((0, 8), (1, 4))),
        "out_weight": bell_draw(streams_of[4], (D, D), (D // 16) ** -0.5, 0.75, ((0, 8), (1, 4))),
        "up_weight": bell_draw(streams_of[5], (D, FF), D ** -0.5, 0.1875, ((0, 8), (1, 4))),
        "down_weight": bell_draw(streams_of[6], (FF, D), FF ** -0.5, 0.09375, ((0, 8), (1, 4))),
        "norm_gains": jnp.clip(1.0 + 0.1 * jax.random.normal(streams_of[7], (4, D), jnp.float32), 0.5, 1.5).astype(jnp.bfloat16),
    }


NORM_EPSILON = 1e-05
MASKED_SCORE = -1e+30

@jax.custom_vjp
def low(v):
    return lax.optimization_barrier(v.astype(jnp.bfloat16)).astype(jnp.float32)

@jax.custom_vjp
def low_back(v):
    return v

def low_keep(v):
    return (low(v), None)

def low_pass(kept, grad):
    return (grad,)

def back_keep(v):
    return (v, None)

def back_low(kept, grad):
    return (low(grad),)
low.defvjp(low_keep, low_pass)
low_back.defvjp(back_keep, back_low)

def rounded_both(values):
    return low(low_back(values))

def normalize(values, scales):
    centre = lax.optimization_barrier(jnp.mean(values, axis=-1, keepdims=True))
    shifted = values - centre
    spread = lax.optimization_barrier(jnp.mean(shifted * shifted, axis=-1, keepdims=True))
    return shifted * lax.rsqrt(spread + NORM_EPSILON) * scales

def highest(former, latter):
    return jnp.dot(former, latter, precision=lax.Precision.HIGHEST, preferred_element_type=jnp.float32)

def attend_whole(operands):
    queries, keys_all, values_all, prefix_len = operands
    length = queries.shape[0]
    query_heads = queries.reshape(length, HEADS, HEAD)
    key_heads = keys_all.reshape(length, HEADS, HEAD)
    value_heads = values_all.reshape(length, HEADS, HEAD)
    scores = jnp.einsum('qhd,khd->hqk', query_heads, key_heads, precision=lax.Precision.HIGHEST) * HEAD ** (-0.5)
    scores = low_back(scores)
    position = jnp.arange(length, dtype=jnp.int32)
    allowed = (position[None, :] <= position[:, None]) | (position[None, :] < prefix_len)
    scores = jnp.where(allowed[None], scores, MASKED_SCORE)
    largest = lax.optimization_barrier(jnp.max(scores, axis=-1, keepdims=True))
    weights = jnp.exp(scores - largest)
    probs = low(weights / lax.optimization_barrier(jnp.sum(weights, axis=-1, keepdims=True)))
    mixed = jnp.einsum('hqk,khd->qhd', probs, value_heads, precision=lax.Precision.HIGHEST)
    return mixed.reshape(length, D)

def forward(tokens_f, qkv_f, out_f, up_f, down_f, gains_f, prefix):
    flat_rows = tokens_f.reshape(SEQS * L, D)
    first = low(normalize(flat_rows, gains_f[0]))
    mixed = rounded_both(highest(first, qkv_f))
    queries = mixed[:, :D].reshape(SEQS, L, D)
    keys_all = mixed[:, D:2 * D].reshape(SEQS, L, D)
    values_all = mixed[:, 2 * D:].reshape(SEQS, L, D)
    attended = lax.map(jax.checkpoint(attend_whole), (queries, keys_all, values_all, prefix))
    attended = rounded_both(attended.reshape(SEQS * L, D))
    raw = low_back(highest(attended, out_f))
    second = normalize(raw, gains_f[1])
    middle = flat_rows + second
    third = low(normalize(middle, gains_f[2]))
    hidden = low_back(highest(third, up_f))
    active = low(jax.nn.gelu(hidden, approximate=True))
    down = low_back(highest(active, down_f))
    fourth = normalize(down, gains_f[3])
    result = middle + fourth
    return (result.reshape(SEQS, L, D), (middle, second, fourth))

def reference(tokens, cotangent, prefix, qkv_weight, out_weight, up_weight, down_weight, norm_gains):
    primals = (tokens.astype(jnp.float32), qkv_weight.astype(jnp.float32), out_weight.astype(jnp.float32), up_weight.astype(jnp.float32), down_weight.astype(jnp.float32), norm_gains.astype(jnp.float32))
    result, pull_back, extras = jax.vjp(partial(forward, prefix=prefix), *primals, has_aux=True)
    middle, second, fourth = extras
    grads = pull_back(cotangent.astype(jnp.float32))
    stream_rms = jnp.stack([jnp.sqrt(jnp.mean(middle * middle)), jnp.sqrt(jnp.mean(result * result)), jnp.sqrt(jnp.mean(second * second)), jnp.sqrt(jnp.mean(fourth * fourth))])
    return (result.astype(jnp.bfloat16), grads[0].astype(jnp.bfloat16), grads[1], grads[2], grads[3], grads[4], grads[5], stream_rms)
```

```python
import math
from functools import partial

import jax
import jax.numpy as jnp
from jax import lax
from jax.experimental import pallas as pl
from jax.experimental.pallas import tpu as pltpu
from jax.sharding import PartitionSpec as P

HEAD = 64
NORM_EPSILON = 1e-05
MASKED_SCORE = -1e30
VMEM_LIMIT = 56 * 1024 * 1024
BF = jnp.bfloat16
F32 = jnp.float32
BLOCK_ORDER = (0, 1, 2, 4, 6, 3, 5, 7)
EXTRA = 16
COST = 0.001


def dot_nn(a, b):
    return lax.dot_general(a, b, (((1,), (0,)), ((), ())), preferred_element_type=F32)


def dot_nt(a, b):
    return lax.dot_general(a, b, (((1,), (1,)), ((), ())), preferred_element_type=F32)


def dot_tn(a, b):
    return lax.dot_general(a, b, (((0,), (0,)), ((), ())), preferred_element_type=F32)


def norm_parts(v):
    centre = jnp.mean(v, axis=-1, keepdims=True)
    shifted = v - centre
    spread = jnp.mean(shifted * shifted, axis=-1, keepdims=True)
    scale = lax.rsqrt(spread + NORM_EPSILON)
    return shifted * scale, scale


def norm_back(grad_unit, unit, scale):
    first = jnp.mean(grad_unit, axis=-1, keepdims=True)
    second = jnp.mean(grad_unit * unit, axis=-1, keepdims=True)
    return scale * (grad_unit - first - unit * second)


def seq_place():
    return lax.axis_index("seq").astype(jnp.int32)


def block_places(F):
    if F != 8:
        return [jnp.int32(i) for i in range(F)]
    place = lax.axis_index("fsdp").astype(jnp.int32)
    return [place ^ i for i in BLOCK_ORDER]


class Mover:
    def __init__(self, sems):
        self.sems = sems
        self.used = 0

    def start(self, src, dst):
        copy = pltpu.make_async_copy(src, dst, self.sems.at[self.used])
        self.used += 1
        copy.start()
        return copy


def wait_all(copies):
    for copy in copies:
        copy.wait()


def load_rows(mover, pieces, target, me):
    r = pieces[0].shape[0]
    copies = []
    for slot, piece in enumerate(pieces):
        start = pl.multiple_of((me ^ slot) * r, r)
        copies.append(mover.start(piece, target.at[pl.ds(start, r)]))
    return copies


def store_rows(mover, source, outs, order, me):
    r = outs[0].shape[1]
    copies = []
    for group, out in zip(order, outs):
        for i, slot in enumerate(group):
            start = pl.multiple_of((me ^ slot) * r, r)
            copies.append(mover.start(source.at[pl.ds(start, r)], out.at[i]))
    return copies


def load_blocks(mover, stacks, target, tiles):
    F = sum(stack.shape[0] for stack in stacks)
    places, copies, index = block_places(F), [], 0
    rows = target.shape[0] // F
    for stack in stacks:
        cols = stack.shape[2]
        for i in range(stack.shape[0]):
            start = pl.multiple_of(places[index] * rows, rows)
            index += 1
            for t in range(tiles):
                copies.append(
                    mover.start(
                        stack.at[i, pl.ds(t * rows, rows)],
                        target.at[pl.ds(start, rows), pl.ds(t * cols, cols)],
                    )
                )
    return copies


def load_gains(mover, stacks, target):
    F = sum(stack.shape[0] for stack in stacks)
    places, copies, index = block_places(F), [], 0
    width = target.shape[1] // F
    for stack in stacks:
        last = stack.shape[1] - EXTRA
        for i in range(stack.shape[0]):
            start = pl.multiple_of(places[index] * width, width)
            index += 1
            copies.append(
                mover.start(
                    stack.at[i, pl.ds(last, EXTRA), pl.ds(0, width)],
                    target.at[:, pl.ds(start, width)],
                )
            )
    return copies


def any_spec():
    return pl.BlockSpec(memory_space=pl.ANY)


def hbm_spec():
    return pl.BlockSpec(memory_space=pltpu.HBM)


def smem_spec():
    return pl.BlockSpec(memory_space=pltpu.SMEM)


def vmem_spec():
    return pl.BlockSpec(memory_space=pltpu.VMEM)


def call(body, operands, in_specs, outs, out_specs, scratch, flops, bytes_accessed, name):
    return pl.pallas_call(
        body,
        out_shape=tuple(jax.ShapeDtypeStruct(shape, dtype) for shape, dtype in outs),
        in_specs=in_specs,
        out_specs=tuple(out_specs),
        scratch_shapes=scratch,
        compiler_params=pltpu.CompilerParams(vmem_limit_bytes=VMEM_LIMIT),
        cost_estimate=pl.CostEstimate(
            flops=int(flops * COST), bytes_accessed=int(bytes_accessed * COST), transcendentals=0
        ),
        name=name,
    )(*operands)


def attend_kernel(dims, count, turn, packed, prefix, *refs):
    S, F, r, D, heads = dims
    L, W = S * r, heads * HEAD
    if packed:
        gains_in = None
    else:
        gains_in, refs = refs[0], refs[1:]
    weights, pieces, refs = refs[:count], refs[count : count + S], refs[count + S :]
    a_out, qkv_out, o_out, p_out, gains_out, refs = *refs[:5], refs[5:]
    x_s, w_s, a_s, qkv_s, o_s, p_s, bias_s, raw_s, sems = refs
    me, limit_len = seq_place(), prefix[turn]
    mover = Mover(sems)
    gain_loads = load_gains(mover, weights, raw_s) if packed else []
    loads = load_rows(mover, pieces, x_s, me)
    weight_loads = load_blocks(mover, weights, w_s, 3)
    tile = 128
    limit = L // 2
    for i in range(L // tile):
        shape = (tile, max((i + 1) * tile, limit))
        rows = i * tile + lax.broadcasted_iota(jnp.int32, shape, 0)
        cols = lax.broadcasted_iota(jnp.int32, shape, 1)
        seen = (cols <= rows) | (cols < limit_len)
        bias_s[i * tile : i * tile + tile, : shape[1]] = jnp.where(seen, 0.0, MASKED_SCORE)
    wait_all(gain_loads)
    gains_out[...] = raw_s[0:8, :].astype(F32) if packed else gains_in[...]
    wait_all(loads)
    for i in range(L // tile):
        rows = slice(i * tile, i * tile + tile)
        unit, scale = norm_parts(x_s[rows, :].astype(F32))
        a_s[rows, :] = (unit * gains_out[0:1, :]).astype(BF)
    stores = [mover.start(a_s, a_out)]
    wait_all(weight_loads)
    for c in range(3):
        cols = slice(c * W, c * W + W)
        qkv_s[:, cols] = dot_nn(a_s[...], w_s[:, cols]).astype(BF)
    stores.append(mover.start(qkv_s, qkv_out))
    lane = lax.broadcasted_iota(jnp.int32, (1, 128), 1)
    for pair in range(heads // 2):
        q2 = qkv_s[:, pair * 128 : pair * 128 + 128] * BF(HEAD**-0.5)
        k2 = qkv_s[:, W + pair * 128 : W + pair * 128 + 128]
        v2 = qkv_s[:, 2 * W + pair * 128 : 2 * W + pair * 128 + 128]
        keys, values = [], []
        for side in range(2):
            mine = (lane >= 64) if side else (lane < 64)
            keys.append(jnp.where(mine, k2, BF(0)))
            values.append(jnp.where(mine, v2, BF(0)))
        for i in range(L // tile):
            rows = slice(i * tile, i * tile + tile)
            span = max((i + 1) * tile, limit)
            total = None
            for side in range(2):
                scores = dot_nt(q2[rows], keys[side][:span]) + bias_s[rows, :span]
                top = jnp.max(scores, axis=-1, keepdims=True)
                weights_here = jnp.exp(scores - top)
                share = 1.0 / jnp.sum(weights_here, axis=-1, keepdims=True)
                probs = (weights_here * share).astype(BF)
                p_s[2 * pair + side, rows, :span] = probs
                part = dot_nn(probs, values[side][:span])
                total = part if total is None else total + part
            o_s[rows, pair * 128 : pair * 128 + 128] = total.astype(BF)
        for side in range(2):
            stores.append(mover.start(p_s.at[2 * pair + side], p_out.at[2 * pair + side]))
    stores.append(mover.start(o_s, o_out))
    wait_all(stores)


def attend(dims, turn, prefix, gains, weights, pieces):
    S, F, r, D, heads = dims
    L, W = S * r, heads * HEAD
    outs = [((L, D), BF), ((L, 3 * W), BF), ((L, W), BF), ((heads, L, L), BF), ((8, D), F32)]
    scratch = [
        pltpu.VMEM((L, D), BF),
        pltpu.VMEM((D, 3 * W), BF),
        pltpu.VMEM((L, D), BF),
        pltpu.VMEM((L, 3 * W), BF),
        pltpu.VMEM((L, W), BF),
        pltpu.VMEM((heads, L, L), BF),
        pltpu.VMEM((L, L), F32),
        pltpu.VMEM((EXTRA, D), BF),
        pltpu.SemaphoreType.DMA((S + 4 * F + heads + 3,)),
    ]
    flops = 2 * L * D * 3 * W + 4 * heads * L * L * HEAD * 4
    size = 2 * (2 * L * D + 3 * D * W + 4 * L * W + heads * L * L)
    packed = gains is None
    extra = [] if packed else [gains]
    return call(
        partial(attend_kernel, dims, len(weights), turn, packed),
        (prefix, *extra, *weights, *pieces),
        [smem_spec()]
        + [vmem_spec()] * len(extra)
        + [any_spec()] * (len(weights) + len(pieces)),
        outs,
        [hbm_spec()] * 4 + [vmem_spec()],
        scratch,
        flops,
        size,
        "attend",
    )


def attend_back_kernel(dims, count, order, gains, *refs):
    S, F, r, D, heads = dims
    n = len(order)
    L, W = S * r, heads * HEAD
    weights, refs = refs[:count], refs[count:]
    a_in, qkv, probs_in, pieces, refs = *refs[:3], refs[3 : 3 + S], refs[3 + S :]
    grad_out, stat_out, slots, refs = *refs[:2], refs[2 : 2 + n], refs[2 + n :]
    w_s, qkv_s, p_s, do_s, d_s, grad_s, part_s, a_s, sems = refs
    me = seq_place()
    mover = Mover(sems)
    loads = load_rows(mover, pieces, do_s, me)
    loads.append(mover.start(qkv, qkv_s))
    prob_loads = [mover.start(probs_in.at[h], p_s.at[h]) for h in range(heads)]
    late_loads = load_blocks(mover, weights, w_s, 3)
    late_loads.append(mover.start(a_in, a_s))
    tile = 128
    limit = L // 2
    wait_all(loads)
    lane = lax.broadcasted_iota(jnp.int32, (1, 128), 1)
    for pair in range(heads // 2):
        cols = slice(pair * 128, pair * 128 + 128)
        q2 = qkv_s[:, cols] * BF(HEAD**-0.5)
        k2 = qkv_s[:, W + pair * 128 : W + pair * 128 + 128] * BF(HEAD**-0.5)
        v2 = qkv_s[:, 2 * W + pair * 128 : 2 * W + pair * 128 + 128]
        do2 = do_s[:, cols]
        queries, keys, values, grads = [], [], [], []
        for side in range(2):
            mine = (lane >= 64) if side else (lane < 64)
            queries.append(jnp.where(mine, q2, BF(0)))
            keys.append(jnp.where(mine, k2, BF(0)))
            values.append(jnp.where(mine, v2, BF(0)))
            grads.append(jnp.where(mine, do2, BF(0)))
            prob_loads[2 * pair + side].wait()
        for i in range(L // tile):
            rows = slice(i * tile, i * tile + tile)
            span = max((i + 1) * tile, limit)
            total = None
            for side in range(2):
                probs = p_s[2 * pair + side, rows, :span].astype(F32)
                grad_probs = dot_nt(do2[rows], values[side][:span])
                delta = jnp.sum(probs * grad_probs, axis=-1, keepdims=True)
                grad_scores = (probs * (grad_probs - delta)).astype(BF)
                d_s[side, rows, :span] = grad_scores
                part = dot_nn(grad_scores, keys[side][:span])
                total = part if total is None else total + part
            grad_s[rows, cols] = total.astype(BF)
        for j in range(L // tile):
            columns = slice(j * tile, j * tile + tile)
            low = 0 if (j * tile) < limit else j * tile
            total_k, total_v = None, None
            for side in range(2):
                part = dot_tn(d_s[side, low:, columns], queries[side][low:])
                total_k = part if total_k is None else total_k + part
                part = dot_tn(p_s[2 * pair + side, low:, columns], grads[side][low:])
                total_v = part if total_v is None else total_v + part
            grad_s[columns, W + pair * 128 : W + pair * 128 + 128] = total_k.astype(BF)
            grad_s[columns, 2 * W + pair * 128 : 2 * W + pair * 128 + 128] = total_v.astype(BF)
    stores = [mover.start(grad_s, grad_out)]
    wait_all(late_loads)
    wide = 256
    stat_out[...] = jnp.zeros_like(stat_out)

    for c in range(D // wide):
        cols = slice(c * wide, c * wide + wide)
        part = dot_nt(grad_s[...], w_s[cols, :])
        part_s[:, cols] = part.astype(BF)
        stat_out[0:1, cols] = column_sum(part * a_s[:, cols].astype(F32)) / gains[0:1, cols]
    stores += store_rows(mover, part_s, slots, order, me)
    wait_all(stores)


def attend_back(dims, turn, gains, weights, a, qkv, probs, pieces):
    S, F, r, D, heads = dims
    L, W = S * r, heads * HEAD
    outs = [((L, 3 * W), BF), ((8, D), F32)] + slot_shapes(S, turn, (r, D))
    blocks = 3 * F
    scratch = [
        pltpu.VMEM((D, 3 * W), BF),
        pltpu.VMEM((L, 3 * W), BF),
        pltpu.VMEM((heads, L, L), BF),
        pltpu.VMEM((L, W), BF),
        pltpu.VMEM((2, L, L), BF),
        pltpu.VMEM((L, 3 * W), BF),
        pltpu.VMEM((L, D), BF),
        pltpu.VMEM((L, D), BF),
        pltpu.SemaphoreType.DMA((2 * S + heads + 3 + blocks,)),
    ]
    flops = 2 * L * D * 3 * W + 8 * heads * L * L * HEAD * 4
    size = 2 * (2 * L * D + 3 * D * W + 7 * L * W + heads * L * L)
    return call(
        partial(attend_back_kernel, dims, len(weights), slot_order(S, turn)),
        (gains, *weights, a, qkv, probs, *pieces),
        [vmem_spec()]
        + [any_spec()] * (3 + len(weights) + len(pieces)),
        outs,
        [hbm_spec(), vmem_spec()] + [hbm_spec()] * (len(outs) - 2),
        scratch,
        flops,
        size,
        "attend_back",
    )


def project_kernel(dims, first_call, gains, *refs):
    S, F, r, D, W = dims
    L = S * r
    if first_call:
        weights, refs = refs[:S], refs[S:]
    else:
        weights, refs = refs[0], refs[1:]
    xs, os, refs = refs[:S], refs[S : 2 * S], refs[2 * S :]
    b_out, u_own, h_own = refs[:3]
    refs = refs[3:]
    if first_call:
        w_out, refs = refs[0], refs[1:]
    x_s, o_s, w_s, u_s, h_s, b_s, sems = refs
    me = seq_place()
    places = block_places(F)
    mover = Mover(sems)
    loads, stores = [], []
    for slot in range(S):
        start = pl.multiple_of((me ^ slot) * W, W)
        loads.append(mover.start(os[slot], o_s.at[:, pl.ds(start, W)]))
        if first_call:
            rows = weights[slot].shape[1]
            for i in range(weights[slot].shape[0]):
                place = pl.multiple_of(places[i] * rows, rows)
                loads.append(
                    mover.start(
                        weights[slot].at[i], w_s.at[pl.ds(place, rows), pl.ds(start, W)]
                    )
                )
    if not first_call:
        loads.append(mover.start(weights, w_s))
    x_loads = load_rows(mover, xs, x_s, me)
    wide = 256
    wait_all(loads)
    if first_call:
        stores.append(mover.start(w_s, w_out))

    wait_all(x_loads)
    tall = 256
    for i in range(L // tall):
        rows = slice(i * tall, i * tall + tall)
        for c in range(D // wide):
            cols = slice(c * wide, c * wide + wide)
            u_s[rows, cols] = dot_nn(o_s[rows, :], w_s[:, cols])
        unit, scale = norm_parts(u_s[rows, :])
        h = x_s[rows, :].astype(F32) + unit * gains[1:2, :]
        h_s[rows, :] = h
        unit, scale = norm_parts(h)
        b_s[rows, :] = (unit * gains[2:3, :]).astype(BF)
    own = pl.ds(pl.multiple_of(me * r, r), r)
    stores += [
        mover.start(b_s, b_out),
        mover.start(u_s.at[own], u_own),
        mover.start(h_s.at[own], h_own),
    ]
    wait_all(stores)


def project(dims, gains, weights, xs, os):
    S, F, r, D, W = dims
    L = S * r
    first_call = isinstance(weights, list)
    outs = [((L, D), BF), ((r, D), F32), ((r, D), F32)]
    if first_call:
        outs.append(((D, D), BF))
    operands = weights if first_call else [weights]
    blocks = S * weights[0].shape[0] if first_call else 1
    scratch = [
        pltpu.VMEM((L, D), BF),
        pltpu.VMEM((L, D), BF),
        pltpu.VMEM((D, D), BF),
        pltpu.VMEM((L, D), F32),
        pltpu.VMEM((L, D), F32),
        pltpu.VMEM((L, D), BF),
        pltpu.SemaphoreType.DMA((2 * S + blocks + 5,)),
    ]
    return call(
        partial(project_kernel, dims, first_call),
        (gains, *operands, *xs, *os),
        [vmem_spec()] + [any_spec()] * (len(operands) + 2 * S),
        outs,
        [hbm_spec()] * len(outs),
        scratch,
        2 * L * D * D,
        2 * (D * D + 4 * L * D + 5 * r * D),
        "project",
    )


def load_up(mover, ff_w, up_s):
    H = up_s.shape[1]
    return [mover.start(ff_w.at[:, pl.ds(0, H)], up_s)]


def down_places(D, H, S, F):
    W, R = D // S, D // F
    for f in range(F):
        for i in range(H // W):
            yield (
                (pl.ds(f * R, R), pl.ds(H + i * W, W)),
                (pl.ds(f // S * (R * (H // W)) + i * R, R), pl.ds(f % S * W, W)),
            )


def load_down(mover, ff_w, down_s, S, F):
    H, D = down_s.shape
    return [mover.start(ff_w.at[a], down_s.at[b]) for a, b in down_places(D, H, S, F)]


def feed_kernel(dims, order, ff_w, b_in, *refs):
    S, F, r, D, W, H = dims
    n = len(order)
    g_out, gp_out, slots, refs = *refs[:2], refs[2 : 2 + n], refs[2 + n :]
    up_s, down_s, b_s, g_s, gp_s, m_s, sems = refs
    me = seq_place()
    mover = Mover(sems)
    loads = [mover.start(b_in, b_s)] + load_up(mover, ff_w, up_s)
    down_loads = load_down(mover, ff_w, down_s, S, F)
    wide = 256
    wait_all(loads)
    root = math.sqrt(2.0 / math.pi)

    for c in range(H // wide):
        cols = slice(c * wide, c * wide + wide)
        z = dot_nn(b_s[...], up_s[:, cols])
        square = z * z
        bent = jnp.tanh(z * (root + root * 0.044715 * square))
        side = 0.5 + 0.5 * bent
        g_s[:, cols] = (z * side).astype(BF)
        slope = z * (root + 3.0 * root * 0.044715 * square)
        gp_s[:, cols] = (side + (0.5 * slope) * (1.0 - bent * bent)).astype(BF)
    stores = [mover.start(g_s, g_out), mover.start(gp_s, gp_out)]
    wait_all(down_loads)

    for c in range(D // wide):
        cols = slice(c * wide, c * wide + wide)
        m_s[:, cols] = dot_nn(g_s[...], down_s[:, cols]).astype(BF)
    stores += store_rows(mover, m_s, slots, order, me)
    wait_all(stores)


def feed(dims, turn, ff_w, b_rows):
    S, F, r, D, W, H = dims
    L = S * r
    outs = [((L, H), BF), ((L, H), BF)] + slot_shapes(S, turn, (r, D))
    scratch = [
        pltpu.VMEM((D, H), BF),
        pltpu.VMEM((H, D), BF),
        pltpu.VMEM((L, D), BF),
        pltpu.VMEM((L, H), BF),
        pltpu.VMEM((L, H), BF),
        pltpu.VMEM((L, D), BF),
        pltpu.SemaphoreType.DMA((S + F * (H // W) + 4,)),
    ]
    return call(
        partial(feed_kernel, dims, slot_order(S, turn)),
        (ff_w, b_rows),
        [any_spec()] * 2,
        outs,
        [hbm_spec()] * len(outs),
        scratch,
        4 * L * D * H,
        2 * (2 * D * H + 2 * L * D + 2 * L * H),
        "feed",
    )


def feed_back_kernel(dims, order, ff_w, gp, *refs):
    S, F, r, D, W, H = dims
    pieces, dm_out, dz_out, refs = refs[:S], *refs[S : S + 2], refs[S + 2 :]
    slots, refs = refs[: len(order)], refs[len(order) :]
    up_s, down_s, gp_s, dm_s, dz_s, part_s, sems = refs
    me = seq_place()
    mover = Mover(sems)
    loads = load_rows(mover, pieces, dm_s, me)
    down_loads = load_down(mover, ff_w, down_s, S, F)
    down_loads.append(mover.start(gp, gp_s))
    up_loads = load_up(mover, ff_w, up_s)
    wide = 256
    wait_all(loads)
    stores = [mover.start(dm_s, dm_out)]
    wait_all(down_loads)

    for c in range(H // wide):
        cols = slice(c * wide, c * wide + wide)
        grad = dot_nt(dm_s[...], down_s[cols, :])
        dz_s[:, cols] = (grad * gp_s[:, cols].astype(F32)).astype(BF)
    stores.append(mover.start(dz_s, dz_out))
    wait_all(up_loads)

    for c in range(D // wide):
        cols = slice(c * wide, c * wide + wide)
        part_s[:, cols] = dot_nt(dz_s[...], up_s[cols, :]).astype(BF)
    stores += store_rows(mover, part_s, slots, order, me)
    wait_all(stores)


def feed_back(dims, turn, ff_w, gp, pieces):
    S, F, r, D, W, H = dims
    L = S * r
    outs = [((L, D), BF), ((L, H), BF)] + slot_shapes(S, turn, (r, D))
    scratch = [
        pltpu.VMEM((D, H), BF),
        pltpu.VMEM((H, D), BF),
        pltpu.VMEM((L, H), BF),
        pltpu.VMEM((L, D), BF),
        pltpu.VMEM((L, H), BF),
        pltpu.VMEM((L, D), BF),
        pltpu.SemaphoreType.DMA((2 * S + F * (H // W) + 4,)),
    ]
    return call(
        partial(feed_back_kernel, dims, slot_order(S, turn)),
        (ff_w, gp, *pieces),
        [any_spec()] * (2 + S),
        outs,
        [hbm_spec()] * len(outs),
        scratch,
        4 * L * D * H,
        2 * (2 * D * H + 3 * L * D + 2 * L * H),
        "feed_back",
    )


def feed_outer_kernel(dims, count, *refs):
    S, F, D, W, H = dims
    ins, (out, *held, sum_s, sems) = refs[: 4 * count], refs[4 * count :]
    mover = Mover(sems)
    loads = [mover.start(a, b) for a, b in zip(ins, held)]
    g_rows, dm_rows = held[:count], held[count : 2 * count]
    b_rows, dz_rows = held[2 * count : 3 * count], held[3 * count :]
    wide = 256
    R = D // F
    tall = R * (H // W)
    stores = []
    wait_all(loads[: 2 * count])
    for c in range(D // wide):
        total = None
        for b in range(count):
            part = dot_tn(g_rows[b][...], dm_rows[b][:, c * wide : c * wide + wide])
            total = part if total is None else total + part
        total = total.astype(BF)
        for k in range(max(wide // W, 1)):
            for j in range(F // S):
                f = j * S + (c * wide) // W + k
                for i in range(H // W):
                    sum_s[f * R : f * R + R, H + i * W : H + i * W + W] = total[
                        j * tall + i * R : j * tall + i * R + R, k * W : k * W + W
                    ]
    stores.append(mover.start(sum_s.at[:, pl.ds(H, H)], out.at[:, pl.ds(H, H)]))
    wait_all(loads[2 * count :])
    for c in range(H // wide):
        total = None
        cols = slice(c * wide, c * wide + wide)
        for b in range(count):
            part = dot_tn(b_rows[b][...], dz_rows[b][:, cols])
            total = part if total is None else total + part
        sum_s[:, cols] = total.astype(BF)
        piece = pl.ds(c * wide, wide)
        stores.append(mover.start(sum_s.at[:, piece], out.at[:, piece]))
    wait_all(stores)


def feed_outer(dims, b_rows, dz_rows, g_rows, dm_rows):
    S, F, D, W, H = dims
    count = len(b_rows)
    L = b_rows[0].shape[0]
    operands = (*g_rows, *dm_rows, *b_rows, *dz_rows)
    return call(
        partial(feed_outer_kernel, dims, count),
        operands,
        [any_spec()] * len(operands),
        [((D, 2 * H), BF)],
        [hbm_spec()],
        [pltpu.VMEM(x.shape, BF) for x in operands]
        + [pltpu.VMEM((D, 2 * H), BF), pltpu.SemaphoreType.DMA((4 * count + 1 + H // 256,))],
        4 * count * L * D * H,
        2 * (count * 2 * L * (D + H) + 2 * D * H),
        "feed_outer",
    )[0]


def total_of(refs, rows):
    total = None
    for ref, used in zip(refs, (1, 1, 1)):
        for i in range(used):
            value = ref[i, rows, :].astype(F32)
            total = value if total is None else total + value
    return total


def column_sum(v):
    return jnp.sum(v, axis=0, keepdims=True)


def finish_kernel(count, gains, u_ref, h_ref, dy_ref, *refs):
    terms, (y_out, dm_hbm, stat_out, dm_out, sems) = refs[:count], refs[count:]
    mover = Mover(sems)
    half = dm_out.shape[0] // 2
    stats = [None] * 5
    for part in range(2):
        rows = slice(part * half, part * half + half)
        m = total_of(terms, rows)
        unit, scale = norm_parts(m)
        f = unit * gains[3:4, :]
        h = h_ref[rows, :]
        y = h + f
        y_out[rows, :] = y.astype(BF)
        dy = dy_ref[rows, :].astype(F32)
        dm = norm_back(dy * gains[3:4, :], unit, scale)
        dm_out[rows, :] = dm.astype(BF)
        if part == 1:
            store = mover.start(dm_out, dm_hbm)
        second, unused = norm_parts(u_ref[rows, :])
        e = second * gains[1:2, :]
        values = [dy * unit, h * h, y * y, e * e, f * f]
        for index, value in enumerate(values):
            value = column_sum(value)
            stats[index] = value if part == 0 else stats[index] + value
    stat_out[...] = jnp.zeros_like(stat_out)
    for index in range(5):
        stat_out[3 + index : 4 + index, :] = stats[index]
    store.wait()


def finish(gains, u, h, dy, terms):
    r, D = u.shape
    outs = [((r, D), BF), ((r, D), BF), ((8, D), F32)]
    operands = (gains, u, h, dy, *terms)
    return call(
        partial(finish_kernel, len(terms)),
        operands,
        [vmem_spec()] * len(operands),
        outs,
        [vmem_spec(), hbm_spec(), vmem_spec()],
        [pltpu.VMEM((r, D), BF), pltpu.SemaphoreType.DMA((1,))],
        60 * r * D,
        r * D * 20,
        "finish",
    )


def middle_kernel(count, S, out_hbm, gains, u_ref, h_ref, dy_ref, *refs):
    terms, refs = refs[:count], refs[count:]
    dh_out, du_hbm, stat_out = refs[:3]
    pieces, (du_out, out_w, do_s, sems) = refs[3 : 3 + S], refs[3 + S :]
    mover = Mover(sems)
    load = mover.start(out_hbm, out_w)
    r, D = u_ref.shape
    half = r // 2
    W = D // S
    me = seq_place()
    stats = [None] * 2
    for part in range(2):
        rows = slice(part * half, part * half + half)
        back = total_of(terms, rows)
        unit, scale = norm_parts(h_ref[rows, :])
        third = column_sum(back * unit)
        dh = dy_ref[rows, :].astype(F32) + norm_back(back * gains[2:3, :], unit, scale)
        dh_out[rows, :] = dh
        unit, scale = norm_parts(u_ref[rows, :])
        second = column_sum(dh * unit)
        du_out[rows, :] = norm_back(dh * gains[1:2, :], unit, scale).astype(BF)
        for index, value in enumerate((second, third)):
            stats[index] = value if part == 0 else stats[index] + value
    stat_out[...] = jnp.zeros_like(stat_out)
    stat_out[1:2, :] = stats[0]
    stat_out[2:3, :] = stats[1]
    stores = [mover.start(du_out, du_hbm)]
    load.wait()
    for slot in range(S):
        rows = pl.ds(pl.multiple_of((me ^ slot) * W, W), W)
        do_s[slot] = dot_nt(du_out[...], out_w[rows, :]).astype(BF)
        stores.append(mover.start(do_s.at[slot], pieces[slot]))
    wait_all(stores)


def middle(S, gains, out_w, u, h, dy, terms):
    r, D = u.shape
    outs = [((r, D), F32), ((r, D), BF), ((8, D), F32)] + [((r, D // S), BF)] * S
    operands = (out_w, gains, u, h, dy, *terms)
    return call(
        partial(middle_kernel, len(terms), S),
        operands,
        [any_spec()] + [vmem_spec()] * (len(operands) - 1),
        outs,
        [vmem_spec(), hbm_spec(), vmem_spec()] + [hbm_spec()] * S,
        [
            pltpu.VMEM((r, D), BF),
            pltpu.VMEM((D, D), BF),
            pltpu.VMEM((S, r, D // S), BF),
            pltpu.SemaphoreType.DMA((2 + S,)),
        ],
        2 * r * D * D,
        2 * D * D + r * D * 24,
        "middle",
    )


def last_kernel(count, gains, x_ref, dh_ref, *refs):
    terms, (out,) = refs[:count], refs[count:]
    r, D = x_ref.shape
    half = r // 2
    for part in range(2):
        rows = slice(part * half, part * half + half)
        back = total_of(terms, rows)
        unit, scale = norm_parts(x_ref[rows, :].astype(F32))
        grad = dh_ref[rows, :] + norm_back(back * gains[0:1, :], unit, scale)
        out[rows, :] = grad.astype(BF)


def last(gains, x, dh, terms):
    r, D = x.shape
    operands = (gains, x, dh, *terms)
    return call(
        partial(last_kernel, len(terms)),
        operands,
        [vmem_spec()] * len(operands),
        [((r, D), BF)],
        [vmem_spec()],
        [],
        40 * r * D,
        r * D * 14,
        "last",
    )[0]


def rest_outer_kernel(dims, count, many, *refs):
    S, F, D, W = dims
    stats, refs = refs[:many], refs[many:]
    n = (3 + S) * count
    ins, (out, *held, sum_s, stat_s, sems) = refs[:n], refs[n:]
    mover = Mover(sems)
    o_rows, dus = held[:count], held[count : 2 * count]
    a_rows, grads = held[2 * count : 3 * count], held[3 * count :]
    loads = [mover.start(a, b) for a, b in zip(ins[:count], o_rows)]
    for b in range(count):
        pieces = ins[count + b * S : count + b * S + S]
        loads += load_rows(mover, pieces, dus[b], seq_place())
    late = [mover.start(a, b) for a, b in zip(ins[(1 + S) * count :], held[2 * count :])]
    R = D // F
    places = [pl.multiple_of(place * R, R) for place in block_places(F)]
    stores = []
    if F == 8:
        total = stats[0][...]
        for other in stats[1:]:
            total = total + other[...]
        squares = total[4:8, 0:R]
        for i in range(1, F):
            squares = squares + total[4:8, i * R : i * R + R]
        joined = jnp.concatenate([total[0:4], jnp.concatenate([squares] * F, axis=1)], axis=0)
        stat_s[0:8, :] = joined.astype(BF)
        stat_s[8:16, :] = jnp.zeros_like(total).astype(BF)
        for i in range(F):
            stores.append(
                mover.start(
                    stat_s.at[:, pl.ds(places[i], R)],
                    out.at[i, pl.ds(4 * R, EXTRA), pl.ds(0, R)],
                )
            )
    wait_all(loads)
    total = None
    for b in range(count):
        part = dot_tn(o_rows[b][...], dus[b][...])
        total = part if total is None else total + part
    sum_s[0:W, 3 * W : 3 * W + D] = total.astype(BF)
    for i, place in enumerate(block_places(F)):
        row = pl.multiple_of(place // S * R, R)
        col = pl.multiple_of(3 * W + place % S * W, W)
        stores.append(
            mover.start(sum_s.at[pl.ds(row, R), pl.ds(col, W)], out.at[i, pl.ds(3 * R, R)])
        )
    wait_all(late)
    for t in range(3):
        cols = slice(t * W, t * W + W)
        total = None
        for b in range(count):
            part = dot_tn(a_rows[b][...], grads[b][:, cols])
            total = part if total is None else total + part
        sum_s[:, cols] = total.astype(BF)
        for i in range(F):
            stores.append(
                mover.start(
                    sum_s.at[pl.ds(places[i], R), pl.ds(t * W, W)],
                    out.at[i, pl.ds(t * R, R)],
                )
            )
    wait_all(stores)


def rest_outer(dims, stats, o_rows, dus, a_rows, grads):
    S, F, D, W = dims
    count = len(o_rows)
    L = o_rows[0].shape[0]
    operands = (*o_rows, *[piece for du in dus for piece in du], *a_rows, *grads)
    return call(
        partial(rest_outer_kernel, dims, count, len(stats)),
        (*stats, *operands),
        [vmem_spec()] * len(stats) + [any_spec()] * len(operands),
        [((F, 4 * (D // F) + EXTRA, W), BF)],
        [hbm_spec()],
        [pltpu.VMEM(x.shape, BF) for x in o_rows]
        + [pltpu.VMEM((L, D), BF)] * count
        + [pltpu.VMEM(x.shape, BF) for x in (*a_rows, *grads)]
        + [
            pltpu.VMEM((D, 3 * W + D), BF),
            pltpu.VMEM((EXTRA, D), BF),
            pltpu.SemaphoreType.DMA(((3 + S) * count + 5 * F,)),
        ],
        8 * count * L * D * W,
        2 * (count * L * (2 * D + 4 * W) + 4 * D * W),
        "rest_outer",
    )[0]


def flip(bits, size):
    return [(i, i ^ bits) for i in range(size)]


def add_low(*terms):
    total = terms[0].astype(F32)
    for term in terms[1:]:
        total = total + term.astype(F32)
    return total.astype(BF)


def gather_slots(own, S, me, turn):
    if S != 4:
        full = lax.all_gather(own, "seq")
        return [
            lax.dynamic_index_in_dim(full, me ^ slot, 0, keepdims=False) for slot in range(S)
        ]
    one = lax.ppermute(own, "seq", flip(1, S))
    two = lax.ppermute(own, "seq", flip(2, S))
    if turn % 2 == 0:
        far = lax.ppermute(one, "seq", flip(2, S))
    else:
        far = lax.ppermute(two, "seq", flip(1, S))
    return [own, one, two, far]


def slot_order(S, turn):
    if S != 4:
        return [[slot] for slot in range(S)]
    first, second = (1, 2) if turn % 2 == 0 else (2, 1)
    return [[0], [first, 3], [second]]


def slot_shapes(S, turn, shape):
    return [((len(group), *shape), BF) for group in slot_order(S, turn)]


def scatter_slots(groups, S, me, turn):
    if S != 4:
        order = jnp.take(jnp.concatenate(groups), me ^ jnp.arange(S), axis=0)
        return [lax.psum_scatter(order, "seq", scatter_dimension=0, tiled=True)]
    first, second = (1, 2) if turn % 2 == 0 else (2, 1)
    got = lax.ppermute(groups[1], "seq", flip(first, S))
    joined = lax.ppermute(add_low(groups[2][0], got[1]), "seq", flip(second, S))
    return [groups[0], got, joined[None]]


def swap_slots(pieces, S):
    return [pieces[0]] + [lax.ppermute(pieces[j], "seq", flip(j, S)) for j in range(1, S)]


def sum_everywhere(v, S, F):
    if S != 4 or F != 8:
        return lax.psum(v, ("seq", "fsdp"))
    v = v + lax.ppermute(v, "fsdp", flip(1, F))
    v = v + lax.ppermute(v, "seq", flip(1, S))
    v = v + lax.ppermute(v, "seq", flip(2, S))
    v = v + lax.ppermute(v, "fsdp", flip(2, F))
    return v + lax.ppermute(v, "fsdp", flip(4, F))


def gather_blocks(block, F, early=()):
    if F != 8:
        return [lax.all_gather(block, "fsdp")]
    near = lax.ppermute(block, "fsdp", flip(1, F))
    far = [lax.ppermute(block, "fsdp", flip(j, F)) for j in (2, 4, 6)]
    rest = lax.ppermute(after(jnp.stack(far), early), "fsdp", flip(1, F))
    return [block[None], near[None]] + [piece[None] for piece in far] + [rest]


def after(value, *others):
    return lax.optimization_barrier((value, others))[0]


def scatter_blocks(parts, F):
    if F != 8:
        return lax.psum_scatter(parts, "fsdp", scatter_dimension=0, tiled=False)
    mine = jnp.concatenate([parts[:1], parts[2:5]])
    other = jnp.concatenate([parts[1:2], parts[5:]])
    mine = add_low(mine, lax.ppermute(other, "fsdp", flip(1, F)))
    got = [lax.ppermute(mine[j], "fsdp", flip(2 * j, F)) for j in (1, 2, 3)]
    return add_low(mine[0], *got)


def blocks_in(blocks, S, me):
    moved = []
    for j in range(3):
        pairs = [(s, (3 * s + j) % S) for s in range(S)]
        moved.append(lax.ppermute(blocks[j], "seq", pairs))
    stack = jnp.stack(moved)
    return [
        lax.dynamic_index_in_dim(stack, (me + S * t) % 3, 0, keepdims=False) for t in range(3)
    ]


def blocks_out(stack, S, me):
    moved = []
    for j in range(3):
        t = ((j - me) * (S % 3)) % 3
        piece = lax.dynamic_index_in_dim(stack, t, 0, keepdims=False)
        pairs = [((3 * s + j) % S, s) for s in range(S)]
        moved.append(lax.ppermute(piece, "seq", pairs))
    return jnp.concatenate(moved, axis=1)


def turn_pairs(S, F):
    each = F // S
    return [
        (s * F + f, (f // each) * F + (f % each) * S + s) for s in range(S) for f in range(F)
    ]


def shards(tokens, cotangent, prefix, qkv_weight, out_weight, up_weight, down_weight, norm_gains):
    S, F = lax.axis_size("seq"), lax.axis_size("fsdp")
    B, r, D = tokens.shape
    heads = D // HEAD // S
    W = D // S
    R = D // F
    H = up_weight.shape[1]
    tiles = H // W
    me = seq_place()
    place = lax.axis_index("fsdp").astype(jnp.int32)
    pairs = turn_pairs(S, F)

    blocks = [qkv_weight[:, j * W : j * W + W] for j in range(3)]
    gain_rows = jnp.pad(norm_gains, ((0, EXTRA - 4), (0, W - R)))
    first_block = jnp.concatenate(blocks_in(blocks, S, me) + [out_weight, gain_rows])
    xs = [gather_slots(tokens[b], S, me, b) for b in range(B)]
    stacks = gather_blocks(first_block, F, xs)
    down_mine = lax.ppermute(down_weight, ("seq", "fsdp"), pairs)
    ff_mine = jnp.concatenate(
        [up_weight] + [down_mine[i * R : i * R + R] for i in range(tiles)], axis=1
    )
    ff_mine = after(ff_mine, stacks[-1])
    ff_full = lax.all_gather(ff_mine, "fsdp", axis=0, tiled=True)
    gains = None
    if F != 8:
        gains = lax.all_gather(norm_gains, "fsdp", axis=1, tiled=True).astype(F32)
        gains = jnp.pad(gains, ((0, 4), (0, 0)))
    out_stack = jnp.concatenate([stack[:, 3 * R : 4 * R] for stack in stacks])
    out_slots = gather_slots(out_stack, S, me, 0)

    att_dims = (S, F, r, D, heads)
    ff_dims = (S, F, r, D, W, H)
    a_all, qkv_all, p_all, os, os_own = [], [], [], [], []
    for b in range(B):
        a, qkv, o, p, gains_full = attend(att_dims, b, prefix, gains, stacks, xs[b])
        a_all.append(a)
        qkv_all.append(qkv)
        p_all.append(p)
        os_own.append(o)
        os.append(gather_slots(o, S, me, b))
    gains = gains_full
    b_all, u_own, h_own = [], [], []
    out_full = out_slots
    for b in range(B):
        res = project((S, F, r, D, W), gains, out_full, xs[b], os[b])
        b_all.append(res[0])
        u_own.append(res[1])
        h_own.append(res[2])
        if b == 0:
            out_full = res[3]
    g_all, gp_all, m_terms = [], [], []
    for b in range(B):
        res = feed(ff_dims, b, ff_full, b_all[b])
        g_all.append(res[0])
        gp_all.append(res[1])
        m_terms.append(scatter_slots(list(res[2:]), S, me, b))
    ys, stats, dms = [], [], []
    for b in range(B):
        y, dm, stat = finish(gains, u_own[b], h_own[b], cotangent[b], m_terms[b])
        ys.append(y)
        stats.append(stat)
        dms.append(gather_slots(dm, S, me, b))
    dm_all, dz_all, h_terms = [], [], []
    for b in range(B):
        res = feed_back(ff_dims, b, ff_full, gp_all[b], dms[b])
        dm_all.append(res[0])
        dz_all.append(res[1])
        h_terms.append(scatter_slots(list(res[2:]), S, me, b))
    ff_part = feed_outer((S, F, D, W, H), b_all, dz_all, g_all, dm_all)
    ff_sum = lax.psum_scatter(ff_part, "fsdp", scatter_dimension=0, tiled=True)
    dhs, dus, dos = [], [], []
    for b in range(B):
        res = middle(S, gains, out_full, u_own[b], h_own[b], cotangent[b], h_terms[b])
        dhs.append(res[0])
        dos.append(swap_slots(list(res[3:]), S))
        dus.append(res[1])
        stats.append(res[2])
    dus = after(dus, dos)
    dus = [gather_slots(dus[b], S, me, b) for b in range(B)]
    dqkvs, x_terms = [], []
    for b in range(B):
        res = attend_back(att_dims, b, gains, stacks, a_all[b], qkv_all[b], p_all[b], dos[b])
        dqkvs.append(res[0])
        stats.append(res[1])
        x_terms.append(scatter_slots(list(res[2:]), S, me, b))
    rest_part = rest_outer((S, F, D, W), stats, os_own, dus, a_all, dqkvs)
    rest = scatter_blocks(rest_part, F)
    qkv_own = blocks_out(jnp.stack([rest[t * R : t * R + R] for t in range(3)]), S, me)
    input_grads = [last(gains, tokens[b], dhs[b], x_terms[b]) for b in range(B)]

    down_sum = jnp.concatenate(
        [ff_sum[:, H + i * W : H + i * W + W] for i in range(tiles)], axis=0
    )
    back_pairs = [(b, a) for a, b in pairs]
    down_own = lax.ppermute(down_sum, ("seq", "fsdp"), back_pairs)
    out_own = lax.ppermute(rest[3 * R : 4 * R], ("seq", "fsdp"), back_pairs)
    if F == 8 and S == 4:
        part = rest[4 * R : 4 * R + 8, :R].astype(F32)
        part = part + sum(lax.ppermute(part, "seq", flip(j, S)) for j in (1, 2, 3))
        gains_grad, squares = part[:4], jnp.sum(part[4:], axis=1)
    else:
        totals = lax.psum(sum(stats), ("seq", "fsdp"))
        gains_grad = lax.dynamic_slice_in_dim(totals[:4], place * R, R, 1)
        squares = jnp.sum(totals[4:], axis=1)
    entries = B * r * D * S * F
    stream_rms = jnp.sqrt(squares / entries)
    return (
        jnp.stack(ys),
        jnp.stack(input_grads),
        qkv_own.astype(F32),
        out_own.astype(F32),
        ff_sum[:, :H].astype(F32),
        down_own.astype(F32),
        gains_grad,
        stream_rms,
    )


def solution(mesh):
    in_specs = (
        P("fsdp", "seq", None),
        P("fsdp", "seq", None),
        P("fsdp"),
        P("fsdp", "seq"),
        P("fsdp", "seq"),
        P("fsdp", "seq"),
        P("fsdp", "seq"),
        P(None, "fsdp"),
    )
    out_specs = (
        P("fsdp", "seq", None),
        P("fsdp", "seq", None),
        P("fsdp", "seq"),
        P("fsdp", "seq"),
        P("fsdp", "seq"),
        P("fsdp", "seq"),
        P(None, "fsdp"),
        P(),
    )
    return jax.shard_map(shards, mesh=mesh, in_specs=in_specs, out_specs=out_specs, check_vma=False)
```

```python
import math
from functools import partial

import jax
import jax.numpy as jnp
from jax import lax
from jax.experimental import pallas as pl
from jax.experimental.pallas import tpu as pltpu
from jax.sharding import PartitionSpec as P

HEAD = 64
NORM_EPSILON = 1e-05
MASKED_SCORE = -1e30
VMEM_LIMIT = 56 * 1024 * 1024
BF = jnp.bfloat16
F32 = jnp.float32
BLOCK_ORDER = (0, 1, 2, 4, 6, 3, 5, 7)
EXTRA = 16
COST = 0.001


def dot_nn(a, b):
    return lax.dot_general(a, b, (((1,), (0,)), ((), ())), preferred_element_type=F32)


def dot_nt(a, b):
    return lax.dot_general(a, b, (((1,), (1,)), ((), ())), preferred_element_type=F32)


def dot_tn(a, b):
    return lax.dot_general(a, b, (((0,), (0,)), ((), ())), preferred_element_type=F32)


def norm_parts(v):
    centre = jnp.mean(v, axis=-1, keepdims=True)
    shifted = v - centre
    spread = jnp.mean(shifted * shifted, axis=-1, keepdims=True)
    scale = lax.rsqrt(spread + NORM_EPSILON)
    return shifted * scale, scale


def norm_back(grad_unit, unit, scale):
    first = jnp.mean(grad_unit, axis=-1, keepdims=True)
    second = jnp.mean(grad_unit * unit, axis=-1, keepdims=True)
    return scale * (grad_unit - first - unit * second)


def seq_place():
    return lax.axis_index("seq").astype(jnp.int32)


def block_places(F):
    if F != 8:
        return [jnp.int32(i) for i in range(F)]
    place = lax.axis_index("fsdp").astype(jnp.int32)
    return [place ^ i for i in BLOCK_ORDER]


class Mover:
    def __init__(self, sems):
        self.sems = sems
        self.used = 0

    def start(self, src, dst):
        copy = pltpu.make_async_copy(src, dst, self.sems.at[self.used])
        self.used += 1
        copy.start()
        return copy


def wait_all(copies):
    for copy in copies:
        copy.wait()


def load_rows(mover, pieces, target, me):
    r = pieces[0].shape[0]
    copies = []
    for slot, piece in enumerate(pieces):
        start = pl.multiple_of((me ^ slot) * r, r)
        copies.append(mover.start(piece, target.at[pl.ds(start, r)]))
    return copies


def store_rows(mover, source, outs, order, me):
    r = outs[0].shape[1]
    copies = []
    for group, out in zip(order, outs):
        for i, slot in enumerate(group):
            start = pl.multiple_of((me ^ slot) * r, r)
            copies.append(mover.start(source.at[pl.ds(start, r)], out.at[i]))
    return copies


def load_blocks(mover, stacks, target, tiles):
    F = sum(stack.shape[0] for stack in stacks)
    places, copies, index = block_places(F), [], 0
    rows = target.shape[0] // F
    for stack in stacks:
        cols = stack.shape[2]
        for i in range(stack.shape[0]):
            start = pl.multiple_of(places[index] * rows, rows)
            index += 1
            for t in range(tiles):
                copies.append(
                    mover.start(
                        stack.at[i, pl.ds(t * rows, rows)],
                        target.at[pl.ds(start, rows), pl.ds(t * cols, cols)],
                    )
                )
    return copies


def load_gains(mover, stacks, target):
    F = sum(stack.shape[0] for stack in stacks)
    places, copies, index = block_places(F), [], 0
    width = target.shape[1] // F
    for stack in stacks:
        last = stack.shape[1] - EXTRA
        for i in range(stack.shape[0]):
            start = pl.multiple_of(places[index] * width, width)
            index += 1
            copies.append(
                mover.start(
                    stack.at[i, pl.ds(last, EXTRA), pl.ds(0, width)],
                    target.at[:, pl.ds(start, width)],
                )
            )
    return copies


def any_spec():
    return pl.BlockSpec(memory_space=pl.ANY)


def hbm_spec():
    return pl.BlockSpec(memory_space=pltpu.HBM)


def smem_spec():
    return pl.BlockSpec(memory_space=pltpu.SMEM)


def vmem_spec():
    return pl.BlockSpec(memory_space=pltpu.VMEM)


def call(body, operands, in_specs, outs, out_specs, scratch, flops, bytes_accessed, name, aliases={}):
    return pl.pallas_call(
        body,
        out_shape=tuple(jax.ShapeDtypeStruct(shape, dtype) for shape, dtype in outs),
        in_specs=in_specs,
        out_specs=tuple(out_specs),
        scratch_shapes=scratch,
        input_output_aliases=aliases,
        compiler_params=pltpu.CompilerParams(vmem_limit_bytes=VMEM_LIMIT),
        cost_estimate=pl.CostEstimate(
            flops=int(flops * COST), bytes_accessed=int(bytes_accessed * COST), transcendentals=0
        ),
        name=name,
    )(*operands)


def attend_kernel(dims, count, turn, packed, prefix, *refs):
    S, F, r, D, heads = dims
    L, W = S * r, heads * HEAD
    if packed:
        gains_in = None
    else:
        gains_in, refs = refs[0], refs[1:]
    weights, pieces, refs = refs[:count], refs[count : count + S], refs[count + S :]
    a_out, qkv_out, o_out, p_out, gains_out, refs = *refs[:5], refs[5:]
    x_s, w_s, a_s, qkv_s, o_s, p_s, bias_s, raw_s, sems = refs
    me, limit_len = seq_place(), prefix[turn]
    mover = Mover(sems)
    gain_loads = load_gains(mover, weights, raw_s) if packed else []
    loads = load_rows(mover, [piece.at[turn] for piece in pieces], x_s, me)
    weight_loads = load_blocks(mover, weights, w_s, 3)
    tile = 128
    limit = L // 2
    for i in range(L // tile):
        shape = (tile, max((i + 1) * tile, limit))
        rows = i * tile + lax.broadcasted_iota(jnp.int32, shape, 0)
        cols = lax.broadcasted_iota(jnp.int32, shape, 1)
        seen = (cols <= rows) | (cols < limit_len)
        bias_s[i * tile : i * tile + tile, : shape[1]] = jnp.where(seen, 0.0, MASKED_SCORE)
    wait_all(gain_loads)
    gains_out[...] = raw_s[0:8, :].astype(F32) if packed else gains_in[...]
    wait_all(loads)
    for i in range(L // tile):
        rows = slice(i * tile, i * tile + tile)
        unit, scale = norm_parts(x_s[rows, :].astype(F32))
        a_s[rows, :] = (unit * gains_out[0:1, :]).astype(BF)
    stores = [mover.start(a_s, a_out)]
    wait_all(weight_loads)
    for c in range(3):
        cols = slice(c * W, c * W + W)
        qkv_s[:, cols] = dot_nn(a_s[...], w_s[:, cols]).astype(BF)
    stores.append(mover.start(qkv_s, qkv_out))
    lane = lax.broadcasted_iota(jnp.int32, (1, 128), 1)
    for pair in range(heads // 2):
        q2 = qkv_s[:, pair * 128 : pair * 128 + 128] * BF(HEAD**-0.5)
        k2 = qkv_s[:, W + pair * 128 : W + pair * 128 + 128]
        v2 = qkv_s[:, 2 * W + pair * 128 : 2 * W + pair * 128 + 128]
        keys, values = [], []
        for side in range(2):
            mine = (lane >= 64) if side else (lane < 64)
            keys.append(jnp.where(mine, k2, BF(0)))
            values.append(jnp.where(mine, v2, BF(0)))
        for i in range(L // tile):
            rows = slice(i * tile, i * tile + tile)
            span = max((i + 1) * tile, limit)
            total = None
            for side in range(2):
                scores = dot_nt(q2[rows], keys[side][:span]) + bias_s[rows, :span]
                top = jnp.max(scores, axis=-1, keepdims=True)
                weights_here = jnp.exp(scores - top)
                share = 1.0 / jnp.sum(weights_here, axis=-1, keepdims=True)
                probs = (weights_here * share).astype(BF)
                p_s[2 * pair + side, rows, :span] = probs
                part = dot_nn(probs, values[side][:span])
                total = part if total is None else total + part
            o_s[rows, pair * 128 : pair * 128 + 128] = total.astype(BF)
        for side in range(2):
            stores.append(mover.start(p_s.at[2 * pair + side], p_out.at[2 * pair + side]))
    stores.append(mover.start(o_s, o_out))
    wait_all(stores)


def attend(dims, turn, prefix, gains, weights, pieces):
    S, F, r, D, heads = dims
    L, W = S * r, heads * HEAD
    outs = [((L, D), BF), ((L, 3 * W), BF), ((L, W), BF), ((heads, L, L), BF), ((8, D), F32)]
    scratch = [
        pltpu.VMEM((L, D), BF),
        pltpu.VMEM((D, 3 * W), BF),
        pltpu.VMEM((L, D), BF),
        pltpu.VMEM((L, 3 * W), BF),
        pltpu.VMEM((L, W), BF),
        pltpu.VMEM((heads, L, L), BF),
        pltpu.VMEM((L, L), F32),
        pltpu.VMEM((EXTRA, D), BF),
        pltpu.SemaphoreType.DMA((S + 4 * F + heads + 3,)),
    ]
    flops = 2 * L * D * 3 * W + 4 * heads * L * L * HEAD * 4
    size = 2 * (2 * L * D + 3 * D * W + 4 * L * W + heads * L * L)
    packed = gains is None
    extra = [] if packed else [gains]
    return call(
        partial(attend_kernel, dims, len(weights), turn, packed),
        (prefix, *extra, *weights, *pieces),
        [smem_spec()]
        + [vmem_spec()] * len(extra)
        + [any_spec()] * (len(weights) + len(pieces)),
        outs,
        [hbm_spec()] * 4 + [vmem_spec()],
        scratch,
        flops,
        size,
        "attend",
    )


def attend_back_kernel(dims, count, order, gains_in, out_w, *refs):
    S, F, r, D, heads = dims
    n = len(order)
    L, W = S * r, heads * HEAD
    weights, refs = refs[:count], refs[count:]
    a_in, qkv, probs_in, pieces, refs = *refs[:3], refs[3 : 3 + S], refs[3 + S :]
    grad_out, stat_out, slots, refs = *refs[:2], refs[2 : 2 + n], refs[2 + n :]
    w_s, qkv_s, p_s, du_s, do_s, d_s, grad_s, part_s, a_s, out_s, gains, sems = refs
    me = seq_place()
    mover = Mover(sems)
    own = pl.ds(pl.multiple_of(me * W, W), W)
    loads = load_out(mover, out_w, out_s, own, me, S) + load_rows(mover, pieces, du_s, me)
    loads.append(mover.start(qkv, qkv_s))
    prob_loads = [mover.start(probs_in.at[h], p_s.at[h]) for h in range(heads)]
    late_loads = load_blocks(mover, weights, w_s, 3)
    late_loads.append(mover.start(a_in, a_s))
    late_loads.append(mover.start(gains_in, gains))
    tile = 128
    limit = L // 2
    wait_all(loads)
    do_s[...] = dot_nt(du_s[...], out_s[...]).astype(BF)
    lane = lax.broadcasted_iota(jnp.int32, (1, 128), 1)
    for pair in range(heads // 2):
        cols = slice(pair * 128, pair * 128 + 128)
        q2 = qkv_s[:, cols] * BF(HEAD**-0.5)
        k2 = qkv_s[:, W + pair * 128 : W + pair * 128 + 128] * BF(HEAD**-0.5)
        v2 = qkv_s[:, 2 * W + pair * 128 : 2 * W + pair * 128 + 128]
        do2 = do_s[:, cols]
        queries, keys, values, grads = [], [], [], []
        for side in range(2):
            mine = (lane >= 64) if side else (lane < 64)
            queries.append(jnp.where(mine, q2, BF(0)))
            keys.append(jnp.where(mine, k2, BF(0)))
            values.append(jnp.where(mine, v2, BF(0)))
            grads.append(jnp.where(mine, do2, BF(0)))
            prob_loads[2 * pair + side].wait()
        for i in range(L // tile):
            rows = slice(i * tile, i * tile + tile)
            span = max((i + 1) * tile, limit)
            total = None
            for side in range(2):
                probs = p_s[2 * pair + side, rows, :span].astype(F32)
                grad_probs = dot_nt(do2[rows], values[side][:span])
                delta = jnp.sum(probs * grad_probs, axis=-1, keepdims=True)
                grad_scores = (probs * (grad_probs - delta)).astype(BF)
                d_s[side, rows, :span] = grad_scores
                part = dot_nn(grad_scores, keys[side][:span])
                total = part if total is None else total + part
            grad_s[rows, cols] = total.astype(BF)
        for j in range(L // tile):
            columns = slice(j * tile, j * tile + tile)
            low = 0 if (j * tile) < limit else j * tile
            total_k, total_v = None, None
            for side in range(2):
                part = dot_tn(d_s[side, low:, columns], queries[side][low:])
                total_k = part if total_k is None else total_k + part
                part = dot_tn(p_s[2 * pair + side, low:, columns], grads[side][low:])
                total_v = part if total_v is None else total_v + part
            grad_s[columns, W + pair * 128 : W + pair * 128 + 128] = total_k.astype(BF)
            grad_s[columns, 2 * W + pair * 128 : 2 * W + pair * 128 + 128] = total_v.astype(BF)
    stores = [mover.start(grad_s, grad_out)]
    wait_all(late_loads)
    wide = 256
    stat_out[...] = jnp.zeros_like(stat_out)

    for c in range(D // wide):
        cols = slice(c * wide, c * wide + wide)
        part = dot_nt(grad_s[...], w_s[cols, :])
        part_s[:, cols] = part.astype(BF)
        stat_out[0:1, cols] = column_sum(part * a_s[:, cols].astype(F32)) / gains[0:1, cols]
    stores += store_rows(mover, part_s, slots, order, me)
    wait_all(stores)


def attend_back(dims, turn, gains, out_w, weights, a, qkv, probs, pieces):
    S, F, r, D, heads = dims
    L, W = S * r, heads * HEAD
    outs = [((L, 3 * W), BF), ((8, D), F32)] + slot_shapes(S, turn, (r, D))
    blocks = 3 * F
    scratch = [
        pltpu.VMEM((D, 3 * W), BF),
        pltpu.VMEM((L, 3 * W), BF),
        pltpu.VMEM((heads, L, L), BF),
        pltpu.VMEM((L, D), BF),
        pltpu.VMEM((L, W), BF),
        pltpu.VMEM((2, L, L), BF),
        pltpu.VMEM((L, 3 * W), BF),
        pltpu.VMEM((L, D), BF),
        pltpu.VMEM((L, D), BF),
        pltpu.VMEM((W, D), BF),
        pltpu.VMEM((8, D), F32),
        pltpu.SemaphoreType.DMA((3 * S + heads + 5 + blocks,)),
    ]
    flops = 2 * L * D * 4 * W + 8 * heads * L * L * HEAD * 4
    size = 2 * (2 * L * D + 3 * D * W + 7 * L * W + heads * L * L)
    return call(
        partial(attend_back_kernel, dims, len(weights), slot_order(S, turn)),
        (gains, out_w, *weights, a, qkv, probs, *pieces),
        [any_spec()] * 2
        + [any_spec()] * (3 + len(weights) + len(pieces)),
        outs,
        [hbm_spec(), vmem_spec()] + [hbm_spec()] * (len(outs) - 2),
        scratch,
        flops,
        size,
        "attend_back",
    )


def load_out(mover, ff_w, target, rows, me, S):
    D = target.shape[1]
    W, base = D // S, ff_w.shape[1] - D
    copies = []
    for slot in range(S):
        start = pl.multiple_of((me ^ slot) * W, W)
        copies.append(
            mover.start(
                ff_w.at[rows, pl.ds(base + slot * W, W)], target.at[:, pl.ds(start, W)]
            )
        )
    return copies


def load_up(mover, ff_w, up_s):
    H = up_s.shape[1]
    return [mover.start(ff_w.at[:, pl.ds(0, H)], up_s)]


def down_places(D, H, S, F):
    W, R = D // S, D // F
    for f in range(F):
        for i in range(H // W):
            yield (
                (pl.ds(f * R, R), pl.ds(H + i * W, W)),
                (pl.ds(f // S * (R * (H // W)) + i * R, R), pl.ds(f % S * W, W)),
            )


def load_down(mover, ff_w, down_s, S, F):
    H, D = down_s.shape
    return [mover.start(ff_w.at[a], down_s.at[b]) for a, b in down_places(D, H, S, F)]


def feed_kernel(dims, order, turn, gains_in, ff_w, *refs):
    S, F, r, D, W, H = dims
    L, n = S * r, len(order)
    xs, os, refs = refs[:S], refs[S : 2 * S], refs[2 * S :]
    b_out, u_own, h_own, g_out, gp_out, slots, refs = *refs[:5], refs[5 : 5 + n], refs[5 + n :]
    x_s, o_s, out_s, u_s, h_s, up_s, down_s, b_s, g_s, gp_s, m_s, gains, sems = refs
    me = seq_place()
    mover = Mover(sems)
    loads = [mover.start(gains_in, gains)]
    for slot in range(S):
        start = pl.multiple_of((me ^ slot) * W, W)
        loads.append(mover.start(os[slot], o_s.at[:, pl.ds(start, W)]))
    loads += load_out(mover, ff_w, out_s, pl.ds(0, D), me, S)
    loads += load_rows(mover, [x.at[turn] for x in xs], x_s, me)
    up_loads = load_up(mover, ff_w, up_s)
    down_loads = load_down(mover, ff_w, down_s, S, F)
    wide, tall = 256, 256
    wait_all(loads)
    for i in range(L // tall):
        rows = slice(i * tall, i * tall + tall)
        for c in range(D // wide):
            cols = slice(c * wide, c * wide + wide)
            u_s[rows, cols] = dot_nn(o_s[rows, :], out_s[:, cols])
        unit, scale = norm_parts(u_s[rows, :])
        h = x_s[rows, :].astype(F32) + unit * gains[1:2, :]
        h_s[rows, :] = h
        unit, scale = norm_parts(h)
        b_s[rows, :] = (unit * gains[2:3, :]).astype(BF)
    own = pl.ds(pl.multiple_of(me * r, r), r)
    stores = [
        mover.start(b_s, b_out),
        mover.start(u_s.at[own], u_own),
        mover.start(h_s.at[own], h_own),
    ]
    wait_all(up_loads)
    root = math.sqrt(2.0 / math.pi)
    for c in range(H // wide):
        cols = slice(c * wide, c * wide + wide)
        z = dot_nn(b_s[...], up_s[:, cols])
        square = z * z
        bent = jnp.tanh(z * (root + root * 0.044715 * square))
        side = 0.5 + 0.5 * bent
        g_s[:, cols] = (z * side).astype(BF)
        slope = z * (root + 3.0 * root * 0.044715 * square)
        gp_s[:, cols] = (side + (0.5 * slope) * (1.0 - bent * bent)).astype(BF)
    stores += [mover.start(g_s, g_out), mover.start(gp_s, gp_out)]
    wait_all(down_loads)
    for c in range(D // wide):
        cols = slice(c * wide, c * wide + wide)
        m_s[:, cols] = dot_nn(g_s[...], down_s[:, cols]).astype(BF)
    stores += store_rows(mover, m_s, slots, order, me)
    wait_all(stores)


def feed(dims, turn, gains, ff_w, xs, os):
    S, F, r, D, W, H = dims
    L = S * r
    outs = [((L, D), BF), ((r, D), F32), ((r, D), F32), ((L, H), BF), ((L, H), BF)]
    outs += slot_shapes(S, turn, (r, D))
    scratch = [
        pltpu.VMEM((L, D), BF),
        pltpu.VMEM((L, D), BF),
        pltpu.VMEM((D, D), BF),
        pltpu.VMEM((L, D), F32),
        pltpu.VMEM((L, D), F32),
        pltpu.VMEM((D, H), BF),
        pltpu.VMEM((H, D), BF),
        pltpu.VMEM((L, D), BF),
        pltpu.VMEM((L, H), BF),
        pltpu.VMEM((L, H), BF),
        pltpu.VMEM((L, D), BF),
        pltpu.VMEM((8, D), F32),
        pltpu.SemaphoreType.DMA((4 * S + F * (H // W) + 7,)),
    ]
    return call(
        partial(feed_kernel, dims, slot_order(S, turn), turn),
        (gains, ff_w, *xs, *os),
        [any_spec()] * (2 + 2 * S),
        outs,
        [hbm_spec()] * len(outs),
        scratch,
        2 * L * D * D + 4 * L * D * H,
        2 * (D * D + 2 * D * H + 5 * L * D + 2 * L * H),
        "feed",
    )


def feed_back_kernel(dims, order, ff_w, gp, *refs):
    S, F, r, D, W, H = dims
    pieces, dm_out, dz_out, refs = refs[:S], *refs[S : S + 2], refs[S + 2 :]
    slots, refs = refs[: len(order)], refs[len(order) :]
    up_s, down_s, gp_s, dm_s, dz_s, part_s, sems = refs
    me = seq_place()
    mover = Mover(sems)
    loads = load_rows(mover, pieces, dm_s, me)
    down_loads = load_down(mover, ff_w, down_s, S, F)
    down_loads.append(mover.start(gp, gp_s))
    up_loads = load_up(mover, ff_w, up_s)
    wide = 256
    wait_all(loads)
    stores = [mover.start(dm_s, dm_out)]
    wait_all(down_loads)

    for c in range(H // wide):
        cols = slice(c * wide, c * wide + wide)
        grad = dot_nt(dm_s[...], down_s[cols, :])
        dz_s[:, cols] = (grad * gp_s[:, cols].astype(F32)).astype(BF)
    stores.append(mover.start(dz_s, dz_out))
    wait_all(up_loads)

    for c in range(D // wide):
        cols = slice(c * wide, c * wide + wide)
        part_s[:, cols] = dot_nt(dz_s[...], up_s[cols, :]).astype(BF)
    stores += store_rows(mover, part_s, slots, order, me)
    wait_all(stores)


def feed_back(dims, turn, ff_w, gp, pieces):
    S, F, r, D, W, H = dims
    L = S * r
    outs = [((L, D), BF), ((L, H), BF)] + slot_shapes(S, turn, (r, D))
    scratch = [
        pltpu.VMEM((D, H), BF),
        pltpu.VMEM((H, D), BF),
        pltpu.VMEM((L, H), BF),
        pltpu.VMEM((L, D), BF),
        pltpu.VMEM((L, H), BF),
        pltpu.VMEM((L, D), BF),
        pltpu.SemaphoreType.DMA((2 * S + F * (H // W) + 4,)),
    ]
    return call(
        partial(feed_back_kernel, dims, slot_order(S, turn)),
        (ff_w, gp, *pieces),
        [any_spec()] * (2 + S),
        outs,
        [hbm_spec()] * len(outs),
        scratch,
        4 * L * D * H,
        2 * (2 * D * H + 3 * L * D + 2 * L * H),
        "feed_back",
    )


def feed_outer_kernel(dims, count, *refs):
    S, F, D, W, H = dims
    ins, (out, *held, sum_s, sems) = refs[: 4 * count], refs[4 * count :]
    mover = Mover(sems)
    loads = [mover.start(a, b) for a, b in zip(ins, held)]
    g_rows, dm_rows = held[:count], held[count : 2 * count]
    b_rows, dz_rows = held[2 * count : 3 * count], held[3 * count :]
    wide = 256
    R = D // F
    tall = R * (H // W)
    stores = []
    wait_all(loads[: 2 * count])
    for c in range(D // wide):
        total = None
        for b in range(count):
            part = dot_tn(g_rows[b][...], dm_rows[b][:, c * wide : c * wide + wide])
            total = part if total is None else total + part
        total = total.astype(BF)
        for k in range(max(wide // W, 1)):
            for j in range(F // S):
                f = j * S + (c * wide) // W + k
                for i in range(H // W):
                    sum_s[f * R : f * R + R, H + i * W : H + i * W + W] = total[
                        j * tall + i * R : j * tall + i * R + R, k * W : k * W + W
                    ]
    stores.append(mover.start(sum_s.at[:, pl.ds(H, H)], out.at[:, pl.ds(H, H)]))
    wait_all(loads[2 * count :])
    for c in range(H // wide):
        total = None
        cols = slice(c * wide, c * wide + wide)
        for b in range(count):
            part = dot_tn(b_rows[b][...], dz_rows[b][:, cols])
            total = part if total is None else total + part
        sum_s[:, cols] = total.astype(BF)
        piece = pl.ds(c * wide, wide)
        stores.append(mover.start(sum_s.at[:, piece], out.at[:, piece]))
    wait_all(stores)


def feed_outer(dims, b_rows, dz_rows, g_rows, dm_rows):
    S, F, D, W, H = dims
    count = len(b_rows)
    L = b_rows[0].shape[0]
    operands = (*g_rows, *dm_rows, *b_rows, *dz_rows)
    return call(
        partial(feed_outer_kernel, dims, count),
        operands,
        [any_spec()] * len(operands),
        [((D, 2 * H), BF)],
        [hbm_spec()],
        [pltpu.VMEM(x.shape, BF) for x in operands]
        + [pltpu.VMEM((D, 2 * H), BF), pltpu.SemaphoreType.DMA((4 * count + 1 + H // 256,))],
        4 * count * L * D * H,
        2 * (count * 2 * L * (D + H) + 2 * D * H),
        "feed_outer",
    )[0]


def total_of(refs, rows):
    total = None
    for ref in refs:
        value = ref[0, rows, :].astype(F32)
        total = value if total is None else total + value
    return total


def column_sum(v):
    return jnp.sum(v, axis=0, keepdims=True)


def finish_kernel(turn, *refs):
    if turn:
        refs = refs[1:]
    count = (len(refs) - 6) // 2
    ins, (y_hbm, dm_hbm, stat_out), refs = refs[:count], refs[count : count + 3], refs[count + 3 :]
    held, (y_out, dm_out, sems) = refs[: len(ins)], refs[len(ins) :]
    mover = Mover(sems)
    wait_all([mover.start(a, b) for a, b in zip(ins, held)])
    gains, u_ref, h_ref, dy_ref, *terms = held
    half = dm_out.shape[0] // 2
    stats = [None] * 5
    for part in range(2):
        rows = slice(part * half, part * half + half)
        m = total_of(terms, rows)
        unit, scale = norm_parts(m)
        f = unit * gains[3:4, :]
        h = h_ref[rows, :]
        y = h + f
        y_out[rows, :] = y.astype(BF)
        dy = dy_ref[rows, :].astype(F32)
        dm = norm_back(dy * gains[3:4, :], unit, scale)
        dm_out[rows, :] = dm.astype(BF)
        if part == 1:
            stores = [mover.start(dm_out, dm_hbm), mover.start(y_out, y_hbm.at[turn])]
        second, unused = norm_parts(u_ref[rows, :])
        e = second * gains[1:2, :]
        values = [dy * unit, h * h, y * y, e * e, f * f]
        for index, value in enumerate(values):
            value = column_sum(value)
            stats[index] = value if part == 0 else stats[index] + value
    stat_out[...] = jnp.zeros_like(stat_out)
    for index in range(5):
        stat_out[3 + index : 4 + index, :] = stats[index]
    wait_all(stores)


def finish(turn, B, joined, gains, u, h, dy, terms):
    r, D = u.shape
    outs = [((B, r, D), BF), ((r, D), BF), ((8, D), F32)]
    operands = (gains, u, h, dy, *terms)
    first = [] if joined is None else [joined]
    return call(
        partial(finish_kernel, turn),
        (*first, *operands),
        [hbm_spec()] * len(first) + [any_spec()] * len(operands),
        outs,
        [hbm_spec(), hbm_spec(), vmem_spec()],
        [pltpu.VMEM(x.shape, x.dtype) for x in operands]
        + [pltpu.VMEM((r, D), BF)] * 2
        + [pltpu.SemaphoreType.DMA((len(operands) + 2,))],
        60 * r * D,
        r * D * 20,
        "finish",
        {0: 0} if first else {},
    )


def middle_kernel(*refs):
    count = (len(refs) - 6) // 2
    ins, (dh_out, du_hbm, stat_out), refs = refs[:count], refs[count : count + 3], refs[count + 3 :]
    held, (dh_s, du_out, sems) = refs[: len(ins)], refs[len(ins) :]
    mover = Mover(sems)
    wait_all([mover.start(a, b) for a, b in zip(ins, held)])
    gains, u_ref, h_ref, dy_ref, *terms = held
    r, D = u_ref.shape
    half = r // 2
    stats = [None] * 2
    for part in range(2):
        rows = slice(part * half, part * half + half)
        back = total_of(terms, rows)
        unit, scale = norm_parts(h_ref[rows, :])
        third = column_sum(back * unit)
        dh = dy_ref[rows, :].astype(F32) + norm_back(back * gains[2:3, :], unit, scale)
        dh_s[rows, :] = dh
        unit, scale = norm_parts(u_ref[rows, :])
        second = column_sum(dh * unit)
        du_out[rows, :] = norm_back(dh * gains[1:2, :], unit, scale).astype(BF)
        for index, value in enumerate((second, third)):
            stats[index] = value if part == 0 else stats[index] + value
    stores = [mover.start(du_out, du_hbm), mover.start(dh_s, dh_out)]
    stat_out[...] = jnp.zeros_like(stat_out)
    stat_out[1:2, :] = stats[0]
    stat_out[2:3, :] = stats[1]
    wait_all(stores)


def middle(gains, u, h, dy, terms):
    r, D = u.shape
    outs = [((r, D), F32), ((r, D), BF), ((8, D), F32)]
    operands = (gains, u, h, dy, *terms)
    return call(
        middle_kernel,
        operands,
        [any_spec()] * len(operands),
        outs,
        [hbm_spec(), hbm_spec(), vmem_spec()],
        [pltpu.VMEM(x.shape, x.dtype) for x in operands]
        + [
            pltpu.VMEM((r, D), F32),
            pltpu.VMEM((r, D), BF),
            pltpu.SemaphoreType.DMA((len(operands) + 2,)),
        ],
        60 * r * D,
        r * D * 24,
        "middle",
    )


def last_kernel(turn, *refs):
    if turn:
        refs = refs[1:]
    count = (len(refs) - 3) // 2
    ins, joined, held, (out, sems) = refs[:count], refs[count], refs[count + 1 : -2], refs[-2:]
    mover = Mover(sems)
    wait_all([mover.start(a, b) for a, b in zip(ins, held)])
    gains, x_ref, dh_ref, *terms = held
    r, D = x_ref.shape
    half = r // 2
    for part in range(2):
        rows = slice(part * half, part * half + half)
        back = total_of(terms, rows)
        unit, scale = norm_parts(x_ref[rows, :].astype(F32))
        grad = dh_ref[rows, :] + norm_back(back * gains[0:1, :], unit, scale)
        out[rows, :] = grad.astype(BF)
    mover.start(out, joined.at[turn]).wait()


def last(turn, B, joined, gains, x, dh, terms):
    r, D = x.shape
    operands = (gains, x, dh, *terms)
    first = [] if joined is None else [joined]
    return call(
        partial(last_kernel, turn),
        (*first, *operands),
        [hbm_spec()] * len(first) + [any_spec()] * len(operands),
        [((B, r, D), BF)],
        [hbm_spec()],
        [pltpu.VMEM(x.shape, x.dtype) for x in operands]
        + [pltpu.VMEM((r, D), BF), pltpu.SemaphoreType.DMA((len(operands) + 1,))],
        40 * r * D,
        r * D * 14,
        "last",
        {0: 0} if first else {},
    )[0]


def block_groups(F):
    return [[0, 2, 3, 4], [1, 5, 6, 7]] if F == 8 else [list(range(F))]


def out_grad_kernel(dims, count, *refs):
    S, F, D, W = dims
    groups = block_groups(F)
    ins, outs, refs = refs[: (1 + S) * count], refs[(1 + S) * count :], None
    outs, (*held, sum_s, sems) = outs[: len(groups)], outs[len(groups) :]
    mover = Mover(sems)
    o_rows, dus = held[:count], held[count:]
    loads = [mover.start(a, b) for a, b in zip(ins[:count], o_rows)]
    for b in range(count):
        pieces = ins[count + b * S : count + b * S + S]
        loads += load_rows(mover, pieces, dus[b], seq_place())
    R = D // F
    places = block_places(F)
    stores = []
    wait_all(loads)
    total = None
    for b in range(count):
        part = dot_tn(o_rows[b][...], dus[b][...])
        total = part if total is None else total + part
    sum_s[...] = total.astype(BF)
    for group, out in zip(groups, outs):
        for i, index in enumerate(group):
            row = pl.multiple_of(places[index] // S * R, R)
            col = pl.multiple_of(places[index] % S * W, W)
            stores.append(
                mover.start(
                    sum_s.at[pl.ds(row, R), pl.ds(col, W)], out.at[i, pl.ds(3 * R, R)]
                )
            )
    wait_all(stores)


def out_grad(dims, o_rows, dus):
    S, F, D, W = dims
    count = len(o_rows)
    L = o_rows[0].shape[0]
    groups = block_groups(F)
    operands = (*o_rows, *[piece for du in dus for piece in du])
    return call(
        partial(out_grad_kernel, dims, count),
        operands,
        [any_spec()] * len(operands),
        [((len(group), 4 * (D // F) + EXTRA, W), BF) for group in groups],
        [hbm_spec()] * len(groups),
        [pltpu.VMEM(x.shape, BF) for x in o_rows]
        + [pltpu.VMEM((L, D), BF)] * count
        + [pltpu.VMEM((W, D), BF), pltpu.SemaphoreType.DMA(((1 + S) * count + F,))],
        2 * count * L * D * W,
        2 * (count * L * (D + W) + D * W),
        "out_grad",
    )


def qkv_grad_kernel(dims, count, many, *refs):
    S, F, D, W = dims
    groups = block_groups(F)
    n = len(groups)
    stats, refs = refs[n : n + many], refs[n + many :]
    ins, refs = refs[: 2 * count], refs[2 * count :]
    outs, (*held, sum_s, stat_s, sems) = refs[:n], refs[n:]
    held_stats, held = held[:many], held[many:]
    mover = Mover(sems)
    early = [mover.start(a, b) for a, b in zip(stats, held_stats)]
    loads = [mover.start(a, b) for a, b in zip(ins, held)]
    a_rows, grads = held[:count], held[count:]
    R = D // F
    places = [pl.multiple_of(place * R, R) for place in block_places(F)]
    stores = []
    wait_all(early)
    if F == 8:
        total = held_stats[0][...]
        for other in held_stats[1:]:
            total = total + other[...]
        squares = total[4:8, 0:R]
        for i in range(1, F):
            squares = squares + total[4:8, i * R : i * R + R]
        joined = jnp.concatenate([total[0:4], jnp.concatenate([squares] * F, axis=1)], axis=0)
        stat_s[0:8, 0:D] = joined.astype(BF)
        stat_s[8:16, 0:D] = jnp.zeros_like(total).astype(BF)
        for group, out in zip(groups, outs):
            for i, index in enumerate(group):
                stores.append(
                    mover.start(
                        stat_s.at[:, pl.ds(places[index], R)],
                        out.at[i, pl.ds(4 * R, EXTRA), pl.ds(0, R)],
                    )
                )
    wait_all(loads)
    for t in range(3):
        cols = slice(t * W, t * W + W)
        total = None
        for b in range(count):
            part = dot_tn(a_rows[b][...], grads[b][:, cols])
            total = part if total is None else total + part
        sum_s[:, cols] = total.astype(BF)
        for group, out in zip(groups, outs):
            for i, index in enumerate(group):
                stores.append(
                    mover.start(
                        sum_s.at[pl.ds(places[index], R), pl.ds(t * W, W)],
                        out.at[i, pl.ds(t * R, R)],
                    )
                )
    wait_all(stores)


def qkv_grad(dims, parts, stats, a_rows, grads):
    S, F, D, W = dims
    count = len(a_rows)
    L = a_rows[0].shape[0]
    operands = (*parts, *stats, *a_rows, *grads)
    return pl.pallas_call(
        partial(qkv_grad_kernel, dims, count, len(stats)),
        out_shape=tuple(jax.ShapeDtypeStruct(part.shape, part.dtype) for part in parts),
        in_specs=[hbm_spec()] * len(parts) + [any_spec()] * (len(operands) - len(parts)),
        out_specs=tuple([hbm_spec()] * len(parts)),
        input_output_aliases={i: i for i in range(len(parts))},
        scratch_shapes=[pltpu.VMEM(x.shape, x.dtype) for x in (*stats, *a_rows, *grads)]
        + [
            pltpu.VMEM((D, 3 * W), BF),
            pltpu.VMEM((EXTRA, D), BF),
            pltpu.SemaphoreType.DMA((2 * count + len(stats) + 4 * F,)),
        ],
        compiler_params=pltpu.CompilerParams(vmem_limit_bytes=VMEM_LIMIT),
        name="qkv_grad",
    )(*operands)


def pair_sum_kernel(mine, got, *refs):
    outs, (mine_s, got_s, sum_s, sems) = refs[:4], refs[4:]
    mover = Mover(sems)
    loads = []
    for i in range(4):
        loads.append((mover.start(mine.at[i], mine_s.at[i]), mover.start(got.at[i], got_s.at[i])))
    stores = []
    for i in (3, 2, 1, 0):
        wait_all(loads[i])
        sum_s[i] = (mine_s[i].astype(F32) + got_s[i].astype(F32)).astype(BF)
        stores.append(mover.start(sum_s.at[i], outs[i]))
    wait_all(stores)


def pair_sum(mine, got):
    shape = mine.shape[1:]
    return call(
        pair_sum_kernel,
        (mine, got),
        [any_spec()] * 2,
        [(shape, BF)] * 4,
        [hbm_spec()] * 4,
        [pltpu.VMEM(mine.shape, BF)] * 3 + [pltpu.SemaphoreType.DMA((12,))],
        mine.size,
        6 * mine.size,
        "pair_sum",
    )


def last_sum_kernel(S, R, *refs):
    ins, (*moved, out_tile, stat_out), refs = refs[:4], refs[4:9], refs[9:]
    held, (sum_s, sems) = refs[:4], refs[4:]
    mover = Mover(sems)
    wait_all([mover.start(a, b) for a, b in zip(ins, held)])
    total = held[0][...].astype(F32)
    for ref in held[1:]:
        total = total + ref[...].astype(F32)
    sum_s[...] = total.astype(BF)
    stat_out[...] = total[4 * R : 4 * R + 8, 0 : stat_out.shape[1]]
    me = seq_place()
    stores = [mover.start(sum_s.at[pl.ds(3 * R, R)], out_tile)]
    for j in range(3):
        t = lax.rem((j - me + 3 * S) * (S % 3), 3)
        start = pl.multiple_of(t * R, R)
        stores.append(mover.start(sum_s.at[pl.ds(start, R)], moved[j].at[pl.ds(0, R)]))
        stores.append(
            mover.start(sum_s.at[pl.ds(4 * R, EXTRA)], moved[j].at[pl.ds(R, EXTRA)])
        )
    wait_all(stores)


def last_sum(S, R, terms):
    rows, W = terms[0].shape
    return call(
        partial(last_sum_kernel, S, R),
        tuple(terms),
        [any_spec()] * 4,
        [((R + EXTRA, W), BF)] * 3 + [((R, W), BF), ((8, R), F32)],
        [hbm_spec()] * 4 + [vmem_spec()],
        [pltpu.VMEM((rows, W), BF)] * 5 + [pltpu.SemaphoreType.DMA((11,))],
        4 * rows * W,
        10 * rows * W,
        "last_sum",
    )


def flip(bits, size):
    return [(i, i ^ bits) for i in range(size)]


def add_low(*terms):
    total = terms[0].astype(F32)
    for term in terms[1:]:
        total = total + term.astype(F32)
    return total.astype(BF)


def gather_slots(own, S, me, turn):
    if S != 4:
        full = lax.all_gather(own, "seq")
        return [
            lax.dynamic_index_in_dim(full, me ^ slot, 0, keepdims=False) for slot in range(S)
        ]
    far = lax.ppermute(own, "seq", flip(3, S))
    return [own] + [lax.ppermute(own, "seq", flip(j, S)) for j in (1, 2)] + [far]


def slot_order(S, turn):
    return [[slot] for slot in range(S)]


def slot_shapes(S, turn, shape):
    return [((len(group), *shape), BF) for group in slot_order(S, turn)]


def scatter_slots(groups, S, me, turn):
    if S != 4:
        order = jnp.take(jnp.concatenate(groups), me ^ jnp.arange(S), axis=0)
        return [lax.psum_scatter(order, "seq", scatter_dimension=0, tiled=True)]
    return [groups[0]] + [lax.ppermute(groups[j], "seq", flip(j, S)) for j in (3, 1, 2)]


def swap_slots(pieces, S):
    return [pieces[0]] + [lax.ppermute(pieces[j], "seq", flip(j, S)) for j in range(1, S)]


def sum_everywhere(v, S, F):
    if S != 4 or F != 8:
        return lax.psum(v, ("seq", "fsdp"))
    v = v + lax.ppermute(v, "fsdp", flip(1, F))
    v = v + lax.ppermute(v, "seq", flip(1, S))
    v = v + lax.ppermute(v, "seq", flip(2, S))
    v = v + lax.ppermute(v, "fsdp", flip(2, F))
    return v + lax.ppermute(v, "fsdp", flip(4, F))


def gather_blocks(block, F, early=()):
    if F != 8:
        return [lax.all_gather(block, "fsdp")]
    near = lax.ppermute(block, "fsdp", flip(1, F))
    far = [lax.ppermute(block, "fsdp", flip(j, F)) for j in (2, 4, 6)]
    far = after(far, near, *early)
    rest = [lax.ppermute(piece, "fsdp", flip(1, F)) for piece in far]
    return [piece[None] for piece in (block, near, *far, *rest)]


def after(value, *others):
    return lax.optimization_barrier((value, others))[0]


def blocks_in(blocks, S, me):
    moved = []
    for j in range(3):
        pairs = [(s, (3 * s + j) % S) for s in range(S)]
        moved.append(lax.ppermute(blocks[j], "seq", pairs))
    stack = jnp.stack(moved)
    return [
        lax.dynamic_index_in_dim(stack, (me + S * t) % 3, 0, keepdims=False) for t in range(3)
    ]


def blocks_out_pairs(S, j):
    return [((3 * s + j) % S, s) for s in range(S)]


def blocks_out(stack, S, me):
    moved = []
    for j in range(3):
        t = ((j - me) * (S % 3)) % 3
        piece = lax.dynamic_index_in_dim(stack, t, 0, keepdims=False)
        moved.append(lax.ppermute(piece, "seq", blocks_out_pairs(S, j)))
    return jnp.concatenate(moved, axis=1)


def turn_pairs(S, F):
    each = F // S
    return [
        (s * F + f, (f // each) * F + (f % each) * S + s) for s in range(S) for f in range(F)
    ]


def shards(tokens, cotangent, prefix, qkv_weight, out_weight, up_weight, down_weight, norm_gains):
    S, F = lax.axis_size("seq"), lax.axis_size("fsdp")
    B, r, D = tokens.shape
    heads = D // HEAD // S
    W = D // S
    R = D // F
    H = up_weight.shape[1]
    tiles = H // W
    me = seq_place()
    place = lax.axis_index("fsdp").astype(jnp.int32)
    pairs = turn_pairs(S, F)

    blocks = [qkv_weight[:, j * W : j * W + W] for j in range(3)]
    gain_rows = jnp.pad(norm_gains, ((0, EXTRA - 4), (0, W - R)))
    first_block = jnp.concatenate(blocks_in(blocks, S, me) + [gain_rows])
    tokens_late, down_late, out_late = tokens, down_weight, out_weight
    all_x = gather_slots(tokens_late, S, me, 0)
    stacks = gather_blocks(first_block, F, all_x)
    out_tiles = gather_slots(out_late, S, me, 0)
    down_mine = lax.ppermute(down_late, ("seq", "fsdp"), pairs)
    ff_mine = jnp.concatenate(
        [up_weight] + [down_mine[i * R : i * R + R] for i in range(tiles)] + out_tiles, axis=1
    )
    ff_full = lax.all_gather(ff_mine, "fsdp", axis=0, tiled=True)
    gains = None
    if F != 8:
        gains = lax.all_gather(norm_gains, "fsdp", axis=1, tiled=True).astype(F32)
        gains = jnp.pad(gains, ((0, 4), (0, 0)))
    att_dims = (S, F, r, D, heads)
    ff_dims = (S, F, r, D, W, H)
    a_all, qkv_all, p_all, os, os_own = [], [], [], [], []
    for b in range(B):
        a, qkv, o, p, gains_full = attend(att_dims, b, prefix, gains, stacks, all_x)
        a_all.append(a)
        qkv_all.append(qkv)
        p_all.append(p)
        os_own.append(o)
        os.append(gather_slots(o, S, me, b))
    gains = gains_full
    b_all, u_own, h_own, g_all, gp_all, m_terms = [], [], [], [], [], []
    for b in range(B):
        res = feed(ff_dims, b, gains, ff_full, all_x, os[b])
        b_all.append(res[0])
        u_own.append(res[1])
        h_own.append(res[2])
        g_all.append(res[3])
        gp_all.append(res[4])
        m_terms.append(scatter_slots(list(res[5:]), S, me, b))
    y, stats, dms = None, [], []
    for b in range(B):
        y, dm, stat = finish(b, B, y, gains, u_own[b], h_own[b], cotangent[b], m_terms[b])
        stats.append(stat)
        dms.append(gather_slots(dm, S, me, b))
    dm_all, dz_all, h_terms = [], [], []
    for b in range(B):
        res = feed_back(ff_dims, b, ff_full, gp_all[b], dms[b])
        dm_all.append(res[0])
        dz_all.append(res[1])
        h_terms.append(scatter_slots(list(res[2:]), S, me, b))
    dhs, dus = [], []
    for b in range(B):
        dh, du, stat = middle(gains, u_own[b], h_own[b], cotangent[b], h_terms[b])
        dhs.append(dh)
        dus.append(gather_slots(du, S, me, b))
        stats.append(stat)
    dm_all = after(dm_all, h_terms[0])
    ff_part = feed_outer((S, F, D, W, H), b_all, dz_all, g_all, dm_all)
    ff_sum = lax.psum_scatter(ff_part, "fsdp", scatter_dimension=0, tiled=True)
    back_pairs = [(b, a) for a, b in pairs]
    down_sum = jnp.concatenate(
        [ff_sum[:, H + i * W : H + i * W + W] for i in range(tiles)], axis=0
    )
    down_own = lax.ppermute(down_sum, ("seq", "fsdp"), back_pairs)
    down_grad = down_own.astype(F32)
    up_grad = ff_sum[:, :H].astype(F32)
    dqkvs, x_terms = [], []
    for b in range(B):
        res = attend_back(
            att_dims, b, gains, ff_full, stacks, a_all[b], qkv_all[b], p_all[b], dus[b]
        )
        dqkvs.append(res[0])
        stats.append(res[1])
        x_terms.append(scatter_slots(list(res[2:]), S, me, b))
    grad_dims = (S, F, D, W)
    parts = after(out_grad(grad_dims, os_own, dus), dqkvs)
    parts = after(parts, x_terms[0])
    parts = qkv_grad(grad_dims, parts, stats, a_all, dqkvs)
    if F == 8 and S == 4:
        kept = pair_sum(parts[0], lax.ppermute(parts[1], "fsdp", flip(1, F)))
        kept = after(kept, down_own)
        got = [lax.ppermute(kept[j], "fsdp", flip(2 * j, F)) for j in (3, 2, 1)]
        got = after(got, down_grad, up_grad)
        *moved, out_tile, stat = last_sum(S, R, [kept[0], *got])
        moved = [lax.ppermute(moved[j], "seq", blocks_out_pairs(S, j)) for j in range(3)]
        missed = lax.ppermute(stat, "seq", flip(3, S))
        for piece in moved:
            missed = missed + piece[R : R + 8, :R].astype(F32)
        qkv_own = jnp.concatenate([piece[:R] for piece in moved], axis=1)
        gains_grad, squares = missed[:4], jnp.sum(missed[4:], axis=1)
    else:
        rest = lax.psum_scatter(parts[0], "fsdp", scatter_dimension=0, tiled=False)
        qkv_own = blocks_out(jnp.stack([rest[t * R : t * R + R] for t in range(3)]), S, me)
        out_tile = rest[3 * R : 4 * R]
        totals = lax.psum(sum(stats), ("seq", "fsdp"))
        gains_grad = lax.dynamic_slice_in_dim(totals[:4], place * R, R, 1)
        squares = jnp.sum(totals[4:], axis=1)
    input_grad = None
    for b in range(B):
        input_grad = last(b, B, input_grad, gains, tokens[b], dhs[b], x_terms[b])

    out_own = lax.ppermute(out_tile, ("seq", "fsdp"), back_pairs)
    entries = B * r * D * S * F
    stream_rms = jnp.sqrt(squares / entries)
    return (
        y,
        input_grad,
        qkv_own.astype(F32),
        out_own.astype(F32),
        up_grad,
        down_grad,
        gains_grad,
        stream_rms,
    )


def solution(mesh):
    in_specs = (
        P("fsdp", "seq", None),
        P("fsdp", "seq", None),
        P("fsdp"),
        P("fsdp", "seq"),
        P("fsdp", "seq"),
        P("fsdp", "seq"),
        P("fsdp", "seq"),
        P(None, "fsdp"),
    )
    out_specs = (
        P("fsdp", "seq", None),
        P("fsdp", "seq", None),
        P("fsdp", "seq"),
        P("fsdp", "seq"),
        P("fsdp", "seq"),
        P("fsdp", "seq"),
        P(None, "fsdp"),
        P(),
    )
    return jax.shard_map(shards, mesh=mesh, in_specs=in_specs, out_specs=out_specs, check_vma=False)
```

```python
import math
from functools import partial

import jax
import jax.numpy as jnp
from jax import lax
from jax.experimental import pallas as pl
from jax.experimental.pallas import tpu as pltpu
from jax.sharding import PartitionSpec as P

HEAD = 64
NORM_EPSILON = 1e-05
MASKED_SCORE = -1e30
VMEM_LIMIT = 56 * 1024 * 1024
BF = jnp.bfloat16
F32 = jnp.float32
BLOCK_ORDER = (0, 1, 2, 4, 6, 3, 5, 7)
EXTRA = 16
COST = 0.001


def dot_nn(a, b):
    return lax.dot_general(a, b, (((1,), (0,)), ((), ())), preferred_element_type=F32)


def dot_nt(a, b):
    return lax.dot_general(a, b, (((1,), (1,)), ((), ())), preferred_element_type=F32)


def dot_tn(a, b):
    return lax.dot_general(a, b, (((0,), (0,)), ((), ())), preferred_element_type=F32)


def norm_parts(v):
    centre = jnp.mean(v, axis=-1, keepdims=True)
    shifted = v - centre
    spread = jnp.mean(shifted * shifted, axis=-1, keepdims=True)
    scale = lax.rsqrt(spread + NORM_EPSILON)
    return shifted * scale, scale


def norm_back(grad_unit, unit, scale):
    first = jnp.mean(grad_unit, axis=-1, keepdims=True)
    second = jnp.mean(grad_unit * unit, axis=-1, keepdims=True)
    return scale * (grad_unit - first - unit * second)


def seq_place():
    return lax.axis_index("seq").astype(jnp.int32)


def block_places(F):
    if F != 8:
        return [jnp.int32(i) for i in range(F)]
    place = lax.axis_index("fsdp").astype(jnp.int32)
    return [place ^ i for i in BLOCK_ORDER]


class Mover:
    def __init__(self, sems):
        self.sems = sems
        self.used = 0

    def start(self, src, dst):
        copy = pltpu.make_async_copy(src, dst, self.sems.at[self.used])
        self.used += 1
        copy.start()
        return copy


def wait_all(copies):
    for copy in copies:
        copy.wait()


def load_rows(mover, pieces, target, me):
    r = pieces[0].shape[0]
    copies = []
    for slot, piece in enumerate(pieces):
        start = pl.multiple_of((me ^ slot) * r, r)
        copies.append(mover.start(piece, target.at[pl.ds(start, r)]))
    return copies


def store_rows(mover, source, outs, order, me):
    r = outs[0].shape[1]
    copies = []
    for group, out in zip(order, outs):
        for i, slot in enumerate(group):
            start = pl.multiple_of((me ^ slot) * r, r)
            copies.append(mover.start(source.at[pl.ds(start, r)], out.at[i]))
    return copies


def load_blocks(mover, stacks, target, tiles):
    F = sum(stack.shape[0] for stack in stacks)
    places, copies, index = block_places(F), [], 0
    rows = target.shape[0] // F
    for stack in stacks:
        cols = stack.shape[2]
        for i in range(stack.shape[0]):
            start = pl.multiple_of(places[index] * rows, rows)
            index += 1
            for t in range(tiles):
                copies.append(
                    mover.start(
                        stack.at[i, pl.ds(t * rows, rows)],
                        target.at[pl.ds(start, rows), pl.ds(t * cols, cols)],
                    )
                )
    return copies


def load_gains(mover, stacks, target):
    F = sum(stack.shape[0] for stack in stacks)
    places, copies, index = block_places(F), [], 0
    width = target.shape[1] // F
    for stack in stacks:
        last = stack.shape[1] - EXTRA
        for i in range(stack.shape[0]):
            start = pl.multiple_of(places[index] * width, width)
            index += 1
            copies.append(
                mover.start(
                    stack.at[i, pl.ds(last, EXTRA), pl.ds(0, width)],
                    target.at[:, pl.ds(start, width)],
                )
            )
    return copies


def any_spec():
    return pl.BlockSpec(memory_space=pl.ANY)


def hbm_spec():
    return pl.BlockSpec(memory_space=pltpu.HBM)


def smem_spec():
    return pl.BlockSpec(memory_space=pltpu.SMEM)


def vmem_spec():
    return pl.BlockSpec(memory_space=pltpu.VMEM)


def call(body, operands, in_specs, outs, out_specs, scratch, flops, bytes_accessed, name, aliases={}):
    return pl.pallas_call(
        body,
        out_shape=tuple(jax.ShapeDtypeStruct(shape, dtype) for shape, dtype in outs),
        in_specs=in_specs,
        out_specs=tuple(out_specs),
        scratch_shapes=scratch,
        input_output_aliases=aliases,
        compiler_params=pltpu.CompilerParams(vmem_limit_bytes=VMEM_LIMIT),
        cost_estimate=pl.CostEstimate(
            flops=int(flops * COST), bytes_accessed=int(bytes_accessed * COST), transcendentals=0
        ),
        name=name,
    )(*operands)


def attend_kernel(dims, count, turn, packed, prefix, *refs):
    S, F, r, D, heads = dims
    L, W = S * r, heads * HEAD
    if packed:
        gains_in = None
    else:
        gains_in, refs = refs[0], refs[1:]
    weights, pieces, refs = refs[:count], refs[count : count + S], refs[count + S :]
    a_out, qkv_out, o_out, p_out, gains_out, refs = *refs[:5], refs[5:]
    x_s, w_s, a_s, qkv_s, o_s, p_s, bias_s, raw_s, sems = refs
    me, limit_len = seq_place(), prefix[turn]
    mover = Mover(sems)
    gain_loads = load_gains(mover, weights, raw_s) if packed else []
    loads = load_rows(mover, [piece.at[turn] for piece in pieces], x_s, me)
    weight_loads = load_blocks(mover, weights, w_s, 3)
    tile = 128
    limit = L // 2
    for i in range(L // tile):
        shape = (tile, max((i + 1) * tile, limit))
        rows = i * tile + lax.broadcasted_iota(jnp.int32, shape, 0)
        cols = lax.broadcasted_iota(jnp.int32, shape, 1)
        seen = (cols <= rows) | (cols < limit_len)
        bias_s[i * tile : i * tile + tile, : shape[1]] = jnp.where(seen, 0.0, MASKED_SCORE)
    wait_all(gain_loads)
    gains_out[...] = raw_s[0:8, :].astype(F32) if packed else gains_in[...]
    wait_all(loads)
    for i in range(L // tile):
        rows = slice(i * tile, i * tile + tile)
        unit, scale = norm_parts(x_s[rows, :].astype(F32))
        a_s[rows, :] = (unit * gains_out[0:1, :]).astype(BF)
    stores = [mover.start(a_s, a_out)]
    wait_all(weight_loads)
    for c in range(3):
        cols = slice(c * W, c * W + W)
        qkv_s[:, cols] = dot_nn(a_s[...], w_s[:, cols]).astype(BF)
    stores.append(mover.start(qkv_s, qkv_out))
    lane = lax.broadcasted_iota(jnp.int32, (1, 128), 1)
    for pair in range(heads // 2):
        q2 = qkv_s[:, pair * 128 : pair * 128 + 128] * BF(HEAD**-0.5)
        k2 = qkv_s[:, W + pair * 128 : W + pair * 128 + 128]
        v2 = qkv_s[:, 2 * W + pair * 128 : 2 * W + pair * 128 + 128]
        keys, values = [], []
        for side in range(2):
            mine = (lane >= 64) if side else (lane < 64)
            keys.append(jnp.where(mine, k2, BF(0)))
            values.append(jnp.where(mine, v2, BF(0)))
        for i in range(L // tile):
            rows = slice(i * tile, i * tile + tile)
            span = max((i + 1) * tile, limit)
            total = None
            for side in range(2):
                scores = dot_nt(q2[rows], keys[side][:span]) + bias_s[rows, :span]
                top = jnp.max(scores, axis=-1, keepdims=True)
                weights_here = jnp.exp(scores - top)
                share = 1.0 / jnp.sum(weights_here, axis=-1, keepdims=True)
                probs = (weights_here * share).astype(BF)
                p_s[2 * pair + side, rows, :span] = probs
                part = dot_nn(probs, values[side][:span])
                total = part if total is None else total + part
            o_s[rows, pair * 128 : pair * 128 + 128] = total.astype(BF)
        for side in range(2):
            stores.append(mover.start(p_s.at[2 * pair + side], p_out.at[2 * pair + side]))
    stores.append(mover.start(o_s, o_out))
    wait_all(stores)


def attend(dims, turn, prefix, gains, weights, pieces):
    S, F, r, D, heads = dims
    L, W = S * r, heads * HEAD
    outs = [((L, D), BF), ((L, 3 * W), BF), ((L, W), BF), ((heads, L, L), BF), ((8, D), F32)]
    scratch = [
        pltpu.VMEM((L, D), BF),
        pltpu.VMEM((D, 3 * W), BF),
        pltpu.VMEM((L, D), BF),
        pltpu.VMEM((L, 3 * W), BF),
        pltpu.VMEM((L, W), BF),
        pltpu.VMEM((heads, L, L), BF),
        pltpu.VMEM((L, L), F32),
        pltpu.VMEM((EXTRA, D), BF),
        pltpu.SemaphoreType.DMA((S + 4 * F + heads + 3,)),
    ]
    flops = 2 * L * D * 3 * W + 4 * heads * L * L * HEAD * 4
    size = 2 * (2 * L * D + 3 * D * W + 4 * L * W + heads * L * L)
    packed = gains is None
    extra = [] if packed else [gains]
    return call(
        partial(attend_kernel, dims, len(weights), turn, packed),
        (prefix, *extra, *weights, *pieces),
        [smem_spec()]
        + [vmem_spec()] * len(extra)
        + [any_spec()] * (len(weights) + len(pieces)),
        outs,
        [hbm_spec()] * 4 + [vmem_spec()],
        scratch,
        flops,
        size,
        "attend",
    )


def attend_back_kernel(dims, count, order, gains_in, out_w, *refs):
    S, F, r, D, heads = dims
    n = len(order)
    L, W = S * r, heads * HEAD
    weights, refs = refs[:count], refs[count:]
    a_in, qkv, probs_in, pieces, refs = *refs[:3], refs[3 : 3 + S], refs[3 + S :]
    grad_out, stat_out, slots, refs = *refs[:2], refs[2 : 2 + n], refs[2 + n :]
    w_s, qkv_s, p_s, du_s, do_s, d_s, grad_s, part_s, a_s, out_s, gains, sems = refs
    me = seq_place()
    mover = Mover(sems)
    own = pl.ds(pl.multiple_of(me * W, W), W)
    loads = load_out(mover, out_w, out_s, own, me, S) + load_rows(mover, pieces, du_s, me)
    loads.append(mover.start(qkv, qkv_s))
    prob_loads = [mover.start(probs_in.at[h], p_s.at[h]) for h in range(heads)]
    late_loads = load_blocks(mover, weights, w_s, 3)
    late_loads.append(mover.start(a_in, a_s))
    late_loads.append(mover.start(gains_in, gains))
    tile = 128
    limit = L // 2
    wait_all(loads)
    do_s[...] = dot_nt(du_s[...], out_s[...]).astype(BF)
    lane = lax.broadcasted_iota(jnp.int32, (1, 128), 1)
    for pair in range(heads // 2):
        cols = slice(pair * 128, pair * 128 + 128)
        q2 = qkv_s[:, cols] * BF(HEAD**-0.5)
        k2 = qkv_s[:, W + pair * 128 : W + pair * 128 + 128] * BF(HEAD**-0.5)
        v2 = qkv_s[:, 2 * W + pair * 128 : 2 * W + pair * 128 + 128]
        do2 = do_s[:, cols]
        queries, keys, values, grads = [], [], [], []
        for side in range(2):
            mine = (lane >= 64) if side else (lane < 64)
            queries.append(jnp.where(mine, q2, BF(0)))
            keys.append(jnp.where(mine, k2, BF(0)))
            values.append(jnp.where(mine, v2, BF(0)))
            grads.append(jnp.where(mine, do2, BF(0)))
            prob_loads[2 * pair + side].wait()
        for i in range(L // tile):
            rows = slice(i * tile, i * tile + tile)
            span = max((i + 1) * tile, limit)
            total = None
            for side in range(2):
                probs = p_s[2 * pair + side, rows, :span].astype(F32)
                grad_probs = dot_nt(do2[rows], values[side][:span])
                delta = jnp.sum(probs * grad_probs, axis=-1, keepdims=True)
                grad_scores = (probs * (grad_probs - delta)).astype(BF)
                d_s[side, rows, :span] = grad_scores
                part = dot_nn(grad_scores, keys[side][:span])
                total = part if total is None else total + part
            grad_s[rows, cols] = total.astype(BF)
        for j in range(L // tile):
            columns = slice(j * tile, j * tile + tile)
            low = 0 if (j * tile) < limit else j * tile
            total_k, total_v = None, None
            for side in range(2):
                part = dot_tn(d_s[side, low:, columns], queries[side][low:])
                total_k = part if total_k is None else total_k + part
                part = dot_tn(p_s[2 * pair + side, low:, columns], grads[side][low:])
                total_v = part if total_v is None else total_v + part
            grad_s[columns, W + pair * 128 : W + pair * 128 + 128] = total_k.astype(BF)
            grad_s[columns, 2 * W + pair * 128 : 2 * W + pair * 128 + 128] = total_v.astype(BF)
    stores = [mover.start(grad_s, grad_out)]
    wait_all(late_loads)
    wide = 256
    stat_out[...] = jnp.zeros_like(stat_out)

    for c in range(D // wide):
        cols = slice(c * wide, c * wide + wide)
        part = dot_nt(grad_s[...], w_s[cols, :])
        part_s[:, cols] = part.astype(BF)
        stat_out[0:1, cols] = column_sum(part * a_s[:, cols].astype(F32)) / gains[0:1, cols]
    stores += store_rows(mover, part_s, slots, order, me)
    wait_all(stores)


def attend_back(dims, turn, gains, out_w, weights, a, qkv, probs, pieces):
    S, F, r, D, heads = dims
    L, W = S * r, heads * HEAD
    outs = [((L, 3 * W), BF), ((8, D), F32)] + slot_shapes(S, turn, (r, D))
    blocks = 3 * F
    scratch = [
        pltpu.VMEM((D, 3 * W), BF),
        pltpu.VMEM((L, 3 * W), BF),
        pltpu.VMEM((heads, L, L), BF),
        pltpu.VMEM((L, D), BF),
        pltpu.VMEM((L, W), BF),
        pltpu.VMEM((2, L, L), BF),
        pltpu.VMEM((L, 3 * W), BF),
        pltpu.VMEM((L, D), BF),
        pltpu.VMEM((L, D), BF),
        pltpu.VMEM((W, D), BF),
        pltpu.VMEM((8, D), F32),
        pltpu.SemaphoreType.DMA((3 * S + heads + 5 + blocks,)),
    ]
    flops = 2 * L * D * 4 * W + 8 * heads * L * L * HEAD * 4
    size = 2 * (2 * L * D + 3 * D * W + 7 * L * W + heads * L * L)
    return call(
        partial(attend_back_kernel, dims, len(weights), slot_order(S, turn)),
        (gains, out_w, *weights, a, qkv, probs, *pieces),
        [any_spec()] * 2
        + [any_spec()] * (3 + len(weights) + len(pieces)),
        outs,
        [hbm_spec(), vmem_spec()] + [hbm_spec()] * (len(outs) - 2),
        scratch,
        flops,
        size,
        "attend_back",
    )


def load_out(mover, ff_w, target, rows, me, S):
    D = target.shape[1]
    W, base = D // S, ff_w.shape[1] - D
    copies = []
    for slot in range(S):
        start = pl.multiple_of((me ^ slot) * W, W)
        copies.append(
            mover.start(
                ff_w.at[rows, pl.ds(base + slot * W, W)], target.at[:, pl.ds(start, W)]
            )
        )
    return copies


def in_plane(S, F):
    return S == 4 and F == 8


def load_up(mover, ff_w, up_s, me, S, F):
    H = up_s.shape[1]
    if not in_plane(S, F):
        return [mover.start(ff_w.at[:, pl.ds(0, H)], up_s)]
    W, copies = H // S, []
    for slot in range(S):
        start = pl.multiple_of((me ^ slot) * W, W)
        copies.append(
            mover.start(ff_w.at[:, pl.ds(slot * W, W)], up_s.at[:, pl.ds(start, W)])
        )
    return copies


def down_places(D, H, me, S, F):
    W, R = D // S, D // F
    if in_plane(S, F):
        for f in range(F):
            for col in range(2):
                part = col ^ lax.div(me, 2)
                for t in range(2):
                    start = pl.multiple_of(H + (2 * part + t) * W, W)
                    yield (
                        (pl.ds(f * R, R), pl.ds(start, W)),
                        (pl.ds(f // 2 * 2 * R + t * R, R), pl.ds((f % 2 + 2 * col) * W, W)),
                    )
        return
    for f in range(F):
        for i in range(H // W):
            yield (
                (pl.ds(f * R, R), pl.ds(H + i * W, W)),
                (pl.ds(f // S * (R * (H // W)) + i * R, R), pl.ds(f % S * W, W)),
            )


def load_down(mover, ff_w, down_s, me, S, F):
    H, D = down_s.shape
    return [mover.start(ff_w.at[a], down_s.at[b]) for a, b in down_places(D, H, me, S, F)]


def feed_kernel(dims, order, turn, gains_in, ff_w, *refs):
    S, F, r, D, W, H = dims
    L, n = S * r, len(order)
    xs, os, refs = refs[:S], refs[S : 2 * S], refs[2 * S :]
    b_out, u_own, h_own, g_out, gp_out, slots, refs = *refs[:5], refs[5 : 5 + n], refs[5 + n :]
    x_s, o_s, out_s, u_s, h_s, up_s, down_s, b_s, g_s, gp_s, m_s, gains, sems = refs
    me = seq_place()
    mover = Mover(sems)
    loads = [mover.start(gains_in, gains)]
    for slot in range(S):
        start = pl.multiple_of((me ^ slot) * W, W)
        loads.append(mover.start(os[slot], o_s.at[:, pl.ds(start, W)]))
    loads += load_out(mover, ff_w, out_s, pl.ds(0, D), me, S)
    loads += load_rows(mover, [x.at[turn] for x in xs], x_s, me)
    up_loads = load_up(mover, ff_w, up_s, me, S, F)
    down_loads = load_down(mover, ff_w, down_s, me, S, F)
    wide, tall = 256, 256
    wait_all(loads)
    for i in range(L // tall):
        rows = slice(i * tall, i * tall + tall)
        for c in range(D // wide):
            cols = slice(c * wide, c * wide + wide)
            u_s[rows, cols] = dot_nn(o_s[rows, :], out_s[:, cols])
        unit, scale = norm_parts(u_s[rows, :])
        h = x_s[rows, :].astype(F32) + unit * gains[1:2, :]
        h_s[rows, :] = h
        unit, scale = norm_parts(h)
        b_s[rows, :] = (unit * gains[2:3, :]).astype(BF)
    own = pl.ds(pl.multiple_of(me * r, r), r)
    stores = [
        mover.start(b_s, b_out),
        mover.start(u_s.at[own], u_own),
        mover.start(h_s.at[own], h_own),
    ]
    wait_all(up_loads)
    root = math.sqrt(2.0 / math.pi)
    for c in range(H // wide):
        cols = slice(c * wide, c * wide + wide)
        z = dot_nn(b_s[...], up_s[:, cols])
        square = z * z
        bent = jnp.tanh(z * (root + root * 0.044715 * square))
        side = 0.5 + 0.5 * bent
        g_s[:, cols] = (z * side).astype(BF)
        slope = z * (root + 3.0 * root * 0.044715 * square)
        gp_s[:, cols] = (side + (0.5 * slope) * (1.0 - bent * bent)).astype(BF)
    stores += [mover.start(g_s, g_out), mover.start(gp_s, gp_out)]
    wait_all(down_loads)
    for c in range(D // wide):
        cols = slice(c * wide, c * wide + wide)
        m_s[:, cols] = dot_nn(g_s[...], down_s[:, cols]).astype(BF)
    stores += store_rows(mover, m_s, slots, order, me)
    wait_all(stores)


def feed(dims, turn, gains, ff_w, xs, os):
    S, F, r, D, W, H = dims
    L = S * r
    outs = [((L, D), BF), ((r, D), F32), ((r, D), F32), ((L, H), BF), ((L, H), BF)]
    outs += slot_shapes(S, turn, (r, D))
    scratch = [
        pltpu.VMEM((L, D), BF),
        pltpu.VMEM((L, D), BF),
        pltpu.VMEM((D, D), BF),
        pltpu.VMEM((L, D), F32),
        pltpu.VMEM((L, D), F32),
        pltpu.VMEM((D, H), BF),
        pltpu.VMEM((H, D), BF),
        pltpu.VMEM((L, D), BF),
        pltpu.VMEM((L, H), BF),
        pltpu.VMEM((L, H), BF),
        pltpu.VMEM((L, D), BF),
        pltpu.VMEM((8, D), F32),
        pltpu.SemaphoreType.DMA((5 * S + F * (H // W) + 7,)),
    ]
    return call(
        partial(feed_kernel, dims, slot_order(S, turn), turn),
        (gains, ff_w, *xs, *os),
        [any_spec()] * (2 + 2 * S),
        outs,
        [hbm_spec()] * len(outs),
        scratch,
        2 * L * D * D + 4 * L * D * H,
        2 * (D * D + 2 * D * H + 5 * L * D + 2 * L * H),
        "feed",
    )


def feed_back_kernel(dims, order, ff_w, gp, *refs):
    S, F, r, D, W, H = dims
    pieces, dm_out, dz_out, refs = refs[:S], *refs[S : S + 2], refs[S + 2 :]
    slots, refs = refs[: len(order)], refs[len(order) :]
    up_s, down_s, gp_s, dm_s, dz_s, part_s, sems = refs
    me = seq_place()
    mover = Mover(sems)
    loads = load_rows(mover, pieces, dm_s, me)
    down_loads = load_down(mover, ff_w, down_s, me, S, F)
    down_loads.append(mover.start(gp, gp_s))
    up_loads = load_up(mover, ff_w, up_s, me, S, F)
    wide = 256
    wait_all(loads)
    stores = [mover.start(dm_s, dm_out)]
    wait_all(down_loads)

    for c in range(H // wide):
        cols = slice(c * wide, c * wide + wide)
        grad = dot_nt(dm_s[...], down_s[cols, :])
        dz_s[:, cols] = (grad * gp_s[:, cols].astype(F32)).astype(BF)
    stores.append(mover.start(dz_s, dz_out))
    wait_all(up_loads)

    for c in range(D // wide):
        cols = slice(c * wide, c * wide + wide)
        part_s[:, cols] = dot_nt(dz_s[...], up_s[cols, :]).astype(BF)
    stores += store_rows(mover, part_s, slots, order, me)
    wait_all(stores)


def feed_back(dims, turn, ff_w, gp, pieces):
    S, F, r, D, W, H = dims
    L = S * r
    outs = [((L, D), BF), ((L, H), BF)] + slot_shapes(S, turn, (r, D))
    scratch = [
        pltpu.VMEM((D, H), BF),
        pltpu.VMEM((H, D), BF),
        pltpu.VMEM((L, H), BF),
        pltpu.VMEM((L, D), BF),
        pltpu.VMEM((L, H), BF),
        pltpu.VMEM((L, D), BF),
        pltpu.SemaphoreType.DMA((3 * S + F * (H // W) + 4,)),
    ]
    return call(
        partial(feed_back_kernel, dims, slot_order(S, turn)),
        (ff_w, gp, *pieces),
        [any_spec()] * (2 + S),
        outs,
        [hbm_spec()] * len(outs),
        scratch,
        4 * L * D * H,
        2 * (2 * D * H + 3 * L * D + 2 * L * H),
        "feed_back",
    )


def feed_outer_kernel(dims, count, *refs):
    S, F, D, W, H = dims
    ins, (out, *held, down_s, up_s, sems) = refs[: 4 * count], refs[4 * count :]
    me = seq_place()
    mover = Mover(sems)
    loads = [mover.start(a, b) for a, b in zip(ins, held)]
    g_rows, dm_rows = held[:count], held[count : 2 * count]
    b_rows, dz_rows = held[2 * count : 3 * count], held[3 * count :]
    wide = 256
    stores = []
    wait_all(loads[: 2 * count])
    for c in range(D // wide):
        total = None
        cols = slice(c * wide, c * wide + wide)
        for b in range(count):
            part = dot_tn(g_rows[b][...], dm_rows[b][:, cols])
            total = part if total is None else total + part
        down_s[:, cols] = total.astype(BF)
    stores += [
        mover.start(down_s.at[b], out.at[a]) for a, b in down_places(D, H, me, S, F)
    ]
    wait_all(loads[2 * count :])
    for c in range(H // wide):
        total = None
        cols = slice(c * wide, c * wide + wide)
        for b in range(count):
            part = dot_tn(b_rows[b][...], dz_rows[b][:, cols])
            total = part if total is None else total + part
        up_s[:, cols] = total.astype(BF)
        piece = pl.ds(c * wide, wide)
        target = piece
        if in_plane(S, F):
            target = pl.ds(pl.multiple_of((me ^ c) * wide, wide), wide)
        stores.append(mover.start(up_s.at[:, piece], out.at[:, target]))
    wait_all(stores)


def feed_outer(dims, b_rows, dz_rows, g_rows, dm_rows):
    S, F, D, W, H = dims
    count = len(b_rows)
    L = b_rows[0].shape[0]
    operands = (*g_rows, *dm_rows, *b_rows, *dz_rows)
    return call(
        partial(feed_outer_kernel, dims, count),
        operands,
        [any_spec()] * len(operands),
        [((D, 2 * H), BF)],
        [hbm_spec()],
        [pltpu.VMEM(x.shape, BF) for x in operands]
        + [
            pltpu.VMEM((H, D), BF),
            pltpu.VMEM((D, H), BF),
            pltpu.SemaphoreType.DMA((4 * count + F * (H // W) + H // 256,)),
        ],
        4 * count * L * D * H,
        2 * (count * 2 * L * (D + H) + 2 * D * H),
        "feed_outer",
    )[0]


def feed_last_kernel(S, F, *refs):
    came, got, (up_out, down_out, held, sems) = refs[:S], refs[S], refs[S + 1 :]
    me = seq_place()
    core = lax.rem(lax.axis_index("fsdp").astype(jnp.int32), 2)
    mover = Mover(sems)
    loads = [mover.start(a, held.at[j]) for j, a in enumerate(came)]
    R, W = up_out.shape[0], up_out.shape[1] // S
    wait_all(loads)
    for slot in range(S):
        start = pl.multiple_of((me ^ slot) * W, W)
        up_out[:, pl.ds(start, W)] = held[slot, 0:R, :].astype(F32)
    near = lax.rem(me, 2) == core
    for k in range(2):
        rows = slice(k * 2 * R, k * 2 * R + 2 * R)
        here = held[me ^ (2 * core + k), R : 3 * R, :]
        down_out[rows, :] = jnp.where(near, here, got[k]).astype(F32)


def feed_last(S, F, came, got):
    R, W = came[0].shape[0] // 3, came[0].shape[1]
    return call(
        partial(feed_last_kernel, S, F),
        (*came, got),
        [any_spec()] * S + [vmem_spec()],
        [((R, S * W), F32), ((4 * R, W), F32)],
        [vmem_spec()] * 2,
        [pltpu.VMEM((S, 3 * R, W), BF), pltpu.SemaphoreType.DMA((S,))],
        R * W * S,
        R * W * 40,
        "feed_last",
    )


def total_of(refs, rows):
    total = None
    for ref in refs:
        value = ref[0, rows, :].astype(F32)
        total = value if total is None else total + value
    return total


def column_sum(v):
    return jnp.sum(v, axis=0, keepdims=True)


def finish_kernel(turn, *refs):
    if turn:
        refs = refs[1:]
    count = (len(refs) - 6) // 2
    ins, (y_hbm, dm_hbm, stat_out), refs = refs[:count], refs[count : count + 3], refs[count + 3 :]
    held, (y_out, dm_out, sems) = refs[: len(ins)], refs[len(ins) :]
    mover = Mover(sems)
    wait_all([mover.start(a, b) for a, b in zip(ins, held)])
    gains, u_ref, h_ref, dy_ref, *terms = held
    half = dm_out.shape[0] // 2
    stats = [None] * 5
    for part in range(2):
        rows = slice(part * half, part * half + half)
        m = total_of(terms, rows)
        unit, scale = norm_parts(m)
        f = unit * gains[3:4, :]
        h = h_ref[rows, :]
        y = h + f
        y_out[rows, :] = y.astype(BF)
        dy = dy_ref[rows, :].astype(F32)
        dm = norm_back(dy * gains[3:4, :], unit, scale)
        dm_out[rows, :] = dm.astype(BF)
        if part == 1:
            stores = [mover.start(dm_out, dm_hbm), mover.start(y_out, y_hbm.at[turn])]
        second, unused = norm_parts(u_ref[rows, :])
        e = second * gains[1:2, :]
        values = [dy * unit, h * h, y * y, e * e, f * f]
        for index, value in enumerate(values):
            value = column_sum(value)
            stats[index] = value if part == 0 else stats[index] + value
    stat_out[...] = jnp.zeros_like(stat_out)
    for index in range(5):
        stat_out[3 + index : 4 + index, :] = stats[index]
    wait_all(stores)


def finish(turn, B, joined, gains, u, h, dy, terms):
    r, D = u.shape
    outs = [((B, r, D), BF), ((r, D), BF), ((8, D), F32)]
    operands = (gains, u, h, dy, *terms)
    first = [] if joined is None else [joined]
    return call(
        partial(finish_kernel, turn),
        (*first, *operands),
        [hbm_spec()] * len(first) + [any_spec()] * len(operands),
        outs,
        [hbm_spec(), hbm_spec(), vmem_spec()],
        [pltpu.VMEM(x.shape, x.dtype) for x in operands]
        + [pltpu.VMEM((r, D), BF)] * 2
        + [pltpu.SemaphoreType.DMA((len(operands) + 2,))],
        60 * r * D,
        r * D * 20,
        "finish",
        {0: 0} if first else {},
    )


def middle_kernel(*refs):
    count = (len(refs) - 6) // 2
    ins, (dh_out, du_hbm, stat_out), refs = refs[:count], refs[count : count + 3], refs[count + 3 :]
    held, (dh_s, du_out, sems) = refs[: len(ins)], refs[len(ins) :]
    mover = Mover(sems)
    wait_all([mover.start(a, b) for a, b in zip(ins, held)])
    gains, u_ref, h_ref, dy_ref, *terms = held
    r, D = u_ref.shape
    half = r // 2
    stats = [None] * 2
    for part in range(2):
        rows = slice(part * half, part * half + half)
        back = total_of(terms, rows)
        unit, scale = norm_parts(h_ref[rows, :])
        third = column_sum(back * unit)
        dh = dy_ref[rows, :].astype(F32) + norm_back(back * gains[2:3, :], unit, scale)
        dh_s[rows, :] = dh
        unit, scale = norm_parts(u_ref[rows, :])
        second = column_sum(dh * unit)
        du_out[rows, :] = norm_back(dh * gains[1:2, :], unit, scale).astype(BF)
        for index, value in enumerate((second, third)):
            stats[index] = value if part == 0 else stats[index] + value
    stores = [mover.start(du_out, du_hbm), mover.start(dh_s, dh_out)]
    stat_out[...] = jnp.zeros_like(stat_out)
    stat_out[1:2, :] = stats[0]
    stat_out[2:3, :] = stats[1]
    wait_all(stores)


def middle(gains, u, h, dy, terms):
    r, D = u.shape
    outs = [((r, D), F32), ((r, D), BF), ((8, D), F32)]
    operands = (gains, u, h, dy, *terms)
    return call(
        middle_kernel,
        operands,
        [any_spec()] * len(operands),
        outs,
        [hbm_spec(), hbm_spec(), vmem_spec()],
        [pltpu.VMEM(x.shape, x.dtype) for x in operands]
        + [
            pltpu.VMEM((r, D), F32),
            pltpu.VMEM((r, D), BF),
            pltpu.SemaphoreType.DMA((len(operands) + 2,)),
        ],
        60 * r * D,
        r * D * 24,
        "middle",
    )


def last_kernel(turn, *refs):
    if turn:
        refs = refs[1:]
    count = (len(refs) - 3) // 2
    ins, joined, held, (out, sems) = refs[:count], refs[count], refs[count + 1 : -2], refs[-2:]
    mover = Mover(sems)
    wait_all([mover.start(a, b) for a, b in zip(ins, held)])
    gains, x_ref, dh_ref, *terms = held
    r, D = x_ref.shape
    half = r // 2
    for part in range(2):
        rows = slice(part * half, part * half + half)
        back = total_of(terms, rows)
        unit, scale = norm_parts(x_ref[rows, :].astype(F32))
        grad = dh_ref[rows, :] + norm_back(back * gains[0:1, :], unit, scale)
        out[rows, :] = grad.astype(BF)
    mover.start(out, joined.at[turn]).wait()


def last(turn, B, joined, gains, x, dh, terms):
    r, D = x.shape
    operands = (gains, x, dh, *terms)
    first = [] if joined is None else [joined]
    return call(
        partial(last_kernel, turn),
        (*first, *operands),
        [hbm_spec()] * len(first) + [any_spec()] * len(operands),
        [((B, r, D), BF)],
        [hbm_spec()],
        [pltpu.VMEM(x.shape, x.dtype) for x in operands]
        + [pltpu.VMEM((r, D), BF), pltpu.SemaphoreType.DMA((len(operands) + 1,))],
        40 * r * D,
        r * D * 14,
        "last",
        {0: 0} if first else {},
    )[0]


def block_groups(F):
    return [[0, 2, 3, 4], [1, 5, 6, 7]] if F == 8 else [list(range(F))]


def out_grad_kernel(dims, count, *refs):
    S, F, D, W = dims
    groups = block_groups(F)
    ins, outs, refs = refs[: (1 + S) * count], refs[(1 + S) * count :], None
    outs, (*held, sum_s, sems) = outs[: len(groups)], outs[len(groups) :]
    mover = Mover(sems)
    o_rows, dus = held[:count], held[count:]
    loads = [mover.start(a, b) for a, b in zip(ins[:count], o_rows)]
    for b in range(count):
        pieces = ins[count + b * S : count + b * S + S]
        loads += load_rows(mover, pieces, dus[b], seq_place())
    R = D // F
    places = block_places(F)
    stores = []
    wait_all(loads)
    total = None
    for b in range(count):
        part = dot_tn(o_rows[b][...], dus[b][...])
        total = part if total is None else total + part
    sum_s[...] = total.astype(BF)
    for group, out in zip(groups, outs):
        for i, index in enumerate(group):
            row = pl.multiple_of(places[index] // S * R, R)
            col = pl.multiple_of(places[index] % S * W, W)
            stores.append(
                mover.start(
                    sum_s.at[pl.ds(row, R), pl.ds(col, W)], out.at[i, pl.ds(3 * R, R)]
                )
            )
    wait_all(stores)


def out_grad(dims, o_rows, dus):
    S, F, D, W = dims
    count = len(o_rows)
    L = o_rows[0].shape[0]
    groups = block_groups(F)
    operands = (*o_rows, *[piece for du in dus for piece in du])
    return call(
        partial(out_grad_kernel, dims, count),
        operands,
        [any_spec()] * len(operands),
        [((len(group), 4 * (D // F) + EXTRA, W), BF) for group in groups],
        [hbm_spec()] * len(groups),
        [pltpu.VMEM(x.shape, BF) for x in o_rows]
        + [pltpu.VMEM((L, D), BF)] * count
        + [pltpu.VMEM((W, D), BF), pltpu.SemaphoreType.DMA(((1 + S) * count + F,))],
        2 * count * L * D * W,
        2 * (count * L * (D + W) + D * W),
        "out_grad",
    )


def qkv_grad_kernel(dims, count, many, *refs):
    S, F, D, W = dims
    groups = block_groups(F)
    n = len(groups)
    stats, refs = refs[n : n + many], refs[n + many :]
    ins, refs = refs[: 2 * count], refs[2 * count :]
    outs, (*held, sum_s, stat_s, sems) = refs[:n], refs[n:]
    held_stats, held = held[:many], held[many:]
    mover = Mover(sems)
    early = [mover.start(a, b) for a, b in zip(stats, held_stats)]
    loads = [mover.start(a, b) for a, b in zip(ins, held)]
    a_rows, grads = held[:count], held[count:]
    R = D // F
    places = [pl.multiple_of(place * R, R) for place in block_places(F)]
    stores = []
    wait_all(early)
    if F == 8:
        total = held_stats[0][...]
        for other in held_stats[1:]:
            total = total + other[...]
        squares = total[4:8, 0:R]
        for i in range(1, F):
            squares = squares + total[4:8, i * R : i * R + R]
        joined = jnp.concatenate([total[0:4], jnp.concatenate([squares] * F, axis=1)], axis=0)
        stat_s[0:8, 0:D] = joined.astype(BF)
        stat_s[8:16, 0:D] = jnp.zeros_like(total).astype(BF)
        for group, out in zip(groups, outs):
            for i, index in enumerate(group):
                stores.append(
                    mover.start(
                        stat_s.at[:, pl.ds(places[index], R)],
                        out.at[i, pl.ds(4 * R, EXTRA), pl.ds(0, R)],
                    )
                )
    wait_all(loads)
    for t in range(3):
        cols = slice(t * W, t * W + W)
        total = None
        for b in range(count):
            part = dot_tn(a_rows[b][...], grads[b][:, cols])
            total = part if total is None else total + part
        sum_s[:, cols] = total.astype(BF)
        for group, out in zip(groups, outs):
            for i, index in enumerate(group):
                stores.append(
                    mover.start(
                        sum_s.at[pl.ds(places[index], R), pl.ds(t * W, W)],
                        out.at[i, pl.ds(t * R, R)],
                    )
                )
    wait_all(stores)


def qkv_grad(dims, parts, stats, a_rows, grads):
    S, F, D, W = dims
    count = len(a_rows)
    L = a_rows[0].shape[0]
    operands = (*parts, *stats, *a_rows, *grads)
    return pl.pallas_call(
        partial(qkv_grad_kernel, dims, count, len(stats)),
        out_shape=tuple(jax.ShapeDtypeStruct(part.shape, part.dtype) for part in parts),
        in_specs=[hbm_spec()] * len(parts) + [any_spec()] * (len(operands) - len(parts)),
        out_specs=tuple([hbm_spec()] * len(parts)),
        input_output_aliases={i: i for i in range(len(parts))},
        scratch_shapes=[pltpu.VMEM(x.shape, x.dtype) for x in (*stats, *a_rows, *grads)]
        + [
            pltpu.VMEM((D, 3 * W), BF),
            pltpu.VMEM((EXTRA, D), BF),
            pltpu.SemaphoreType.DMA((2 * count + len(stats) + 4 * F,)),
        ],
        compiler_params=pltpu.CompilerParams(vmem_limit_bytes=VMEM_LIMIT),
        name="qkv_grad",
    )(*operands)


def pair_sum_kernel(mine, got, *refs):
    outs, (mine_s, got_s, sum_s, sems) = refs[:4], refs[4:]
    mover = Mover(sems)
    loads = []
    for i in range(4):
        loads.append((mover.start(mine.at[i], mine_s.at[i]), mover.start(got.at[i], got_s.at[i])))
    stores = []
    for i in (3, 2, 1, 0):
        wait_all(loads[i])
        sum_s[i] = (mine_s[i].astype(F32) + got_s[i].astype(F32)).astype(BF)
        stores.append(mover.start(sum_s.at[i], outs[i]))
    wait_all(stores)


def pair_sum(mine, got):
    shape = mine.shape[1:]
    return call(
        pair_sum_kernel,
        (mine, got),
        [any_spec()] * 2,
        [(shape, BF)] * 4,
        [hbm_spec()] * 4,
        [pltpu.VMEM(mine.shape, BF)] * 3 + [pltpu.SemaphoreType.DMA((12,))],
        mine.size,
        6 * mine.size,
        "pair_sum",
    )


def last_sum_kernel(S, R, *refs):
    ins, (*moved, out_tile, stat_out), refs = refs[:4], refs[4:9], refs[9:]
    held, (sum_s, sems) = refs[:4], refs[4:]
    mover = Mover(sems)
    wait_all([mover.start(a, b) for a, b in zip(ins, held)])
    total = held[0][...].astype(F32)
    for ref in held[1:]:
        total = total + ref[...].astype(F32)
    sum_s[...] = total.astype(BF)
    stat_out[...] = total[4 * R : 4 * R + 8, 0 : stat_out.shape[1]]
    me = seq_place()
    stores = [mover.start(sum_s.at[pl.ds(3 * R, R)], out_tile)]
    for j in range(3):
        t = lax.rem((j - me + 3 * S) * (S % 3), 3)
        start = pl.multiple_of(t * R, R)
        stores.append(mover.start(sum_s.at[pl.ds(start, R)], moved[j].at[pl.ds(0, R)]))
        stores.append(
            mover.start(sum_s.at[pl.ds(4 * R, EXTRA)], moved[j].at[pl.ds(R, EXTRA)])
        )
    wait_all(stores)


def last_sum(S, R, terms):
    rows, W = terms[0].shape
    return call(
        partial(last_sum_kernel, S, R),
        tuple(terms),
        [any_spec()] * 4,
        [((R + EXTRA, W), BF)] * 3 + [((R, W), BF), ((8, R), F32)],
        [hbm_spec()] * 4 + [vmem_spec()],
        [pltpu.VMEM((rows, W), BF)] * 5 + [pltpu.SemaphoreType.DMA((11,))],
        4 * rows * W,
        10 * rows * W,
        "last_sum",
    )


def flip(bits, size):
    return [(i, i ^ bits) for i in range(size)]


def add_low(*terms):
    total = terms[0].astype(F32)
    for term in terms[1:]:
        total = total + term.astype(F32)
    return total.astype(BF)


def gather_slots(own, S, me, turn):
    if S != 4:
        full = lax.all_gather(own, "seq")
        return [
            lax.dynamic_index_in_dim(full, me ^ slot, 0, keepdims=False) for slot in range(S)
        ]
    far = lax.ppermute(own, "seq", flip(3, S))
    return [own] + [lax.ppermute(own, "seq", flip(j, S)) for j in (1, 2)] + [far]


def slot_order(S, turn):
    return [[slot] for slot in range(S)]


def slot_shapes(S, turn, shape):
    return [((len(group), *shape), BF) for group in slot_order(S, turn)]


def scatter_slots(groups, S, me, turn):
    if S != 4:
        order = jnp.take(jnp.concatenate(groups), me ^ jnp.arange(S), axis=0)
        return [lax.psum_scatter(order, "seq", scatter_dimension=0, tiled=True)]
    return [groups[0]] + [lax.ppermute(groups[j], "seq", flip(j, S)) for j in (3, 1, 2)]


def swap_slots(pieces, S):
    return [pieces[0]] + [lax.ppermute(pieces[j], "seq", flip(j, S)) for j in range(1, S)]


def sum_everywhere(v, S, F):
    if S != 4 or F != 8:
        return lax.psum(v, ("seq", "fsdp"))
    v = v + lax.ppermute(v, "fsdp", flip(1, F))
    v = v + lax.ppermute(v, "seq", flip(1, S))
    v = v + lax.ppermute(v, "seq", flip(2, S))
    v = v + lax.ppermute(v, "fsdp", flip(2, F))
    return v + lax.ppermute(v, "fsdp", flip(4, F))


def gather_blocks(block, F, early=()):
    if F != 8:
        return [lax.all_gather(block, "fsdp")]
    near = lax.ppermute(block, "fsdp", flip(1, F))
    far = [lax.ppermute(block, "fsdp", flip(j, F)) for j in (2, 4, 6)]
    far = after(far, near, *early)
    rest = [lax.ppermute(piece, "fsdp", flip(1, F)) for piece in far]
    return [piece[None] for piece in (block, near, *far, *rest)]


def after(value, *others):
    return lax.optimization_barrier((value, others))[0]


def blocks_in(blocks, S, me):
    moved = []
    for j in range(3):
        pairs = [(s, (3 * s + j) % S) for s in range(S)]
        moved.append(lax.ppermute(blocks[j], "seq", pairs))
    stack = jnp.stack(moved)
    return [
        lax.dynamic_index_in_dim(stack, (me + S * t) % 3, 0, keepdims=False) for t in range(3)
    ]


def blocks_out_pairs(S, j):
    return [((3 * s + j) % S, s) for s in range(S)]


def blocks_out(stack, S, me):
    moved = []
    for j in range(3):
        t = ((j - me) * (S % 3)) % 3
        piece = lax.dynamic_index_in_dim(stack, t, 0, keepdims=False)
        moved.append(lax.ppermute(piece, "seq", blocks_out_pairs(S, j)))
    return jnp.concatenate(moved, axis=1)


def turn_pairs(S, F):
    each = F // S
    return [
        (s * F + f, (f // each) * F + (f % each) * S + s) for s in range(S) for f in range(F)
    ]


def shards(tokens, cotangent, prefix, qkv_weight, out_weight, up_weight, down_weight, norm_gains):
    S, F = lax.axis_size("seq"), lax.axis_size("fsdp")
    B, r, D = tokens.shape
    heads = D // HEAD // S
    W = D // S
    R = D // F
    H = up_weight.shape[1]
    tiles = H // W
    me = seq_place()
    place = lax.axis_index("fsdp").astype(jnp.int32)
    pairs = turn_pairs(S, F)

    blocks = [qkv_weight[:, j * W : j * W + W] for j in range(3)]
    gain_rows = jnp.pad(norm_gains, ((0, EXTRA - 4), (0, W - R)))
    first_block = jnp.concatenate(blocks_in(blocks, S, me) + [gain_rows])
    tokens_late, down_late, out_late = tokens, down_weight, out_weight
    all_x = gather_slots(tokens_late, S, me, 0)
    stacks = gather_blocks(first_block, F, all_x)
    axes = ("seq", "fsdp")
    if in_plane(S, F):
        core = place % 2
        other = lax.ppermute(down_late, "fsdp", flip(1, F))
        halves = jnp.concatenate([down_late, other]).reshape(4, 2 * R, W)
        sent = []
        for j in range(S):
            target = me ^ j
            index = jnp.where(target // 2 == core, 0, 2) + target % 2
            piece = lax.dynamic_index_in_dim(halves, index, 0, keepdims=False)
            up_tile = lax.dynamic_slice_in_dim(up_weight, target * W, W, 1)
            sent.append(jnp.concatenate([up_tile, piece, out_late]))
        came = swap_slots(sent, S)
        ups = [message[:R] for message in came]
        out_tiles = [message[3 * R :] for message in came]
        near = (me % 2) ^ core == 0
        pieces = [
            jnp.where(near, came[2 * i][R : 3 * R], came[2 * i + 1][R : 3 * R])
            for i in range(2)
        ]
        downs = [piece[t * R : t * R + R] for piece in pieces for t in range(2)]
    else:
        ups = [up_weight]
        down_mine = lax.ppermute(down_late, axes, pairs)
        downs = [down_mine[i * R : i * R + R] for i in range(tiles)]
        out_tiles = gather_slots(out_late, S, me, 0)
    ff_mine = jnp.concatenate([*ups, *downs, *out_tiles], axis=1)
    ff_full = lax.all_gather(ff_mine, "fsdp", axis=0, tiled=True)
    gains = None
    if F != 8:
        gains = lax.all_gather(norm_gains, "fsdp", axis=1, tiled=True).astype(F32)
        gains = jnp.pad(gains, ((0, 4), (0, 0)))
    att_dims = (S, F, r, D, heads)
    ff_dims = (S, F, r, D, W, H)
    a_all, qkv_all, p_all, os, os_own = [], [], [], [], []
    for b in range(B):
        a, qkv, o, p, gains_full = attend(att_dims, b, prefix, gains, stacks, all_x)
        a_all.append(a)
        qkv_all.append(qkv)
        p_all.append(p)
        os_own.append(o)
        os.append(gather_slots(o, S, me, b))
    gains = gains_full
    b_all, u_own, h_own, g_all, gp_all, m_terms = [], [], [], [], [], []
    for b in range(B):
        res = feed(ff_dims, b, gains, ff_full, all_x, os[b])
        b_all.append(res[0])
        u_own.append(res[1])
        h_own.append(res[2])
        g_all.append(res[3])
        gp_all.append(res[4])
        m_terms.append(scatter_slots(list(res[5:]), S, me, b))
    y, stats, dms = None, [], []
    for b in range(B):
        y, dm, stat = finish(b, B, y, gains, u_own[b], h_own[b], cotangent[b], m_terms[b])
        stats.append(stat)
        dms.append(gather_slots(dm, S, me, b))
    dm_all, dz_all, h_terms = [], [], []
    for b in range(B):
        res = feed_back(ff_dims, b, ff_full, gp_all[b], dms[b])
        dm_all.append(res[0])
        dz_all.append(res[1])
        h_terms.append(scatter_slots(list(res[2:]), S, me, b))
    dhs, dus = [], []
    for b in range(B):
        dh, du, stat = middle(gains, u_own[b], h_own[b], cotangent[b], h_terms[b])
        dhs.append(dh)
        dus.append(gather_slots(du, S, me, b))
        stats.append(stat)
    dm_all = after(dm_all, h_terms[0])
    ff_part = feed_outer((S, F, D, W, H), b_all, dz_all, g_all, dm_all)
    ff_sum = lax.psum_scatter(ff_part, "fsdp", scatter_dimension=0, tiled=True)
    back_pairs = [(b, a) for a, b in pairs]
    if not in_plane(S, F):
        down_sum = jnp.concatenate(
            [ff_sum[:, H + i * W : H + i * W + W] for i in range(tiles)], axis=0
        )
        down_grad = lax.ppermute(down_sum, axes, back_pairs).astype(F32)
        up_grad = ff_sum[:, :H].astype(F32)
    dqkvs, x_terms = [], []
    for b in range(B):
        res = attend_back(
            att_dims, b, gains, ff_full, stacks, a_all[b], qkv_all[b], p_all[b], dus[b]
        )
        dqkvs.append(res[0])
        stats.append(res[1])
        x_terms.append(scatter_slots(list(res[2:]), S, me, b))
    grad_dims = (S, F, D, W)
    parts = after(out_grad(grad_dims, os_own, dus), dqkvs)
    parts = after(parts, x_terms[0])
    parts = qkv_grad(grad_dims, parts, stats, a_all, dqkvs)
    if F == 8 and S == 4:
        kept = pair_sum(parts[0], lax.ppermute(parts[1], "fsdp", flip(1, F)))
        ff_sum = after(ff_sum, kept)
        got = [lax.ppermute(kept[j], "fsdp", flip(2 * j, F)) for j in (3, 2, 1)]
        pieces = [ff_sum[:, H + i * W : H + i * W + W] for i in range(4)]
        sent = [
            jnp.concatenate([ff_sum[:, j * W : j * W + W], *pieces[j // 2 * 2 : j // 2 * 2 + 2]])
            for j in range(S)
        ]
        came = swap_slots(sent, S)
        got = after(got, came)
        whole = jnp.stack(after(came, got))[:, R:]
        away = jnp.stack(
            [
                lax.dynamic_index_in_dim(whole, me ^ (2 * (1 - place % 2) + k), 0, keepdims=False)
                for k in range(2)
            ]
        )
        up_grad, down_grad = feed_last(S, F, came, lax.ppermute(away, "fsdp", flip(1, F)))
        *moved, out_tile, stat = last_sum(S, R, [kept[0], *got])
        moved = [lax.ppermute(moved[j], "seq", blocks_out_pairs(S, j)) for j in range(3)]
        missed = lax.ppermute(stat, "seq", flip(3, S))
        for piece in moved:
            missed = missed + piece[R : R + 8, :R].astype(F32)
        qkv_own = jnp.concatenate([piece[:R] for piece in moved], axis=1)
        gains_grad, squares = missed[:4], jnp.sum(missed[4:], axis=1)
    else:
        rest = lax.psum_scatter(parts[0], "fsdp", scatter_dimension=0, tiled=False)
        qkv_own = blocks_out(jnp.stack([rest[t * R : t * R + R] for t in range(3)]), S, me)
        out_tile = rest[3 * R : 4 * R]
        totals = lax.psum(sum(stats), ("seq", "fsdp"))
        gains_grad = lax.dynamic_slice_in_dim(totals[:4], place * R, R, 1)
        squares = jnp.sum(totals[4:], axis=1)
    input_grad = None
    for b in range(B):
        input_grad = last(b, B, input_grad, gains, tokens[b], dhs[b], x_terms[b])

    out_own = lax.ppermute(out_tile, ("seq", "fsdp"), back_pairs)
    entries = B * r * D * S * F
    stream_rms = jnp.sqrt(squares / entries)
    return (
        y,
        input_grad,
        qkv_own.astype(F32),
        out_own.astype(F32),
        up_grad,
        down_grad,
        gains_grad,
        stream_rms,
    )


def solution(mesh):
    in_specs = (
        P("fsdp", "seq", None),
        P("fsdp", "seq", None),
        P("fsdp"),
        P("fsdp", "seq"),
        P("fsdp", "seq"),
        P("fsdp", "seq"),
        P("fsdp", "seq"),
        P(None, "fsdp"),
    )
    out_specs = (
        P("fsdp", "seq", None),
        P("fsdp", "seq", None),
        P("fsdp", "seq"),
        P("fsdp", "seq"),
        P("fsdp", "seq"),
        P("fsdp", "seq"),
        P(None, "fsdp"),
        P(),
    )
    return jax.shard_map(shards, mesh=mesh, in_specs=in_specs, out_specs=out_specs, check_vma=False)
```

```python
import math
from functools import partial

import jax
import jax.numpy as jnp
from jax import lax
from jax.experimental import pallas as pl
from jax.experimental.pallas import tpu as pltpu
from jax.sharding import PartitionSpec as P

HEAD = 64
NORM_EPSILON = 1e-05
MASKED_SCORE = -1e30
VMEM_LIMIT = 56 * 1024 * 1024
BF = jnp.bfloat16
F32 = jnp.float32
BLOCK_ORDER = (0, 1, 2, 4, 6, 3, 5, 7)
EXTRA = 16
COST = 0.001


def dot_nn(a, b):
    return lax.dot_general(a, b, (((1,), (0,)), ((), ())), preferred_element_type=F32)


def dot_nt(a, b):
    return lax.dot_general(a, b, (((1,), (1,)), ((), ())), preferred_element_type=F32)


def dot_tn(a, b):
    return lax.dot_general(a, b, (((0,), (0,)), ((), ())), preferred_element_type=F32)


def norm_parts(v):
    centre = jnp.mean(v, axis=-1, keepdims=True)
    shifted = v - centre
    spread = jnp.mean(shifted * shifted, axis=-1, keepdims=True)
    scale = lax.rsqrt(spread + NORM_EPSILON)
    return shifted * scale, scale


def norm_back(grad_unit, unit, scale):
    first = jnp.mean(grad_unit, axis=-1, keepdims=True)
    second = jnp.mean(grad_unit * unit, axis=-1, keepdims=True)
    return scale * (grad_unit - first - unit * second)


def seq_place():
    return lax.axis_index("seq").astype(jnp.int32)


def block_places(F):
    if F != 8:
        return [jnp.int32(i) for i in range(F)]
    place = lax.axis_index("fsdp").astype(jnp.int32)
    return [place ^ i for i in BLOCK_ORDER]


class Mover:
    def __init__(self, sems):
        self.sems = sems
        self.used = 0

    def start(self, src, dst):
        copy = pltpu.make_async_copy(src, dst, self.sems.at[self.used])
        self.used += 1
        copy.start()
        return copy


def wait_all(copies):
    for copy in copies:
        copy.wait()


def load_rows(mover, pieces, target, me):
    r = pieces[0].shape[0]
    copies = []
    for slot, piece in enumerate(pieces):
        start = pl.multiple_of((me ^ slot) * r, r)
        copies.append(mover.start(piece, target.at[pl.ds(start, r)]))
    return copies


def store_rows(mover, source, outs, order, me):
    r = outs[0].shape[1]
    copies = []
    for group, out in zip(order, outs):
        for i, slot in enumerate(group):
            start = pl.multiple_of((me ^ slot) * r, r)
            copies.append(mover.start(source.at[pl.ds(start, r)], out.at[i]))
    return copies


def in_plane(S, F):
    return S == 4 and F == 8


def block_at(s, slot):
    if slot == 1:
        return jnp.int32(1)
    odd = lax.rem(s, 2)
    return 2 * odd if slot == 0 else 2 - 2 * odd


def load_qkv(mover, weights, target, me, S, F):
    places, copies = block_places(F), []
    rows, cols = target.shape[0] // F, target.shape[1] // 3
    if in_plane(S, F):
        stacks, moved = weights[:F], weights[F:]
        for slot in range(3):
            sender = me ^ slot
            at = block_at(sender, slot)
            part = lax.div(3 * sender + at, S)
            col = pl.ds(pl.multiple_of(part * cols, cols), cols)
            from_col = pl.ds(pl.multiple_of(at * cols, cols), cols)
            for i in range(F):
                row = pl.ds(pl.multiple_of(places[i] * rows, rows), rows)
                if slot == 0:
                    source = stacks[i].at[0, pl.ds(0, rows), from_col]
                else:
                    source = moved[slot - 1].at[i]
                copies.append(mover.start(source, target.at[row, col]))
        return copies
    stack = weights[0]
    for i in range(F):
        row = pl.ds(pl.multiple_of(places[i] * rows, rows), rows)
        for t in range(3):
            copies.append(
                mover.start(
                    stack.at[i, pl.ds(t * rows, rows)], target.at[row, pl.ds(t * cols, cols)]
                )
            )
    return copies


def load_gains(mover, stacks, target, F):
    places, copies = block_places(F), []
    width = target.shape[1] // F
    for i, stack in enumerate(stacks[:F]):
        start = pl.multiple_of(places[i] * width, width)
        last = stack.shape[1] - EXTRA
        copies.append(
            mover.start(
                stack.at[0, pl.ds(last, EXTRA), pl.ds(0, width)],
                target.at[:, pl.ds(start, width)],
            )
        )
    return copies


def any_spec():
    return pl.BlockSpec(memory_space=pl.ANY)


def hbm_spec():
    return pl.BlockSpec(memory_space=pltpu.HBM)


def smem_spec():
    return pl.BlockSpec(memory_space=pltpu.SMEM)


def vmem_spec():
    return pl.BlockSpec(memory_space=pltpu.VMEM)


def call(body, operands, in_specs, outs, out_specs, scratch, flops, bytes_accessed, name, aliases={}):
    return pl.pallas_call(
        body,
        out_shape=tuple(jax.ShapeDtypeStruct(shape, dtype) for shape, dtype in outs),
        in_specs=in_specs,
        out_specs=tuple(out_specs),
        scratch_shapes=scratch,
        input_output_aliases=aliases,
        compiler_params=pltpu.CompilerParams(vmem_limit_bytes=VMEM_LIMIT),
        cost_estimate=pl.CostEstimate(
            flops=int(flops * COST), bytes_accessed=int(bytes_accessed * COST), transcendentals=0
        ),
        name=name,
    )(*operands)


def attend_kernel(dims, count, turn, packed, prefix, *refs):
    S, F, r, D, heads = dims
    L, W = S * r, heads * HEAD
    if packed:
        gains_in = None
    else:
        gains_in, refs = refs[0], refs[1:]
    weights, pieces, refs = refs[:count], refs[count : count + S], refs[count + S :]
    a_out, qkv_out, o_out, p_out, gains_out, refs = *refs[:5], refs[5:]
    x_s, w_s, a_s, qkv_s, o_s, p_s, bias_s, raw_s, sems = refs
    me, limit_len = seq_place(), prefix[turn]
    mover = Mover(sems)
    gain_loads = load_gains(mover, weights, raw_s, F) if packed else []
    loads = load_rows(mover, [piece.at[0] for piece in pieces], x_s, me)
    weight_loads = load_qkv(mover, weights, w_s, me, S, F)
    tile = 128
    limit = L // 2
    for i in range(L // tile):
        shape = (tile, max((i + 1) * tile, limit))
        rows = i * tile + lax.broadcasted_iota(jnp.int32, shape, 0)
        cols = lax.broadcasted_iota(jnp.int32, shape, 1)
        seen = (cols <= rows) | (cols < limit_len)
        bias_s[i * tile : i * tile + tile, : shape[1]] = jnp.where(seen, 0.0, MASKED_SCORE)
    wait_all(gain_loads)
    gains_out[...] = raw_s[0:8, :].astype(F32) if packed else gains_in[...]
    wait_all(loads)
    for i in range(L // tile):
        rows = slice(i * tile, i * tile + tile)
        unit, scale = norm_parts(x_s[rows, :].astype(F32))
        a_s[rows, :] = (unit * gains_out[0:1, :]).astype(BF)
    stores = [mover.start(a_s, a_out)]
    wait_all(weight_loads)
    for c in range(3):
        cols = slice(c * W, c * W + W)
        qkv_s[:, cols] = dot_nn(a_s[...], w_s[:, cols]).astype(BF)
    stores.append(mover.start(qkv_s, qkv_out))
    lane = lax.broadcasted_iota(jnp.int32, (1, 128), 1)
    for pair in range(heads // 2):
        q2 = qkv_s[:, pair * 128 : pair * 128 + 128] * BF(HEAD**-0.5)
        k2 = qkv_s[:, W + pair * 128 : W + pair * 128 + 128]
        v2 = qkv_s[:, 2 * W + pair * 128 : 2 * W + pair * 128 + 128]
        keys, values = [], []
        for side in range(2):
            mine = (lane >= 64) if side else (lane < 64)
            keys.append(jnp.where(mine, k2, BF(0)))
            values.append(jnp.where(mine, v2, BF(0)))
        for i in range(L // tile):
            rows = slice(i * tile, i * tile + tile)
            span = max((i + 1) * tile, limit)
            total = None
            for side in range(2):
                scores = dot_nt(q2[rows], keys[side][:span]) + bias_s[rows, :span]
                top = jnp.max(scores, axis=-1, keepdims=True)
                weights_here = jnp.exp(scores - top)
                share = 1.0 / jnp.sum(weights_here, axis=-1, keepdims=True)
                probs = (weights_here * share).astype(BF)
                p_s[2 * pair + side, rows, :span] = probs
                part = dot_nn(probs, values[side][:span])
                total = part if total is None else total + part
            o_s[rows, pair * 128 : pair * 128 + 128] = total.astype(BF)
        for side in range(2):
            stores.append(mover.start(p_s.at[2 * pair + side], p_out.at[2 * pair + side]))
    stores.append(mover.start(o_s, o_out))
    wait_all(stores)


def attend(dims, turn, prefix, gains, weights, pieces):
    S, F, r, D, heads = dims
    L, W = S * r, heads * HEAD
    outs = [((L, D), BF), ((L, 3 * W), BF), ((L, W), BF), ((heads, L, L), BF), ((8, D), F32)]
    scratch = [
        pltpu.VMEM((L, D), BF),
        pltpu.VMEM((D, 3 * W), BF),
        pltpu.VMEM((L, D), BF),
        pltpu.VMEM((L, 3 * W), BF),
        pltpu.VMEM((L, W), BF),
        pltpu.VMEM((heads, L, L), BF),
        pltpu.VMEM((L, L), F32),
        pltpu.VMEM((EXTRA, D), BF),
        pltpu.SemaphoreType.DMA((S + 4 * F + heads + 3,)),
    ]
    flops = 2 * L * D * 3 * W + 4 * heads * L * L * HEAD * 4
    size = 2 * (2 * L * D + 3 * D * W + 4 * L * W + heads * L * L)
    packed = gains is None
    extra = [] if packed else [gains]
    return call(
        partial(attend_kernel, dims, len(weights), turn, packed),
        (prefix, *extra, *weights, *pieces),
        [smem_spec()]
        + [vmem_spec()] * len(extra)
        + [any_spec()] * (len(weights) + len(pieces)),
        outs,
        [hbm_spec()] * 4 + [vmem_spec()],
        scratch,
        flops,
        size,
        "attend",
    )


def attend_back_kernel(dims, count, order, gains_in, out_w, *refs):
    S, F, r, D, heads = dims
    n = len(order)
    L, W = S * r, heads * HEAD
    weights, refs = refs[:count], refs[count:]
    a_in, qkv, probs_in, pieces, refs = *refs[:3], refs[3 : 3 + S], refs[3 + S :]
    grad_out, stat_out, slots, refs = *refs[:2], refs[2 : 2 + n], refs[2 + n :]
    w_s, qkv_s, p_s, du_s, do_s, d_s, grad_s, part_s, a_s, out_s, gains, sems = refs
    me = seq_place()
    mover = Mover(sems)
    own = pl.ds(pl.multiple_of(me * W, W), W)
    loads = load_out(mover, out_w, out_s, own, me, S) + load_rows(mover, pieces, du_s, me)
    loads.append(mover.start(qkv, qkv_s))
    prob_loads = [mover.start(probs_in.at[h], p_s.at[h]) for h in range(heads)]
    late_loads = load_qkv(mover, weights, w_s, me, S, F)
    late_loads.append(mover.start(a_in, a_s))
    late_loads.append(mover.start(gains_in, gains))
    tile = 128
    limit = L // 2
    wait_all(loads)
    do_s[...] = dot_nt(du_s[...], out_s[...]).astype(BF)
    lane = lax.broadcasted_iota(jnp.int32, (1, 128), 1)
    for pair in range(heads // 2):
        cols = slice(pair * 128, pair * 128 + 128)
        q2 = qkv_s[:, cols] * BF(HEAD**-0.5)
        k2 = qkv_s[:, W + pair * 128 : W + pair * 128 + 128] * BF(HEAD**-0.5)
        v2 = qkv_s[:, 2 * W + pair * 128 : 2 * W + pair * 128 + 128]
        do2 = do_s[:, cols]
        queries, keys, values, grads = [], [], [], []
        for side in range(2):
            mine = (lane >= 64) if side else (lane < 64)
            queries.append(jnp.where(mine, q2, BF(0)))
            keys.append(jnp.where(mine, k2, BF(0)))
            values.append(jnp.where(mine, v2, BF(0)))
            grads.append(jnp.where(mine, do2, BF(0)))
            prob_loads[2 * pair + side].wait()
        for i in range(L // tile):
            rows = slice(i * tile, i * tile + tile)
            span = max((i + 1) * tile, limit)
            total = None
            for side in range(2):
                probs = p_s[2 * pair + side, rows, :span].astype(F32)
                grad_probs = dot_nt(do2[rows], values[side][:span])
                delta = jnp.sum(probs * grad_probs, axis=-1, keepdims=True)
                grad_scores = (probs * (grad_probs - delta)).astype(BF)
                d_s[side, rows, :span] = grad_scores
                part = dot_nn(grad_scores, keys[side][:span])
                total = part if total is None else total + part
            grad_s[rows, cols] = total.astype(BF)
        for j in range(L // tile):
            columns = slice(j * tile, j * tile + tile)
            low = 0 if (j * tile) < limit else j * tile
            total_k, total_v = None, None
            for side in range(2):
                part = dot_tn(d_s[side, low:, columns], queries[side][low:])
                total_k = part if total_k is None else total_k + part
                part = dot_tn(p_s[2 * pair + side, low:, columns], grads[side][low:])
                total_v = part if total_v is None else total_v + part
            grad_s[columns, W + pair * 128 : W + pair * 128 + 128] = total_k.astype(BF)
            grad_s[columns, 2 * W + pair * 128 : 2 * W + pair * 128 + 128] = total_v.astype(BF)
    stores = [mover.start(grad_s, grad_out)]
    wait_all(late_loads)
    wide = 256
    stat_out[...] = jnp.zeros_like(stat_out)

    for c in range(D // wide):
        cols = slice(c * wide, c * wide + wide)
        part = dot_nt(grad_s[...], w_s[cols, :])
        part_s[:, cols] = part.astype(BF)
        stat_out[0:1, cols] = column_sum(part * a_s[:, cols].astype(F32)) / gains[0:1, cols]
    stores += store_rows(mover, part_s, slots, order, me)
    wait_all(stores)


def attend_back(dims, turn, gains, out_w, weights, a, qkv, probs, pieces):
    S, F, r, D, heads = dims
    L, W = S * r, heads * HEAD
    outs = [((L, 3 * W), BF), ((8, D), F32)] + slot_shapes(S, turn, (r, D))
    blocks = 3 * F
    scratch = [
        pltpu.VMEM((D, 3 * W), BF),
        pltpu.VMEM((L, 3 * W), BF),
        pltpu.VMEM((heads, L, L), BF),
        pltpu.VMEM((L, D), BF),
        pltpu.VMEM((L, W), BF),
        pltpu.VMEM((2, L, L), BF),
        pltpu.VMEM((L, 3 * W), BF),
        pltpu.VMEM((L, D), BF),
        pltpu.VMEM((L, D), BF),
        pltpu.VMEM((W, D), BF),
        pltpu.VMEM((8, D), F32),
        pltpu.SemaphoreType.DMA((3 * S + heads + 5 + blocks,)),
    ]
    flops = 2 * L * D * 4 * W + 8 * heads * L * L * HEAD * 4
    size = 2 * (2 * L * D + 3 * D * W + 7 * L * W + heads * L * L)
    return call(
        partial(attend_back_kernel, dims, len(weights), slot_order(S, turn)),
        (gains, out_w, *weights, a, qkv, probs, *pieces),
        [any_spec()] * 2
        + [any_spec()] * (3 + len(weights) + len(pieces)),
        outs,
        [hbm_spec(), vmem_spec()] + [hbm_spec()] * (len(outs) - 2),
        scratch,
        flops,
        size,
        "attend_back",
    )


def load_out(mover, ff_w, target, rows, me, S):
    D = target.shape[1]
    W, base = D // S, ff_w.shape[1] - D
    copies = []
    for slot in range(S):
        start = pl.multiple_of((me ^ slot) * W, W)
        copies.append(
            mover.start(
                ff_w.at[rows, pl.ds(base + slot * W, W)], target.at[:, pl.ds(start, W)]
            )
        )
    return copies


def load_up(mover, ff_w, up_s, me, S, F):
    H = up_s.shape[1]
    if not in_plane(S, F):
        return [mover.start(ff_w.at[:, pl.ds(0, H)], up_s)]
    W, copies = H // S, []
    for slot in range(S):
        start = pl.multiple_of((me ^ slot) * W, W)
        copies.append(
            mover.start(ff_w.at[:, pl.ds(slot * W, W)], up_s.at[:, pl.ds(start, W)])
        )
    return copies


def down_places(D, H, me, S, F):
    W, R = D // S, D // F
    if in_plane(S, F):
        for f in range(F):
            for col in range(2):
                part = col ^ lax.div(me, 2)
                for t in range(2):
                    start = pl.multiple_of(H + (2 * part + t) * W, W)
                    yield (
                        (pl.ds(f * R, R), pl.ds(start, W)),
                        (pl.ds(f // 2 * 2 * R + t * R, R), pl.ds((f % 2 + 2 * col) * W, W)),
                    )
        return
    for f in range(F):
        for i in range(H // W):
            yield (
                (pl.ds(f * R, R), pl.ds(H + i * W, W)),
                (pl.ds(f // S * (R * (H // W)) + i * R, R), pl.ds(f % S * W, W)),
            )


def load_down(mover, ff_w, down_s, me, S, F):
    H, D = down_s.shape
    return [mover.start(ff_w.at[a], down_s.at[b]) for a, b in down_places(D, H, me, S, F)]


def feed_kernel(dims, order, turn, gains_in, ff_w, *refs):
    S, F, r, D, W, H = dims
    L, n = S * r, len(order)
    xs, os, refs = refs[:S], refs[S : 2 * S], refs[2 * S :]
    b_out, u_own, h_own, g_out, gp_out, slots, refs = *refs[:5], refs[5 : 5 + n], refs[5 + n :]
    x_s, o_s, out_s, u_s, h_s, up_s, down_s, b_s, g_s, gp_s, m_s, gains, sems = refs
    me = seq_place()
    mover = Mover(sems)
    loads = [mover.start(gains_in, gains)]
    for slot in range(S):
        start = pl.multiple_of((me ^ slot) * W, W)
        loads.append(mover.start(os[slot], o_s.at[:, pl.ds(start, W)]))
    loads += load_out(mover, ff_w, out_s, pl.ds(0, D), me, S)
    loads += load_rows(mover, [x.at[0] for x in xs], x_s, me)
    up_loads = load_up(mover, ff_w, up_s, me, S, F)
    down_loads = load_down(mover, ff_w, down_s, me, S, F)
    wide, tall = 256, 256
    wait_all(loads)
    for i in range(L // tall):
        rows = slice(i * tall, i * tall + tall)
        for c in range(D // wide):
            cols = slice(c * wide, c * wide + wide)
            u_s[rows, cols] = dot_nn(o_s[rows, :], out_s[:, cols])
        unit, scale = norm_parts(u_s[rows, :])
        h = x_s[rows, :].astype(F32) + unit * gains[1:2, :]
        h_s[rows, :] = h
        unit, scale = norm_parts(h)
        b_s[rows, :] = (unit * gains[2:3, :]).astype(BF)
    own = pl.ds(pl.multiple_of(me * r, r), r)
    stores = [
        mover.start(b_s, b_out),
        mover.start(u_s.at[own], u_own),
        mover.start(h_s.at[own], h_own),
    ]
    wait_all(up_loads)
    root = math.sqrt(2.0 / math.pi)
    for c in range(H // wide):
        cols = slice(c * wide, c * wide + wide)
        z = dot_nn(b_s[...], up_s[:, cols])
        square = z * z
        bent = jnp.tanh(z * (root + root * 0.044715 * square))
        side = 0.5 + 0.5 * bent
        g_s[:, cols] = (z * side).astype(BF)
        slope = z * (root + 3.0 * root * 0.044715 * square)
        gp_s[:, cols] = (side + (0.5 * slope) * (1.0 - bent * bent)).astype(BF)
    stores += [mover.start(g_s, g_out), mover.start(gp_s, gp_out)]
    wait_all(down_loads)
    for c in range(D // wide):
        cols = slice(c * wide, c * wide + wide)
        m_s[:, cols] = dot_nn(g_s[...], down_s[:, cols]).astype(BF)
    stores += store_rows(mover, m_s, slots, order, me)
    wait_all(stores)


def feed(dims, turn, gains, ff_w, xs, os):
    S, F, r, D, W, H = dims
    L = S * r
    outs = [((L, D), BF), ((r, D), F32), ((r, D), F32), ((L, H), BF), ((L, H), BF)]
    outs += slot_shapes(S, turn, (r, D))
    scratch = [
        pltpu.VMEM((L, D), BF),
        pltpu.VMEM((L, D), BF),
        pltpu.VMEM((D, D), BF),
        pltpu.VMEM((L, D), F32),
        pltpu.VMEM((L, D), F32),
        pltpu.VMEM((D, H), BF),
        pltpu.VMEM((H, D), BF),
        pltpu.VMEM((L, D), BF),
        pltpu.VMEM((L, H), BF),
        pltpu.VMEM((L, H), BF),
        pltpu.VMEM((L, D), BF),
        pltpu.VMEM((8, D), F32),
        pltpu.SemaphoreType.DMA((5 * S + F * (H // W) + 7,)),
    ]
    return call(
        partial(feed_kernel, dims, slot_order(S, turn), turn),
        (gains, ff_w, *xs, *os),
        [any_spec()] * (2 + 2 * S),
        outs,
        [hbm_spec()] * len(outs),
        scratch,
        2 * L * D * D + 4 * L * D * H,
        2 * (D * D + 2 * D * H + 5 * L * D + 2 * L * H),
        "feed",
    )


def feed_back_kernel(dims, order, ff_w, gp, *refs):
    S, F, r, D, W, H = dims
    pieces, dm_out, dz_out, refs = refs[:S], *refs[S : S + 2], refs[S + 2 :]
    slots, refs = refs[: len(order)], refs[len(order) :]
    up_s, down_s, gp_s, dm_s, dz_s, part_s, sems = refs
    me = seq_place()
    mover = Mover(sems)
    loads = load_rows(mover, pieces, dm_s, me)
    down_loads = load_down(mover, ff_w, down_s, me, S, F)
    down_loads.append(mover.start(gp, gp_s))
    up_loads = load_up(mover, ff_w, up_s, me, S, F)
    wide = 256
    wait_all(loads)
    stores = [mover.start(dm_s, dm_out)]
    wait_all(down_loads)

    for c in range(H // wide):
        cols = slice(c * wide, c * wide + wide)
        grad = dot_nt(dm_s[...], down_s[cols, :])
        dz_s[:, cols] = (grad * gp_s[:, cols].astype(F32)).astype(BF)
    stores.append(mover.start(dz_s, dz_out))
    wait_all(up_loads)

    for c in range(D // wide):
        cols = slice(c * wide, c * wide + wide)
        part_s[:, cols] = dot_nt(dz_s[...], up_s[cols, :]).astype(BF)
    stores += store_rows(mover, part_s, slots, order, me)
    wait_all(stores)


def feed_back(dims, turn, ff_w, gp, pieces):
    S, F, r, D, W, H = dims
    L = S * r
    outs = [((L, D), BF), ((L, H), BF)] + slot_shapes(S, turn, (r, D))
    scratch = [
        pltpu.VMEM((D, H), BF),
        pltpu.VMEM((H, D), BF),
        pltpu.VMEM((L, H), BF),
        pltpu.VMEM((L, D), BF),
        pltpu.VMEM((L, H), BF),
        pltpu.VMEM((L, D), BF),
        pltpu.SemaphoreType.DMA((3 * S + F * (H // W) + 4,)),
    ]
    return call(
        partial(feed_back_kernel, dims, slot_order(S, turn)),
        (ff_w, gp, *pieces),
        [any_spec()] * (2 + S),
        outs,
        [hbm_spec()] * len(outs),
        scratch,
        4 * L * D * H,
        2 * (2 * D * H + 3 * L * D + 2 * L * H),
        "feed_back",
    )


def feed_outer_kernel(dims, count, *refs):
    S, F, D, W, H = dims
    ins, (out, *held, down_s, up_s, sems) = refs[: 4 * count], refs[4 * count :]
    me = seq_place()
    mover = Mover(sems)
    loads = [mover.start(a, b) for a, b in zip(ins, held)]
    g_rows, dm_rows = held[:count], held[count : 2 * count]
    b_rows, dz_rows = held[2 * count : 3 * count], held[3 * count :]
    wide = 256
    stores = []
    wait_all(loads[: 2 * count])
    for c in range(D // wide):
        total = None
        cols = slice(c * wide, c * wide + wide)
        for b in range(count):
            part = dot_tn(g_rows[b][...], dm_rows[b][:, cols])
            total = part if total is None else total + part
        down_s[:, cols] = total.astype(BF)
    stores += [
        mover.start(down_s.at[b], out.at[a]) for a, b in down_places(D, H, me, S, F)
    ]
    wait_all(loads[2 * count :])
    for c in range(H // wide):
        total = None
        cols = slice(c * wide, c * wide + wide)
        for b in range(count):
            part = dot_tn(b_rows[b][...], dz_rows[b][:, cols])
            total = part if total is None else total + part
        up_s[:, cols] = total.astype(BF)
        piece = pl.ds(c * wide, wide)
        target = piece
        if in_plane(S, F):
            target = pl.ds(pl.multiple_of((me ^ c) * wide, wide), wide)
        stores.append(mover.start(up_s.at[:, piece], out.at[:, target]))
    wait_all(stores)


def feed_outer(dims, b_rows, dz_rows, g_rows, dm_rows):
    S, F, D, W, H = dims
    count = len(b_rows)
    L = b_rows[0].shape[0]
    operands = (*g_rows, *dm_rows, *b_rows, *dz_rows)
    return call(
        partial(feed_outer_kernel, dims, count),
        operands,
        [any_spec()] * len(operands),
        [((D, 2 * H), BF)],
        [hbm_spec()],
        [pltpu.VMEM(x.shape, BF) for x in operands]
        + [
            pltpu.VMEM((H, D), BF),
            pltpu.VMEM((D, H), BF),
            pltpu.SemaphoreType.DMA((4 * count + F * (H // W) + H // 256,)),
        ],
        4 * count * L * D * H,
        2 * (count * 2 * L * (D + H) + 2 * D * H),
        "feed_outer",
    )[0]


def feed_last_kernel(S, F, *refs):
    came, got, (up_out, down_out, held, sems) = refs[:S], refs[S], refs[S + 1 :]
    me = seq_place()
    core = lax.rem(lax.axis_index("fsdp").astype(jnp.int32), 2)
    mover = Mover(sems)
    loads = [mover.start(a, held.at[j]) for j, a in enumerate(came)]
    R, W = up_out.shape[0], up_out.shape[1] // S
    wait_all(loads)
    for slot in range(S):
        start = pl.multiple_of((me ^ slot) * W, W)
        up_out[:, pl.ds(start, W)] = held[slot, 0:R, :].astype(F32)
    near = lax.rem(me, 2) == core
    for k in range(2):
        rows = slice(k * 2 * R, k * 2 * R + 2 * R)
        here = held[me ^ (2 * core + k), R : 3 * R, :]
        down_out[rows, :] = jnp.where(near, here, got[k]).astype(F32)


def feed_last(S, F, came, got):
    R, W = came[0].shape[0] // 3, came[0].shape[1]
    return call(
        partial(feed_last_kernel, S, F),
        (*came, got),
        [any_spec()] * S + [vmem_spec()],
        [((R, S * W), F32), ((4 * R, W), F32)],
        [vmem_spec()] * 2,
        [pltpu.VMEM((S, 3 * R, W), BF), pltpu.SemaphoreType.DMA((S,))],
        R * W * S,
        R * W * 40,
        "feed_last",
    )


def total_of(refs, rows):
    total = None
    for ref in refs:
        value = ref[0, rows, :].astype(F32)
        total = value if total is None else total + value
    return total


def column_sum(v):
    return jnp.sum(v, axis=0, keepdims=True)


def finish_kernel(turn, *refs):
    if turn:
        refs = refs[1:]
    count = (len(refs) - 6) // 2
    ins, (y_hbm, dm_hbm, stat_out), refs = refs[:count], refs[count : count + 3], refs[count + 3 :]
    held, (y_out, dm_out, sems) = refs[: len(ins)], refs[len(ins) :]
    mover = Mover(sems)
    wait_all([mover.start(a, b) for a, b in zip(ins, held)])
    gains, u_ref, h_ref, dy_ref, *terms = held
    half = dm_out.shape[0] // 2
    stats = [None] * 5
    for part in range(2):
        rows = slice(part * half, part * half + half)
        m = total_of(terms, rows)
        unit, scale = norm_parts(m)
        f = unit * gains[3:4, :]
        h = h_ref[rows, :]
        y = h + f
        y_out[rows, :] = y.astype(BF)
        dy = dy_ref[rows, :].astype(F32)
        dm = norm_back(dy * gains[3:4, :], unit, scale)
        dm_out[rows, :] = dm.astype(BF)
        if part == 1:
            stores = [mover.start(dm_out, dm_hbm), mover.start(y_out, y_hbm.at[turn])]
        second, unused = norm_parts(u_ref[rows, :])
        e = second * gains[1:2, :]
        values = [dy * unit, h * h, y * y, e * e, f * f]
        for index, value in enumerate(values):
            value = column_sum(value)
            stats[index] = value if part == 0 else stats[index] + value
    stat_out[...] = jnp.zeros_like(stat_out)
    for index in range(5):
        stat_out[3 + index : 4 + index, :] = stats[index]
    wait_all(stores)


def finish(turn, B, joined, gains, u, h, dy, terms):
    r, D = u.shape
    outs = [((B, r, D), BF), ((r, D), BF), ((8, D), F32)]
    operands = (gains, u, h, dy, *terms)
    first = [] if joined is None else [joined]
    return call(
        partial(finish_kernel, turn),
        (*first, *operands),
        [hbm_spec()] * len(first) + [any_spec()] * len(operands),
        outs,
        [hbm_spec(), hbm_spec(), vmem_spec()],
        [pltpu.VMEM(x.shape, x.dtype) for x in operands]
        + [pltpu.VMEM((r, D), BF)] * 2
        + [pltpu.SemaphoreType.DMA((len(operands) + 2,))],
        60 * r * D,
        r * D * 20,
        "finish",
        {0: 0} if first else {},
    )


def middle_kernel(*refs):
    count = (len(refs) - 6) // 2
    ins, (dh_out, du_hbm, stat_out), refs = refs[:count], refs[count : count + 3], refs[count + 3 :]
    held, (dh_s, du_out, sems) = refs[: len(ins)], refs[len(ins) :]
    mover = Mover(sems)
    wait_all([mover.start(a, b) for a, b in zip(ins, held)])
    gains, u_ref, h_ref, dy_ref, *terms = held
    r, D = u_ref.shape
    half = r // 2
    stats = [None] * 2
    for part in range(2):
        rows = slice(part * half, part * half + half)
        back = total_of(terms, rows)
        unit, scale = norm_parts(h_ref[rows, :])
        third = column_sum(back * unit)
        dh = dy_ref[rows, :].astype(F32) + norm_back(back * gains[2:3, :], unit, scale)
        dh_s[rows, :] = dh
        unit, scale = norm_parts(u_ref[rows, :])
        second = column_sum(dh * unit)
        du_out[rows, :] = norm_back(dh * gains[1:2, :], unit, scale).astype(BF)
        for index, value in enumerate((second, third)):
            stats[index] = value if part == 0 else stats[index] + value
    stores = [mover.start(du_out, du_hbm), mover.start(dh_s, dh_out)]
    stat_out[...] = jnp.zeros_like(stat_out)
    stat_out[1:2, :] = stats[0]
    stat_out[2:3, :] = stats[1]
    wait_all(stores)


def middle(gains, u, h, dy, terms):
    r, D = u.shape
    outs = [((r, D), F32), ((r, D), BF), ((8, D), F32)]
    operands = (gains, u, h, dy, *terms)
    return call(
        middle_kernel,
        operands,
        [any_spec()] * len(operands),
        outs,
        [hbm_spec(), hbm_spec(), vmem_spec()],
        [pltpu.VMEM(x.shape, x.dtype) for x in operands]
        + [
            pltpu.VMEM((r, D), F32),
            pltpu.VMEM((r, D), BF),
            pltpu.SemaphoreType.DMA((len(operands) + 2,)),
        ],
        60 * r * D,
        r * D * 24,
        "middle",
    )


def last_kernel(turn, *refs):
    if turn:
        refs = refs[1:]
    count = (len(refs) - 3) // 2
    ins, joined, held, (out, sems) = refs[:count], refs[count], refs[count + 1 : -2], refs[-2:]
    mover = Mover(sems)
    wait_all([mover.start(a, b) for a, b in zip(ins, held)])
    gains, x_ref, dh_ref, *terms = held
    r, D = x_ref.shape
    half = r // 2
    for part in range(2):
        rows = slice(part * half, part * half + half)
        back = total_of(terms, rows)
        unit, scale = norm_parts(x_ref[rows, :].astype(F32))
        grad = dh_ref[rows, :] + norm_back(back * gains[0:1, :], unit, scale)
        out[rows, :] = grad.astype(BF)
    mover.start(out, joined.at[turn]).wait()


def last(turn, B, joined, gains, x, dh, terms):
    r, D = x.shape
    operands = (gains, x, dh, *terms)
    first = [] if joined is None else [joined]
    return call(
        partial(last_kernel, turn),
        (*first, *operands),
        [hbm_spec()] * len(first) + [any_spec()] * len(operands),
        [((B, r, D), BF)],
        [hbm_spec()],
        [pltpu.VMEM(x.shape, x.dtype) for x in operands]
        + [pltpu.VMEM((r, D), BF), pltpu.SemaphoreType.DMA((len(operands) + 1,))],
        40 * r * D,
        r * D * 14,
        "last",
        {0: 0} if first else {},
    )[0]


def block_groups(F):
    return [[0, 2, 3, 4], [1, 5, 6, 7]] if F == 8 else [list(range(F))]


def out_grad_kernel(dims, count, *refs):
    S, F, D, W = dims
    groups = block_groups(F)
    ins, outs, refs = refs[: (1 + S) * count], refs[(1 + S) * count :], None
    outs, (*held, sum_s, sems) = outs[: len(groups)], outs[len(groups) :]
    mover = Mover(sems)
    o_rows, dus = held[:count], held[count:]
    loads = [mover.start(a, b) for a, b in zip(ins[:count], o_rows)]
    for b in range(count):
        pieces = ins[count + b * S : count + b * S + S]
        loads += load_rows(mover, pieces, dus[b], seq_place())
    R = D // F
    places = block_places(F)
    stores = []
    wait_all(loads)
    total = None
    for b in range(count):
        part = dot_tn(o_rows[b][...], dus[b][...])
        total = part if total is None else total + part
    sum_s[...] = total.astype(BF)
    for group, out in zip(groups, outs):
        for i, index in enumerate(group):
            row = pl.multiple_of(places[index] // S * R, R)
            col = pl.multiple_of(places[index] % S * W, W)
            stores.append(
                mover.start(
                    sum_s.at[pl.ds(row, R), pl.ds(col, W)], out.at[i, pl.ds(3 * R, R)]
                )
            )
    wait_all(stores)


def out_grad(dims, o_rows, dus):
    S, F, D, W = dims
    count = len(o_rows)
    L = o_rows[0].shape[0]
    groups = block_groups(F)
    operands = (*o_rows, *[piece for du in dus for piece in du])
    return call(
        partial(out_grad_kernel, dims, count),
        operands,
        [any_spec()] * len(operands),
        [((len(group), 4 * (D // F) + EXTRA, W), BF) for group in groups],
        [hbm_spec()] * len(groups),
        [pltpu.VMEM(x.shape, BF) for x in o_rows]
        + [pltpu.VMEM((L, D), BF)] * count
        + [pltpu.VMEM((W, D), BF), pltpu.SemaphoreType.DMA(((1 + S) * count + F,))],
        2 * count * L * D * W,
        2 * (count * L * (D + W) + D * W),
        "out_grad",
    )


def qkv_grad_kernel(dims, count, many, *refs):
    S, F, D, W = dims
    groups = block_groups(F)
    n = len(groups)
    stats, refs = refs[n : n + many], refs[n + many :]
    ins, refs = refs[: 2 * count], refs[2 * count :]
    outs, (*held, sum_s, stat_s, sems) = refs[:n], refs[n:]
    held_stats, held = held[:many], held[many:]
    mover = Mover(sems)
    early = [mover.start(a, b) for a, b in zip(stats, held_stats)]
    loads = [mover.start(a, b) for a, b in zip(ins, held)]
    a_rows, grads = held[:count], held[count:]
    R = D // F
    places = [pl.multiple_of(place * R, R) for place in block_places(F)]
    stores = []
    wait_all(early)
    if F == 8:
        total = held_stats[0][...]
        for other in held_stats[1:]:
            total = total + other[...]
        squares = total[4:8, 0:R]
        for i in range(1, F):
            squares = squares + total[4:8, i * R : i * R + R]
        joined = jnp.concatenate([total[0:4], jnp.concatenate([squares] * F, axis=1)], axis=0)
        stat_s[0:8, 0:D] = joined.astype(BF)
        stat_s[8:16, 0:D] = jnp.zeros_like(total).astype(BF)
        for group, out in zip(groups, outs):
            for i, index in enumerate(group):
                stores.append(
                    mover.start(
                        stat_s.at[:, pl.ds(places[index], R)],
                        out.at[i, pl.ds(4 * R, EXTRA), pl.ds(0, R)],
                    )
                )
    wait_all(loads)
    for t in range(3):
        cols = slice(t * W, t * W + W)
        total = None
        for b in range(count):
            part = dot_tn(a_rows[b][...], grads[b][:, cols])
            total = part if total is None else total + part
        sum_s[:, cols] = total.astype(BF)
        for group, out in zip(groups, outs):
            for i, index in enumerate(group):
                stores.append(
                    mover.start(
                        sum_s.at[pl.ds(places[index], R), pl.ds(t * W, W)],
                        out.at[i, pl.ds(t * R, R)],
                    )
                )
    wait_all(stores)


def qkv_grad(dims, parts, stats, a_rows, grads):
    S, F, D, W = dims
    count = len(a_rows)
    L = a_rows[0].shape[0]
    operands = (*parts, *stats, *a_rows, *grads)
    return pl.pallas_call(
        partial(qkv_grad_kernel, dims, count, len(stats)),
        out_shape=tuple(jax.ShapeDtypeStruct(part.shape, part.dtype) for part in parts),
        in_specs=[hbm_spec()] * len(parts) + [any_spec()] * (len(operands) - len(parts)),
        out_specs=tuple([hbm_spec()] * len(parts)),
        input_output_aliases={i: i for i in range(len(parts))},
        scratch_shapes=[pltpu.VMEM(x.shape, x.dtype) for x in (*stats, *a_rows, *grads)]
        + [
            pltpu.VMEM((D, 3 * W), BF),
            pltpu.VMEM((EXTRA, D), BF),
            pltpu.SemaphoreType.DMA((2 * count + len(stats) + 4 * F,)),
        ],
        compiler_params=pltpu.CompilerParams(vmem_limit_bytes=VMEM_LIMIT),
        name="qkv_grad",
    )(*operands)


def deal_qkv_kernel(F, *refs):
    stacks, (one, two, held, sems) = refs[:F], refs[F:]
    me = seq_place()
    rows, cols = one.shape[1], one.shape[2]
    mover = Mover(sems)
    outs = (one, two)
    loads = []
    for i in range(F):
        for slot in (1, 2):
            start = pl.multiple_of(block_at(me, slot) * cols, cols)
            source = stacks[i].at[0, pl.ds(0, rows), pl.ds(start, cols)]
            loads.append(mover.start(source, held.at[slot - 1, i]))
    wait_all(loads)
    wait_all([mover.start(held.at[j], outs[j]) for j in range(2)])


def deal_qkv(R, W, stacks):
    F = len(stacks)
    return call(
        partial(deal_qkv_kernel, F),
        tuple(stacks),
        [any_spec()] * F,
        [((F, R, W), BF)] * 2,
        [hbm_spec()] * 2,
        [pltpu.VMEM((2, F, R, W), BF), pltpu.SemaphoreType.DMA((2 * F + 2,))],
        0,
        8 * F * R * W,
        "deal_qkv",
    )


def pair_sum_kernel(mine, got, *refs):
    outs, (mine_s, got_s, sum_s, sems) = refs[:4], refs[4:]
    mover = Mover(sems)
    loads = []
    for i in range(4):
        loads.append((mover.start(mine.at[i], mine_s.at[i]), mover.start(got.at[i], got_s.at[i])))
    stores = []
    for i in (3, 2, 1, 0):
        wait_all(loads[i])
        sum_s[i] = (mine_s[i].astype(F32) + got_s[i].astype(F32)).astype(BF)
        stores.append(mover.start(sum_s.at[i], outs[i]))
    wait_all(stores)


def pair_sum(mine, got):
    shape = mine.shape[1:]
    return call(
        pair_sum_kernel,
        (mine, got),
        [any_spec()] * 2,
        [(shape, BF)] * 4,
        [hbm_spec()] * 4,
        [pltpu.VMEM(mine.shape, BF)] * 3 + [pltpu.SemaphoreType.DMA((12,))],
        mine.size,
        6 * mine.size,
        "pair_sum",
    )


def last_sum_kernel(S, R, *refs):
    ins, (*moved, out_tile, stat_out), refs = refs[:4], refs[4:9], refs[9:]
    held, (sum_s, sems) = refs[:4], refs[4:]
    mover = Mover(sems)
    wait_all([mover.start(a, b) for a, b in zip(ins, held)])
    total = held[0][...].astype(F32)
    for ref in held[1:]:
        total = total + ref[...].astype(F32)
    sum_s[...] = total.astype(BF)
    stat_out[...] = total[4 * R : 4 * R + 8, 0 : stat_out.shape[1]]
    me = seq_place()
    stores = [mover.start(sum_s.at[pl.ds(3 * R, R)], out_tile)]
    for j in range(3):
        owner = me ^ j
        start = pl.multiple_of(lax.div(3 * owner + block_at(owner, j), S) * R, R)
        stores.append(mover.start(sum_s.at[pl.ds(start, R)], moved[j].at[pl.ds(0, R)]))
        stores.append(
            mover.start(sum_s.at[pl.ds(4 * R, EXTRA)], moved[j].at[pl.ds(R, EXTRA)])
        )
    wait_all(stores)


def last_sum(S, R, terms):
    rows, W = terms[0].shape
    return call(
        partial(last_sum_kernel, S, R),
        tuple(terms),
        [any_spec()] * 4,
        [((R + EXTRA, W), BF)] * 3 + [((R, W), BF), ((8, R), F32)],
        [hbm_spec()] * 4 + [vmem_spec()],
        [pltpu.VMEM((rows, W), BF)] * 5 + [pltpu.SemaphoreType.DMA((11,))],
        4 * rows * W,
        10 * rows * W,
        "last_sum",
    )


def flip(bits, size):
    return [(i, i ^ bits) for i in range(size)]


def add_low(*terms):
    total = terms[0].astype(F32)
    for term in terms[1:]:
        total = total + term.astype(F32)
    return total.astype(BF)


def gather_slots(own, S, me, turn):
    if S != 4:
        full = lax.all_gather(own, "seq")
        return [
            lax.dynamic_index_in_dim(full, me ^ slot, 0, keepdims=False) for slot in range(S)
        ]
    far = lax.ppermute(own, "seq", flip(3, S))
    return [own] + [lax.ppermute(own, "seq", flip(j, S)) for j in (1, 2)] + [far]


def slot_order(S, turn):
    return [[slot] for slot in range(S)]


def slot_shapes(S, turn, shape):
    return [((len(group), *shape), BF) for group in slot_order(S, turn)]


def scatter_slots(groups, S, me, turn):
    if S != 4:
        order = jnp.take(jnp.concatenate(groups), me ^ jnp.arange(S), axis=0)
        return [lax.psum_scatter(order, "seq", scatter_dimension=0, tiled=True)]
    return [groups[0]] + [lax.ppermute(groups[j], "seq", flip(j, S)) for j in (3, 1, 2)]


def swap_slots(pieces, S):
    return [pieces[0]] + [lax.ppermute(pieces[j], "seq", flip(j, S)) for j in range(1, S)]


def sum_everywhere(v, S, F):
    if S != 4 or F != 8:
        return lax.psum(v, ("seq", "fsdp"))
    v = v + lax.ppermute(v, "fsdp", flip(1, F))
    v = v + lax.ppermute(v, "seq", flip(1, S))
    v = v + lax.ppermute(v, "seq", flip(2, S))
    v = v + lax.ppermute(v, "fsdp", flip(2, F))
    return v + lax.ppermute(v, "fsdp", flip(4, F))


def gather_blocks(block, F, early=()):
    if F != 8:
        return [lax.all_gather(block, "fsdp")]
    near = lax.ppermute(block, "fsdp", flip(1, F))
    far = [lax.ppermute(block, "fsdp", flip(j, F)) for j in (2, 4, 6)]
    far = after(far, near, *early)
    rest = [lax.ppermute(piece, "fsdp", flip(1, F)) for piece in far]
    return [piece[None] for piece in (block, near, *far, *rest)]


def after(value, *others):
    return lax.optimization_barrier((value, others))[0]


def blocks_in(blocks, S, me):
    moved = []
    for j in range(3):
        pairs = [(s, (3 * s + j) % S) for s in range(S)]
        moved.append(lax.ppermute(blocks[j], "seq", pairs))
    stack = jnp.stack(moved)
    return [
        lax.dynamic_index_in_dim(stack, (me + S * t) % 3, 0, keepdims=False) for t in range(3)
    ]


def blocks_out_pairs(S, j):
    return [((3 * s + j) % S, s) for s in range(S)]


def blocks_out(stack, S, me):
    moved = []
    for j in range(3):
        t = ((j - me) * (S % 3)) % 3
        piece = lax.dynamic_index_in_dim(stack, t, 0, keepdims=False)
        moved.append(lax.ppermute(piece, "seq", blocks_out_pairs(S, j)))
    return jnp.concatenate(moved, axis=1)


def turn_pairs(S, F):
    each = F // S
    return [
        (s * F + f, (f // each) * F + (f % each) * S + s) for s in range(S) for f in range(F)
    ]


def shards(tokens, cotangent, prefix, qkv_weight, out_weight, up_weight, down_weight, norm_gains):
    S, F = lax.axis_size("seq"), lax.axis_size("fsdp")
    B, r, D = tokens.shape
    heads = D // HEAD // S
    W = D // S
    R = D // F
    H = up_weight.shape[1]
    tiles = H // W
    me = seq_place()
    place = lax.axis_index("fsdp").astype(jnp.int32)
    pairs = turn_pairs(S, F)

    down_late, out_late = down_weight, out_weight
    axes = ("seq", "fsdp")
    if in_plane(S, F):
        core = place % 2
        other = lax.ppermute(down_late, "fsdp", flip(1, F))
        halves = jnp.concatenate([down_late, other]).reshape(4, 2 * R, W)
        sent = []
        for j in range(S):
            target = me ^ j
            index = jnp.where(target // 2 == core, 0, 2) + target % 2
            piece = lax.dynamic_index_in_dim(halves, index, 0, keepdims=False)
            up_tile = lax.dynamic_slice_in_dim(up_weight, target * W, W, 1)
            sent.append(jnp.concatenate([up_tile, piece, out_late]))
        came = swap_slots(sent, S)
        ups = [message[:R] for message in came]
        out_tiles = [message[3 * R :] for message in came]
        near = (me % 2) ^ core == 0
        pieces = [
            jnp.where(near, came[2 * i][R : 3 * R], came[2 * i + 1][R : 3 * R])
            for i in range(2)
        ]
        downs = [piece[t * R : t * R + R] for piece in pieces for t in range(2)]
    else:
        ups = [up_weight]
        down_mine = lax.ppermute(down_late, axes, pairs)
        downs = [down_mine[i * R : i * R + R] for i in range(tiles)]
        out_tiles = gather_slots(out_late, S, me, 0)
    ff_mine = jnp.concatenate([*ups, *downs, *out_tiles], axis=1)
    if in_plane(S, F):
        gain_rows = jnp.pad(norm_gains, ((0, EXTRA - 4), (0, 3 * W - R)))
        first_block = jnp.concatenate([qkv_weight, gain_rows])
        stacks = gather_blocks(first_block, F, (ff_mine,))
        one, two = deal_qkv(R, W, stacks)
        one = lax.ppermute(one, "seq", flip(1, S))
        two = lax.ppermute(two, "seq", flip(2, S))
        all_x = [gather_slots(tokens[:1], S, me, 0)]
        all_x += [gather_slots(after(tokens[b : b + 1], one, two), S, me, 0) for b in range(1, B)]
        stacks = [*stacks, one, two]
    else:
        blocks = [qkv_weight[:, j * W : j * W + W] for j in range(3)]
        all_x = [gather_slots(tokens[b : b + 1], S, me, 0) for b in range(B)]
        stacks = gather_blocks(jnp.concatenate(blocks_in(blocks, S, me)), F)
    if in_plane(S, F):
        ff_mine = after(ff_mine, stacks[2:5])
    ff_full = lax.all_gather(ff_mine, "fsdp", axis=0, tiled=True)
    gains = None
    if F != 8:
        gains = lax.all_gather(norm_gains, "fsdp", axis=1, tiled=True).astype(F32)
        gains = jnp.pad(gains, ((0, 4), (0, 0)))
    att_dims = (S, F, r, D, heads)
    ff_dims = (S, F, r, D, W, H)
    a_all, qkv_all, p_all, os, os_own = [], [], [], [], []
    for b in range(B):
        a, qkv, o, p, gains_full = attend(att_dims, b, prefix, gains, stacks, all_x[b])
        a_all.append(a)
        qkv_all.append(qkv)
        p_all.append(p)
        os_own.append(o)
        os.append(gather_slots(o, S, me, b))
    gains = gains_full
    b_all, u_own, h_own, g_all, gp_all, m_terms = [], [], [], [], [], []
    for b in range(B):
        res = feed(ff_dims, b, gains, ff_full, all_x[b], os[b])
        b_all.append(res[0])
        u_own.append(res[1])
        h_own.append(res[2])
        g_all.append(res[3])
        gp_all.append(res[4])
        m_terms.append(scatter_slots(list(res[5:]), S, me, b))
    y, stats, dms = None, [], []
    for b in range(B):
        y, dm, stat = finish(b, B, y, gains, u_own[b], h_own[b], cotangent[b], m_terms[b])
        stats.append(stat)
        dms.append(gather_slots(dm, S, me, b))
    dm_all, dz_all, h_terms = [], [], []
    for b in range(B):
        res = feed_back(ff_dims, b, ff_full, gp_all[b], dms[b])
        dm_all.append(res[0])
        dz_all.append(res[1])
        h_terms.append(scatter_slots(list(res[2:]), S, me, b))
    dhs, dus = [], []
    for b in range(B):
        dh, du, stat = middle(gains, u_own[b], h_own[b], cotangent[b], h_terms[b])
        dhs.append(dh)
        dus.append(gather_slots(du, S, me, b))
        stats.append(stat)
    dm_all = after(dm_all, h_terms[0])
    ff_part = feed_outer((S, F, D, W, H), b_all, dz_all, g_all, dm_all)
    ff_sum = lax.psum_scatter(ff_part, "fsdp", scatter_dimension=0, tiled=True)
    back_pairs = [(b, a) for a, b in pairs]
    if not in_plane(S, F):
        down_sum = jnp.concatenate(
            [ff_sum[:, H + i * W : H + i * W + W] for i in range(tiles)], axis=0
        )
        down_grad = lax.ppermute(down_sum, axes, back_pairs).astype(F32)
        up_grad = ff_sum[:, :H].astype(F32)
    dqkvs, x_terms = [], []
    for b in range(B):
        res = attend_back(
            att_dims, b, gains, ff_full, stacks, a_all[b], qkv_all[b], p_all[b], dus[b]
        )
        dqkvs.append(res[0])
        stats.append(res[1])
        x_terms.append(scatter_slots(list(res[2:]), S, me, b))
    grad_dims = (S, F, D, W)
    parts = after(out_grad(grad_dims, os_own, dus), dqkvs)
    parts = after(parts, x_terms[0])
    parts = qkv_grad(grad_dims, parts, stats, a_all, dqkvs)
    if F == 8 and S == 4:
        kept = pair_sum(parts[0], lax.ppermute(parts[1], "fsdp", flip(1, F)))
        ff_sum = after(ff_sum, kept)
        got = [lax.ppermute(kept[j], "fsdp", flip(2 * j, F)) for j in (3, 2, 1)]
        pieces = [ff_sum[:, H + i * W : H + i * W + W] for i in range(4)]
        sent = [
            jnp.concatenate([ff_sum[:, j * W : j * W + W], *pieces[j // 2 * 2 : j // 2 * 2 + 2]])
            for j in range(S)
        ]
        came = swap_slots(sent, S)
        got = after(got, came)
        whole = jnp.stack(came)[:, R:]
        away = jnp.stack(
            [
                lax.dynamic_index_in_dim(whole, me ^ (2 * (1 - place % 2) + k), 0, keepdims=False)
                for k in range(2)
            ]
        )
        up_grad, down_grad = feed_last(S, F, came, lax.ppermute(away, "fsdp", flip(1, F)))
        *moved, out_tile, stat = last_sum(S, R, [kept[0], *got])
        moved[1:] = [lax.ppermute(moved[j], "seq", flip(j, S)) for j in (1, 2)]
        missed = lax.ppermute(stat, "seq", flip(3, S))
        for piece in moved:
            missed = missed + piece[R : R + 8, :R].astype(F32)
        odd = me % 2 == 1
        ends = (moved[0][:R], moved[2][:R])
        qkv_own = jnp.concatenate(
            [jnp.where(odd, ends[1], ends[0]), moved[1][:R], jnp.where(odd, ends[0], ends[1])],
            axis=1,
        )
        gains_grad, squares = missed[:4], jnp.sum(missed[4:], axis=1)
    else:
        rest = lax.psum_scatter(parts[0], "fsdp", scatter_dimension=0, tiled=False)
        qkv_own = blocks_out(jnp.stack([rest[t * R : t * R + R] for t in range(3)]), S, me)
        out_tile = rest[3 * R : 4 * R]
        totals = lax.psum(sum(stats), ("seq", "fsdp"))
        gains_grad = lax.dynamic_slice_in_dim(totals[:4], place * R, R, 1)
        squares = jnp.sum(totals[4:], axis=1)
    input_grad = None
    for b in range(B):
        input_grad = last(b, B, input_grad, gains, tokens[b], dhs[b], x_terms[b])

    out_own = lax.ppermute(out_tile, ("seq", "fsdp"), back_pairs)
    entries = B * r * D * S * F
    stream_rms = jnp.sqrt(squares / entries)
    return (
        y,
        input_grad,
        qkv_own.astype(F32),
        out_own.astype(F32),
        up_grad,
        down_grad,
        gains_grad,
        stream_rms,
    )


def solution(mesh):
    in_specs = (
        P("fsdp", "seq", None),
        P("fsdp", "seq", None),
        P("fsdp"),
        P("fsdp", "seq"),
        P("fsdp", "seq"),
        P("fsdp", "seq"),
        P("fsdp", "seq"),
        P(None, "fsdp"),
    )
    out_specs = (
        P("fsdp", "seq", None),
        P("fsdp", "seq", None),
        P("fsdp", "seq"),
        P("fsdp", "seq"),
        P("fsdp", "seq"),
        P("fsdp", "seq"),
        P(None, "fsdp"),
        P(),
    )
    return jax.shard_map(shards, mesh=mesh, in_specs=in_specs, out_specs=out_specs, check_vma=False)
```

```python
import math
from functools import partial

import jax
import jax.numpy as jnp
from jax import lax
from jax.experimental import pallas as pl
from jax.experimental.pallas import tpu as pltpu
from jax.sharding import PartitionSpec as P

HEAD = 64
NORM_EPSILON = 1e-05
MASKED_SCORE = -1e30
VMEM_LIMIT = 48 * 1024 * 1024
BF = jnp.bfloat16
F32 = jnp.float32
BLOCK_ORDER = (0, 1, 2, 4, 6, 3, 5, 7)
EXTRA = 16
COST = 0.001


def dot_nn(a, b):
    return lax.dot_general(a, b, (((1,), (0,)), ((), ())), preferred_element_type=F32)


def dot_nt(a, b):
    return lax.dot_general(a, b, (((1,), (1,)), ((), ())), preferred_element_type=F32)


def dot_tn(a, b):
    return lax.dot_general(a, b, (((0,), (0,)), ((), ())), preferred_element_type=F32)


def norm_parts(v):
    centre = jnp.mean(v, axis=-1, keepdims=True)
    shifted = v - centre
    spread = jnp.mean(shifted * shifted, axis=-1, keepdims=True)
    scale = lax.rsqrt(spread + NORM_EPSILON)
    return shifted * scale, scale


def norm_back(grad_unit, unit, scale):
    first = jnp.mean(grad_unit, axis=-1, keepdims=True)
    second = jnp.mean(grad_unit * unit, axis=-1, keepdims=True)
    return scale * (grad_unit - first - unit * second)


def seq_place():
    return lax.axis_index("seq").astype(jnp.int32)


def block_places(F):
    if F != 8:
        return [jnp.int32(i) for i in range(F)]
    place = lax.axis_index("fsdp").astype(jnp.int32)
    return [place ^ i for i in BLOCK_ORDER]


class Mover:
    def __init__(self, sems):
        self.sems = sems
        self.used = 0

    def start(self, src, dst):
        copy = pltpu.make_async_copy(src, dst, self.sems.at[self.used])
        self.used += 1
        copy.start()
        return copy


def wait_all(copies):
    for copy in copies:
        copy.wait()


def load_rows(mover, pieces, target, me):
    r = pieces[0].shape[0]
    copies = []
    for slot, piece in enumerate(pieces):
        start = pl.multiple_of((me ^ slot) * r, r)
        copies.append(mover.start(piece, target.at[pl.ds(start, r)]))
    return copies


def store_rows(mover, source, outs, order, me):
    r = outs[0].shape[1]
    copies = []
    for group, out in zip(order, outs):
        for i, slot in enumerate(group):
            start = pl.multiple_of((me ^ slot) * r, r)
            copies.append(mover.start(source.at[pl.ds(start, r)], out.at[i]))
    return copies


def in_plane(S, F):
    return S == 4 and F == 8


def block_at(s, slot):
    if slot == 1:
        return jnp.int32(1)
    odd = lax.rem(s, 2)
    return 2 * odd if slot == 0 else 2 - 2 * odd


def load_qkv(mover, weights, target, me, S, F):
    places, copies = block_places(F), []
    rows, cols = target.shape[0] // F, target.shape[1] // 3
    if in_plane(S, F):
        stacks, moved = weights[:F], weights[F:]
        for slot in range(3):
            sender = me ^ slot
            at = block_at(sender, slot)
            part = lax.div(3 * sender + at, S)
            col = pl.ds(pl.multiple_of(part * cols, cols), cols)
            from_col = pl.ds(pl.multiple_of(at * cols, cols), cols)
            for i in range(F):
                row = pl.ds(pl.multiple_of(places[i] * rows, rows), rows)
                if slot == 0:
                    source = stacks[i].at[0, pl.ds(0, rows), from_col]
                else:
                    source = moved[slot - 1].at[i]
                copies.append(mover.start(source, target.at[row, col]))
        return copies
    stack = weights[0]
    for i in range(F):
        row = pl.ds(pl.multiple_of(places[i] * rows, rows), rows)
        for t in range(3):
            copies.append(
                mover.start(
                    stack.at[i, pl.ds(t * rows, rows)], target.at[row, pl.ds(t * cols, cols)]
                )
            )
    return copies


def load_gains(mover, stacks, target, F):
    places, copies = block_places(F), []
    width = target.shape[1] // F
    for i, stack in enumerate(stacks[:F]):
        start = pl.multiple_of(places[i] * width, width)
        last = stack.shape[1] - EXTRA
        copies.append(
            mover.start(
                stack.at[0, pl.ds(last, EXTRA), pl.ds(0, width)],
                target.at[:, pl.ds(start, width)],
            )
        )
    return copies


def any_spec():
    return pl.BlockSpec(memory_space=pl.ANY)


def hbm_spec():
    return pl.BlockSpec(memory_space=pltpu.HBM)


def smem_spec():
    return pl.BlockSpec(memory_space=pltpu.SMEM)


def vmem_spec():
    return pl.BlockSpec(memory_space=pltpu.VMEM)


def call(body, operands, in_specs, outs, out_specs, scratch, flops, bytes_accessed, name, aliases={}):
    return pl.pallas_call(
        body,
        out_shape=tuple(jax.ShapeDtypeStruct(shape, dtype) for shape, dtype in outs),
        in_specs=in_specs,
        out_specs=tuple(out_specs),
        scratch_shapes=scratch,
        input_output_aliases=aliases,
        compiler_params=pltpu.CompilerParams(vmem_limit_bytes=VMEM_LIMIT),
        cost_estimate=pl.CostEstimate(
            flops=int(flops * COST), bytes_accessed=int(bytes_accessed * COST), transcendentals=0
        ),
        name=name,
    )(*operands)


def attend_kernel(dims, count, turn, packed, prefix, *refs):
    S, F, r, D, heads = dims
    L, W = S * r, heads * HEAD
    if packed:
        gains_in = None
    else:
        gains_in, refs = refs[0], refs[1:]
    weights, pieces, refs = refs[:count], refs[count : count + S], refs[count + S :]
    a_out, qkv_out, o_out, p_out, gains_out, refs = *refs[:5], refs[5:]
    x_s, w_s, a_s, qkv_s, o_s, p_s, bias_s, raw_s, sems = refs
    me, limit_len = seq_place(), prefix[turn]
    mover = Mover(sems)
    gain_loads = load_gains(mover, weights, raw_s, F) if packed else []
    loads = load_rows(mover, [piece.at[0] for piece in pieces], x_s, me)
    weight_loads = load_qkv(mover, weights, w_s, me, S, F)
    tile = 128
    limit = L // 2
    for i in range(L // tile):
        shape = (tile, max((i + 1) * tile, limit))
        rows = i * tile + lax.broadcasted_iota(jnp.int32, shape, 0)
        cols = lax.broadcasted_iota(jnp.int32, shape, 1)
        seen = (cols <= rows) | (cols < limit_len)
        bias_s[i * tile : i * tile + tile, : shape[1]] = jnp.where(seen, 0.0, MASKED_SCORE)
    wait_all(gain_loads)
    gains_out[...] = raw_s[0:8, :].astype(F32) if packed else gains_in[...]
    wait_all(loads)
    for i in range(L // tile):
        rows = slice(i * tile, i * tile + tile)
        unit, scale = norm_parts(x_s[rows, :].astype(F32))
        a_s[rows, :] = (unit * gains_out[0:1, :]).astype(BF)
    stores = [mover.start(a_s, a_out)]
    wait_all(weight_loads)
    for c in range(3):
        cols = slice(c * W, c * W + W)
        qkv_s[:, cols] = dot_nn(a_s[...], w_s[:, cols]).astype(BF)
    stores.append(mover.start(qkv_s, qkv_out))
    lane = lax.broadcasted_iota(jnp.int32, (1, 128), 1)
    for pair in range(heads // 2):
        q2 = qkv_s[:, pair * 128 : pair * 128 + 128] * BF(HEAD**-0.5)
        k2 = qkv_s[:, W + pair * 128 : W + pair * 128 + 128]
        v2 = qkv_s[:, 2 * W + pair * 128 : 2 * W + pair * 128 + 128]
        keys, values = [], []
        for side in range(2):
            mine = (lane >= 64) if side else (lane < 64)
            keys.append(jnp.where(mine, k2, BF(0)))
            values.append(jnp.where(mine, v2, BF(0)))
        for i in range(L // tile):
            rows = slice(i * tile, i * tile + tile)
            span = max((i + 1) * tile, limit)
            total = None
            for side in range(2):
                scores = dot_nt(q2[rows], keys[side][:span]) + bias_s[rows, :span]
                top = jnp.max(scores, axis=-1, keepdims=True)
                weights_here = jnp.exp(scores - top)
                share = 1.0 / jnp.sum(weights_here, axis=-1, keepdims=True)
                probs = (weights_here * share).astype(BF)
                p_s[2 * pair + side, rows, :span] = probs
                part = dot_nn(probs, values[side][:span])
                total = part if total is None else total + part
            o_s[rows, pair * 128 : pair * 128 + 128] = total.astype(BF)
        for side in range(2):
            stores.append(mover.start(p_s.at[2 * pair + side], p_out.at[2 * pair + side]))
    stores.append(mover.start(o_s, o_out))
    wait_all(stores)


def attend(dims, turn, prefix, gains, weights, pieces):
    S, F, r, D, heads = dims
    L, W = S * r, heads * HEAD
    outs = [((L, D), BF), ((L, 3 * W), BF), ((L, W), BF), ((heads, L, L), BF), ((8, D), F32)]
    scratch = [
        pltpu.VMEM((L, D), BF),
        pltpu.VMEM((D, 3 * W), BF),
        pltpu.VMEM((L, D), BF),
        pltpu.VMEM((L, 3 * W), BF),
        pltpu.VMEM((L, W), BF),
        pltpu.VMEM((heads, L, L), BF),
        pltpu.VMEM((L, L), F32),
        pltpu.VMEM((EXTRA, D), BF),
        pltpu.SemaphoreType.DMA((S + 4 * F + heads + 3,)),
    ]
    flops = 2 * L * D * 3 * W + 4 * heads * L * L * HEAD * 4
    size = 2 * (2 * L * D + 3 * D * W + 4 * L * W + heads * L * L)
    packed = gains is None
    extra = [] if packed else [gains]
    return call(
        partial(attend_kernel, dims, len(weights), turn, packed),
        (prefix, *extra, *weights, *pieces),
        [smem_spec()]
        + [vmem_spec()] * len(extra)
        + [any_spec()] * (len(weights) + len(pieces)),
        outs,
        [hbm_spec()] * 4 + [vmem_spec()],
        scratch,
        flops,
        size,
        "attend",
    )


def attend_back_kernel(dims, count, order, gains_in, out_w, *refs):
    S, F, r, D, heads = dims
    n = len(order)
    L, W = S * r, heads * HEAD
    weights, refs = refs[:count], refs[count:]
    a_in, qkv, probs_in, pieces, refs = *refs[:3], refs[3 : 3 + S], refs[3 + S :]
    grad_out, stat_out, slots, refs = *refs[:2], refs[2 : 2 + n], refs[2 + n :]
    w_s, qkv_s, p_s, du_s, do_s, d_s, grad_s, part_s, a_s, out_s, gains, sems = refs
    me = seq_place()
    mover = Mover(sems)
    own = pl.ds(pl.multiple_of(me * W, W), W)
    loads = load_out(mover, out_w, out_s, own, me, S) + load_rows(mover, pieces, du_s, me)
    loads.append(mover.start(qkv, qkv_s))
    prob_loads = [mover.start(probs_in.at[h], p_s.at[h]) for h in range(heads)]
    late_loads = load_qkv(mover, weights, w_s, me, S, F)
    late_loads.append(mover.start(a_in, a_s))
    late_loads.append(mover.start(gains_in, gains))
    tile = 128
    limit = L // 2
    wait_all(loads)
    do_s[...] = dot_nt(du_s[...], out_s[...]).astype(BF)
    lane = lax.broadcasted_iota(jnp.int32, (1, 128), 1)
    for pair in range(heads // 2):
        cols = slice(pair * 128, pair * 128 + 128)
        q2 = qkv_s[:, cols] * BF(HEAD**-0.5)
        k2 = qkv_s[:, W + pair * 128 : W + pair * 128 + 128] * BF(HEAD**-0.5)
        v2 = qkv_s[:, 2 * W + pair * 128 : 2 * W + pair * 128 + 128]
        do2 = do_s[:, cols]
        queries, keys, values, grads = [], [], [], []
        for side in range(2):
            mine = (lane >= 64) if side else (lane < 64)
            queries.append(jnp.where(mine, q2, BF(0)))
            keys.append(jnp.where(mine, k2, BF(0)))
            values.append(jnp.where(mine, v2, BF(0)))
            grads.append(jnp.where(mine, do2, BF(0)))
            prob_loads[2 * pair + side].wait()
        for i in range(L // tile):
            rows = slice(i * tile, i * tile + tile)
            span = max((i + 1) * tile, limit)
            total = None
            for side in range(2):
                probs = p_s[2 * pair + side, rows, :span].astype(F32)
                grad_probs = dot_nt(do2[rows], values[side][:span])
                delta = jnp.sum(probs * grad_probs, axis=-1, keepdims=True)
                grad_scores = (probs * (grad_probs - delta)).astype(BF)
                d_s[side, rows, :span] = grad_scores
                part = dot_nn(grad_scores, keys[side][:span])
                total = part if total is None else total + part
            grad_s[rows, cols] = total.astype(BF)
        for j in range(L // tile):
            columns = slice(j * tile, j * tile + tile)
            low = 0 if (j * tile) < limit else j * tile
            total_k, total_v = None, None
            for side in range(2):
                part = dot_tn(d_s[side, low:, columns], queries[side][low:])
                total_k = part if total_k is None else total_k + part
                part = dot_tn(p_s[2 * pair + side, low:, columns], grads[side][low:])
                total_v = part if total_v is None else total_v + part
            grad_s[columns, W + pair * 128 : W + pair * 128 + 128] = total_k.astype(BF)
            grad_s[columns, 2 * W + pair * 128 : 2 * W + pair * 128 + 128] = total_v.astype(BF)
    stores = [mover.start(grad_s, grad_out)]
    wait_all(late_loads)
    wide = 256
    stat_out[...] = jnp.zeros_like(stat_out)

    for c in range(D // wide):
        cols = slice(c * wide, c * wide + wide)
        part = dot_nt(grad_s[...], w_s[cols, :])
        part_s[:, cols] = part.astype(BF)
        stat_out[0:1, cols] = column_sum(part * a_s[:, cols].astype(F32)) / gains[0:1, cols]
    stores += store_rows(mover, part_s, slots, order, me)
    wait_all(stores)


def attend_back(dims, turn, gains, out_w, weights, a, qkv, probs, pieces):
    S, F, r, D, heads = dims
    L, W = S * r, heads * HEAD
    outs = [((L, 3 * W), BF), ((8, D), F32)] + slot_shapes(S, turn, (r, D))
    blocks = 3 * F
    scratch = [
        pltpu.VMEM((D, 3 * W), BF),
        pltpu.VMEM((L, 3 * W), BF),
        pltpu.VMEM((heads, L, L), BF),
        pltpu.VMEM((L, D), BF),
        pltpu.VMEM((L, W), BF),
        pltpu.VMEM((2, L, L), BF),
        pltpu.VMEM((L, 3 * W), BF),
        pltpu.VMEM((L, D), BF),
        pltpu.VMEM((L, D), BF),
        pltpu.VMEM((W, D), BF),
        pltpu.VMEM((8, D), F32),
        pltpu.SemaphoreType.DMA((3 * S + heads + 5 + blocks,)),
    ]
    flops = 2 * L * D * 4 * W + 8 * heads * L * L * HEAD * 4
    size = 2 * (2 * L * D + 3 * D * W + 7 * L * W + heads * L * L)
    return call(
        partial(attend_back_kernel, dims, len(weights), slot_order(S, turn)),
        (gains, out_w, *weights, a, qkv, probs, *pieces),
        [any_spec()] * 2
        + [any_spec()] * (3 + len(weights) + len(pieces)),
        outs,
        [hbm_spec(), vmem_spec()] + [hbm_spec()] * (len(outs) - 2),
        scratch,
        flops,
        size,
        "attend_back",
    )


def load_out(mover, ff_w, target, rows, me, S):
    D = target.shape[1]
    W, base = D // S, ff_w.shape[1] - D
    copies = []
    for slot in range(S):
        start = pl.multiple_of((me ^ slot) * W, W)
        copies.append(
            mover.start(
                ff_w.at[rows, pl.ds(base + slot * W, W)], target.at[:, pl.ds(start, W)]
            )
        )
    return copies


def load_up(mover, ff_w, up_s, me, S, F):
    H = up_s.shape[1]
    if not in_plane(S, F):
        return [mover.start(ff_w.at[:, pl.ds(0, H)], up_s)]
    W, copies = H // S, []
    for slot in range(S):
        start = pl.multiple_of((me ^ slot) * W, W)
        copies.append(
            mover.start(ff_w.at[:, pl.ds(slot * W, W)], up_s.at[:, pl.ds(start, W)])
        )
    return copies


def down_places(D, H, me, S, F):
    W, R = D // S, D // F
    if in_plane(S, F):
        for f in range(F):
            for col in range(2):
                part = col ^ lax.div(me, 2)
                for t in range(2):
                    start = pl.multiple_of(H + (2 * part + t) * W, W)
                    yield (
                        (pl.ds(f * R, R), pl.ds(start, W)),
                        (pl.ds(f // 2 * 2 * R + t * R, R), pl.ds((f % 2 + 2 * col) * W, W)),
                    )
        return
    for f in range(F):
        for i in range(H // W):
            yield (
                (pl.ds(f * R, R), pl.ds(H + i * W, W)),
                (pl.ds(f // S * (R * (H // W)) + i * R, R), pl.ds(f % S * W, W)),
            )


def load_down(mover, ff_w, down_s, me, S, F):
    H, D = down_s.shape
    return [mover.start(ff_w.at[a], down_s.at[b]) for a, b in down_places(D, H, me, S, F)]


def feed_kernel(dims, order, turn, gains_in, ff_w, *refs):
    S, F, r, D, W, H = dims
    L, n = S * r, len(order)
    xs, os, refs = refs[:S], refs[S : 2 * S], refs[2 * S :]
    b_out, u_own, h_own, g_out, gp_out, slots, refs = *refs[:5], refs[5 : 5 + n], refs[5 + n :]
    x_s, o_s, out_s, u_s, h_s, up_s, down_s, b_s, g_s, gp_s, m_s, gains, sems = refs
    me = seq_place()
    mover = Mover(sems)
    loads = [mover.start(gains_in, gains)]
    for slot in range(S):
        start = pl.multiple_of((me ^ slot) * W, W)
        loads.append(mover.start(os[slot], o_s.at[:, pl.ds(start, W)]))
    loads += load_out(mover, ff_w, out_s, pl.ds(0, D), me, S)
    loads += load_rows(mover, [x.at[0] for x in xs], x_s, me)
    up_loads = load_up(mover, ff_w, up_s, me, S, F)
    down_loads = load_down(mover, ff_w, down_s, me, S, F)
    wide, tall = 256, 256
    wait_all(loads)
    for i in range(L // tall):
        rows = slice(i * tall, i * tall + tall)
        for c in range(D // wide):
            cols = slice(c * wide, c * wide + wide)
            u_s[rows, cols] = dot_nn(o_s[rows, :], out_s[:, cols])
        unit, scale = norm_parts(u_s[rows, :])
        h = x_s[rows, :].astype(F32) + unit * gains[1:2, :]
        h_s[rows, :] = h
        unit, scale = norm_parts(h)
        b_s[rows, :] = (unit * gains[2:3, :]).astype(BF)
    own = pl.ds(pl.multiple_of(me * r, r), r)
    stores = [
        mover.start(b_s, b_out),
        mover.start(u_s.at[own], u_own),
        mover.start(h_s.at[own], h_own),
    ]
    wait_all(up_loads)
    root = math.sqrt(2.0 / math.pi)
    for c in range(H // wide):
        cols = slice(c * wide, c * wide + wide)
        z = dot_nn(b_s[...], up_s[:, cols])
        square = z * z
        bent = jnp.tanh(z * (root + root * 0.044715 * square))
        side = 0.5 + 0.5 * bent
        g_s[:, cols] = (z * side).astype(BF)
        slope = z * (root + 3.0 * root * 0.044715 * square)
        gp_s[:, cols] = (side + (0.5 * slope) * (1.0 - bent * bent)).astype(BF)
    stores += [mover.start(g_s, g_out), mover.start(gp_s, gp_out)]
    wait_all(down_loads)
    for c in range(D // wide):
        cols = slice(c * wide, c * wide + wide)
        m_s[:, cols] = dot_nn(g_s[...], down_s[:, cols]).astype(BF)
    stores += store_rows(mover, m_s, slots, order, me)
    wait_all(stores)


def feed(dims, turn, gains, ff_w, xs, os):
    S, F, r, D, W, H = dims
    L = S * r
    outs = [((L, D), BF), ((r, D), F32), ((r, D), F32), ((L, H), BF), ((L, H), BF)]
    outs += slot_shapes(S, turn, (r, D))
    scratch = [
        pltpu.VMEM((L, D), BF),
        pltpu.VMEM((L, D), BF),
        pltpu.VMEM((D, D), BF),
        pltpu.VMEM((L, D), F32),
        pltpu.VMEM((L, D), F32),
        pltpu.VMEM((D, H), BF),
        pltpu.VMEM((H, D), BF),
        pltpu.VMEM((L, D), BF),
        pltpu.VMEM((L, H), BF),
        pltpu.VMEM((L, H), BF),
        pltpu.VMEM((L, D), BF),
        pltpu.VMEM((8, D), F32),
        pltpu.SemaphoreType.DMA((5 * S + F * (H // W) + 7,)),
    ]
    return call(
        partial(feed_kernel, dims, slot_order(S, turn), turn),
        (gains, ff_w, *xs, *os),
        [any_spec()] * (2 + 2 * S),
        outs,
        [hbm_spec()] * len(outs),
        scratch,
        2 * L * D * D + 4 * L * D * H,
        2 * (D * D + 2 * D * H + 5 * L * D + 2 * L * H),
        "feed",
    )


def feed_back_kernel(dims, order, ff_w, gp, *refs):
    S, F, r, D, W, H = dims
    pieces, dm_out, dz_out, refs = refs[:S], *refs[S : S + 2], refs[S + 2 :]
    slots, refs = refs[: len(order)], refs[len(order) :]
    up_s, down_s, gp_s, dm_s, dz_s, part_s, sems = refs
    me = seq_place()
    mover = Mover(sems)
    loads = load_rows(mover, pieces, dm_s, me)
    down_loads = load_down(mover, ff_w, down_s, me, S, F)
    down_loads.append(mover.start(gp, gp_s))
    up_loads = load_up(mover, ff_w, up_s, me, S, F)
    wide = 256
    wait_all(loads)
    stores = [mover.start(dm_s, dm_out)]
    wait_all(down_loads)

    for c in range(H // wide):
        cols = slice(c * wide, c * wide + wide)
        grad = dot_nt(dm_s[...], down_s[cols, :])
        dz_s[:, cols] = (grad * gp_s[:, cols].astype(F32)).astype(BF)
    stores.append(mover.start(dz_s, dz_out))
    wait_all(up_loads)

    for c in range(D // wide):
        cols = slice(c * wide, c * wide + wide)
        part_s[:, cols] = dot_nt(dz_s[...], up_s[cols, :]).astype(BF)
    stores += store_rows(mover, part_s, slots, order, me)
    wait_all(stores)


def feed_back(dims, turn, ff_w, gp, pieces):
    S, F, r, D, W, H = dims
    L = S * r
    outs = [((L, D), BF), ((L, H), BF)] + slot_shapes(S, turn, (r, D))
    scratch = [
        pltpu.VMEM((D, H), BF),
        pltpu.VMEM((H, D), BF),
        pltpu.VMEM((L, H), BF),
        pltpu.VMEM((L, D), BF),
        pltpu.VMEM((L, H), BF),
        pltpu.VMEM((L, D), BF),
        pltpu.SemaphoreType.DMA((3 * S + F * (H // W) + 4,)),
    ]
    return call(
        partial(feed_back_kernel, dims, slot_order(S, turn)),
        (ff_w, gp, *pieces),
        [any_spec()] * (2 + S),
        outs,
        [hbm_spec()] * len(outs),
        scratch,
        4 * L * D * H,
        2 * (2 * D * H + 3 * L * D + 2 * L * H),
        "feed_back",
    )


def feed_outer_kernel(dims, count, *refs):
    S, F, D, W, H = dims
    ins, (out, *held, down_s, up_s, sems) = refs[: 4 * count], refs[4 * count :]
    me = seq_place()
    mover = Mover(sems)
    loads = [mover.start(a, b) for a, b in zip(ins, held)]
    g_rows, dm_rows = held[:count], held[count : 2 * count]
    b_rows, dz_rows = held[2 * count : 3 * count], held[3 * count :]
    wide = 256
    stores = []
    wait_all(loads[: 2 * count])
    for c in range(D // wide):
        total = None
        cols = slice(c * wide, c * wide + wide)
        for b in range(count):
            part = dot_tn(g_rows[b][...], dm_rows[b][:, cols])
            total = part if total is None else total + part
        down_s[:, cols] = total.astype(BF)
    stores += [
        mover.start(down_s.at[b], out.at[a]) for a, b in down_places(D, H, me, S, F)
    ]
    wait_all(loads[2 * count :])
    for c in range(H // wide):
        total = None
        cols = slice(c * wide, c * wide + wide)
        for b in range(count):
            part = dot_tn(b_rows[b][...], dz_rows[b][:, cols])
            total = part if total is None else total + part
        up_s[:, cols] = total.astype(BF)
        piece = pl.ds(c * wide, wide)
        target = piece
        if in_plane(S, F):
            target = pl.ds(pl.multiple_of((me ^ c) * wide, wide), wide)
        stores.append(mover.start(up_s.at[:, piece], out.at[:, target]))
    wait_all(stores)


def feed_outer(dims, b_rows, dz_rows, g_rows, dm_rows):
    S, F, D, W, H = dims
    count = len(b_rows)
    L = b_rows[0].shape[0]
    operands = (*g_rows, *dm_rows, *b_rows, *dz_rows)
    return call(
        partial(feed_outer_kernel, dims, count),
        operands,
        [any_spec()] * len(operands),
        [((D, 2 * H), BF)],
        [hbm_spec()],
        [pltpu.VMEM(x.shape, BF) for x in operands]
        + [
            pltpu.VMEM((H, D), BF),
            pltpu.VMEM((D, H), BF),
            pltpu.SemaphoreType.DMA((4 * count + F * (H // W) + H // 256,)),
        ],
        4 * count * L * D * H,
        2 * (count * 2 * L * (D + H) + 2 * D * H),
        "feed_outer",
    )[0]


def feed_last_kernel(S, F, *refs):
    came, got, (up_out, down_out, held, sems) = refs[:S], refs[S], refs[S + 1 :]
    me = seq_place()
    core = lax.rem(lax.axis_index("fsdp").astype(jnp.int32), 2)
    mover = Mover(sems)
    loads = [mover.start(a, held.at[j]) for j, a in enumerate(came)]
    R, W = up_out.shape[0], up_out.shape[1] // S
    wait_all(loads)
    for slot in range(S):
        start = pl.multiple_of((me ^ slot) * W, W)
        up_out[:, pl.ds(start, W)] = held[slot, 0:R, :].astype(F32)
    near = lax.rem(me, 2) == core
    for k in range(2):
        rows = slice(k * 2 * R, k * 2 * R + 2 * R)
        here = held[me ^ (2 * core + k), R : 3 * R, :]
        down_out[rows, :] = jnp.where(near, here, got[k]).astype(F32)


def feed_last(S, F, came, got):
    R, W = came[0].shape[0] // 3, came[0].shape[1]
    return call(
        partial(feed_last_kernel, S, F),
        (*came, got),
        [any_spec()] * S + [vmem_spec()],
        [((R, S * W), F32), ((4 * R, W), F32)],
        [vmem_spec()] * 2,
        [pltpu.VMEM((S, 3 * R, W), BF), pltpu.SemaphoreType.DMA((S,))],
        R * W * S,
        R * W * 40,
        "feed_last",
    )


def total_of(refs, rows):
    total = None
    for ref in refs:
        value = ref[0, rows, :].astype(F32)
        total = value if total is None else total + value
    return total


def column_sum(v):
    return jnp.sum(v, axis=0, keepdims=True)


def finish_kernel(turn, *refs):
    if turn:
        refs = refs[1:]
    count = (len(refs) - 6) // 2
    ins, (y_hbm, dm_hbm, stat_out), refs = refs[:count], refs[count : count + 3], refs[count + 3 :]
    held, (y_out, dm_out, sems) = refs[: len(ins)], refs[len(ins) :]
    mover = Mover(sems)
    wait_all([mover.start(a, b) for a, b in zip(ins, held)])
    gains, u_ref, h_ref, dy_ref, *terms = held
    half = dm_out.shape[0] // 2
    stats = [None] * 5
    for part in range(2):
        rows = slice(part * half, part * half + half)
        m = total_of(terms, rows)
        unit, scale = norm_parts(m)
        f = unit * gains[3:4, :]
        h = h_ref[rows, :]
        y = h + f
        y_out[rows, :] = y.astype(BF)
        dy = dy_ref[rows, :].astype(F32)
        dm = norm_back(dy * gains[3:4, :], unit, scale)
        dm_out[rows, :] = dm.astype(BF)
        if part == 1:
            stores = [mover.start(dm_out, dm_hbm), mover.start(y_out, y_hbm.at[turn])]
        second, unused = norm_parts(u_ref[rows, :])
        e = second * gains[1:2, :]
        values = [dy * unit, h * h, y * y, e * e, f * f]
        for index, value in enumerate(values):
            value = column_sum(value)
            stats[index] = value if part == 0 else stats[index] + value
    stat_out[...] = jnp.zeros_like(stat_out)
    for index in range(5):
        stat_out[3 + index : 4 + index, :] = stats[index]
    wait_all(stores)


def finish(turn, B, joined, gains, u, h, dy, terms):
    r, D = u.shape
    outs = [((B, r, D), BF), ((r, D), BF), ((8, D), F32)]
    operands = (gains, u, h, dy, *terms)
    first = [] if joined is None else [joined]
    return call(
        partial(finish_kernel, turn),
        (*first, *operands),
        [hbm_spec()] * len(first) + [any_spec()] * len(operands),
        outs,
        [hbm_spec(), hbm_spec(), vmem_spec()],
        [pltpu.VMEM(x.shape, x.dtype) for x in operands]
        + [pltpu.VMEM((r, D), BF)] * 2
        + [pltpu.SemaphoreType.DMA((len(operands) + 2,))],
        60 * r * D,
        r * D * 20,
        "finish",
        {0: 0} if first else {},
    )


def middle_kernel(*refs):
    count = (len(refs) - 6) // 2
    ins, (dh_out, du_hbm, stat_out), refs = refs[:count], refs[count : count + 3], refs[count + 3 :]
    held, (dh_s, du_out, sems) = refs[: len(ins)], refs[len(ins) :]
    mover = Mover(sems)
    wait_all([mover.start(a, b) for a, b in zip(ins, held)])
    gains, u_ref, h_ref, dy_ref, *terms = held
    r, D = u_ref.shape
    half = r // 2
    stats = [None] * 2
    for part in range(2):
        rows = slice(part * half, part * half + half)
        back = total_of(terms, rows)
        unit, scale = norm_parts(h_ref[rows, :])
        third = column_sum(back * unit)
        dh = dy_ref[rows, :].astype(F32) + norm_back(back * gains[2:3, :], unit, scale)
        dh_s[rows, :] = dh
        unit, scale = norm_parts(u_ref[rows, :])
        second = column_sum(dh * unit)
        du_out[rows, :] = norm_back(dh * gains[1:2, :], unit, scale).astype(BF)
        for index, value in enumerate((second, third)):
            stats[index] = value if part == 0 else stats[index] + value
    stores = [mover.start(du_out, du_hbm), mover.start(dh_s, dh_out)]
    stat_out[...] = jnp.zeros_like(stat_out)
    stat_out[1:2, :] = stats[0]
    stat_out[2:3, :] = stats[1]
    wait_all(stores)


def middle(gains, u, h, dy, terms):
    r, D = u.shape
    outs = [((r, D), F32), ((r, D), BF), ((8, D), F32)]
    operands = (gains, u, h, dy, *terms)
    return call(
        middle_kernel,
        operands,
        [any_spec()] * len(operands),
        outs,
        [hbm_spec(), hbm_spec(), vmem_spec()],
        [pltpu.VMEM(x.shape, x.dtype) for x in operands]
        + [
            pltpu.VMEM((r, D), F32),
            pltpu.VMEM((r, D), BF),
            pltpu.SemaphoreType.DMA((len(operands) + 2,)),
        ],
        60 * r * D,
        r * D * 24,
        "middle",
    )


def last_kernel(turn, *refs):
    if turn:
        refs = refs[1:]
    count = (len(refs) - 3) // 2
    ins, joined, held, (out, sems) = refs[:count], refs[count], refs[count + 1 : -2], refs[-2:]
    mover = Mover(sems)
    wait_all([mover.start(a, b) for a, b in zip(ins, held)])
    gains, x_ref, dh_ref, *terms = held
    r, D = x_ref.shape
    half = r // 2
    for part in range(2):
        rows = slice(part * half, part * half + half)
        back = total_of(terms, rows)
        unit, scale = norm_parts(x_ref[rows, :].astype(F32))
        grad = dh_ref[rows, :] + norm_back(back * gains[0:1, :], unit, scale)
        out[rows, :] = grad.astype(BF)
    mover.start(out, joined.at[turn]).wait()


def last(turn, B, joined, gains, x, dh, terms):
    r, D = x.shape
    operands = (gains, x, dh, *terms)
    first = [] if joined is None else [joined]
    return call(
        partial(last_kernel, turn),
        (*first, *operands),
        [hbm_spec()] * len(first) + [any_spec()] * len(operands),
        [((B, r, D), BF)],
        [hbm_spec()],
        [pltpu.VMEM(x.shape, x.dtype) for x in operands]
        + [pltpu.VMEM((r, D), BF), pltpu.SemaphoreType.DMA((len(operands) + 1,))],
        40 * r * D,
        r * D * 14,
        "last",
        {0: 0} if first else {},
    )[0]


def block_groups(F):
    return [[0, 2, 3, 4], [1, 5, 6, 7]] if F == 8 else [list(range(F))]


def out_grad_kernel(dims, count, *refs):
    S, F, D, W = dims
    groups = block_groups(F)
    ins, outs, refs = refs[: (1 + S) * count], refs[(1 + S) * count :], None
    outs, (*held, sum_s, sems) = outs[: len(groups)], outs[len(groups) :]
    mover = Mover(sems)
    o_rows, dus = held[:count], held[count:]
    loads = [mover.start(a, b) for a, b in zip(ins[:count], o_rows)]
    for b in range(count):
        pieces = ins[count + b * S : count + b * S + S]
        loads += load_rows(mover, pieces, dus[b], seq_place())
    R = D // F
    places = block_places(F)
    stores = []
    wait_all(loads)
    total = None
    for b in range(count):
        part = dot_tn(o_rows[b][...], dus[b][...])
        total = part if total is None else total + part
    sum_s[...] = total.astype(BF)
    for group, out in zip(groups, outs):
        for i, index in enumerate(group):
            row = pl.multiple_of(places[index] // S * R, R)
            col = pl.multiple_of(places[index] % S * W, W)
            stores.append(
                mover.start(
                    sum_s.at[pl.ds(row, R), pl.ds(col, W)], out.at[i, pl.ds(3 * R, R)]
                )
            )
    wait_all(stores)


def out_grad(dims, o_rows, dus):
    S, F, D, W = dims
    count = len(o_rows)
    L = o_rows[0].shape[0]
    groups = block_groups(F)
    operands = (*o_rows, *[piece for du in dus for piece in du])
    return call(
        partial(out_grad_kernel, dims, count),
        operands,
        [any_spec()] * len(operands),
        [((len(group), 4 * (D // F) + EXTRA, W), BF) for group in groups],
        [hbm_spec()] * len(groups),
        [pltpu.VMEM(x.shape, BF) for x in o_rows]
        + [pltpu.VMEM((L, D), BF)] * count
        + [pltpu.VMEM((W, D), BF), pltpu.SemaphoreType.DMA(((1 + S) * count + F,))],
        2 * count * L * D * W,
        2 * (count * L * (D + W) + D * W),
        "out_grad",
    )


def qkv_grad_kernel(dims, count, many, *refs):
    S, F, D, W = dims
    groups = block_groups(F)
    n = len(groups)
    stats, refs = refs[n : n + many], refs[n + many :]
    ins, refs = refs[: 2 * count], refs[2 * count :]
    outs, (*held, sum_s, stat_s, sems) = refs[:n], refs[n:]
    held_stats, held = held[:many], held[many:]
    mover = Mover(sems)
    early = [mover.start(a, b) for a, b in zip(stats, held_stats)]
    loads = [mover.start(a, b) for a, b in zip(ins, held)]
    a_rows, grads = held[:count], held[count:]
    R = D // F
    places = [pl.multiple_of(place * R, R) for place in block_places(F)]
    stores = []
    wait_all(early)
    if F == 8:
        total = held_stats[0][...]
        for other in held_stats[1:]:
            total = total + other[...]
        squares = total[4:8, 0:R]
        for i in range(1, F):
            squares = squares + total[4:8, i * R : i * R + R]
        joined = jnp.concatenate([total[0:4], jnp.concatenate([squares] * F, axis=1)], axis=0)
        stat_s[0:8, 0:D] = joined.astype(BF)
        stat_s[8:16, 0:D] = jnp.zeros_like(total).astype(BF)
        for group, out in zip(groups, outs):
            for i, index in enumerate(group):
                stores.append(
                    mover.start(
                        stat_s.at[:, pl.ds(places[index], R)],
                        out.at[i, pl.ds(4 * R, EXTRA), pl.ds(0, R)],
                    )
                )
    wait_all(loads)
    for t in range(3):
        cols = slice(t * W, t * W + W)
        total = None
        for b in range(count):
            part = dot_tn(a_rows[b][...], grads[b][:, cols])
            total = part if total is None else total + part
        sum_s[:, cols] = total.astype(BF)
        for group, out in zip(groups, outs):
            for i, index in enumerate(group):
                stores.append(
                    mover.start(
                        sum_s.at[pl.ds(places[index], R), pl.ds(t * W, W)],
                        out.at[i, pl.ds(t * R, R)],
                    )
                )
    wait_all(stores)


def qkv_grad(dims, parts, stats, a_rows, grads):
    S, F, D, W = dims
    count = len(a_rows)
    L = a_rows[0].shape[0]
    operands = (*parts, *stats, *a_rows, *grads)
    return pl.pallas_call(
        partial(qkv_grad_kernel, dims, count, len(stats)),
        out_shape=tuple(jax.ShapeDtypeStruct(part.shape, part.dtype) for part in parts),
        in_specs=[hbm_spec()] * len(parts) + [any_spec()] * (len(operands) - len(parts)),
        out_specs=tuple([hbm_spec()] * len(parts)),
        input_output_aliases={i: i for i in range(len(parts))},
        scratch_shapes=[pltpu.VMEM(x.shape, x.dtype) for x in (*stats, *a_rows, *grads)]
        + [
            pltpu.VMEM((D, 3 * W), BF),
            pltpu.VMEM((EXTRA, D), BF),
            pltpu.SemaphoreType.DMA((2 * count + len(stats) + 4 * F,)),
        ],
        compiler_params=pltpu.CompilerParams(vmem_limit_bytes=VMEM_LIMIT),
        name="qkv_grad",
    )(*operands)


def deal_qkv_kernel(F, *refs):
    stacks, (one, two, held, sems) = refs[:F], refs[F:]
    me = seq_place()
    rows, cols = one.shape[1], one.shape[2]
    mover = Mover(sems)
    outs = (one, two)
    loads = []
    for i in range(F):
        for slot in (1, 2):
            start = pl.multiple_of(block_at(me, slot) * cols, cols)
            source = stacks[i].at[0, pl.ds(0, rows), pl.ds(start, cols)]
            loads.append(mover.start(source, held.at[slot - 1, i]))
    wait_all(loads)
    wait_all([mover.start(held.at[j], outs[j]) for j in range(2)])


def deal_qkv(R, W, stacks):
    F = len(stacks)
    return call(
        partial(deal_qkv_kernel, F),
        tuple(stacks),
        [any_spec()] * F,
        [((F, R, W), BF)] * 2,
        [hbm_spec()] * 2,
        [pltpu.VMEM((2, F, R, W), BF), pltpu.SemaphoreType.DMA((2 * F + 2,))],
        0,
        8 * F * R * W,
        "deal_qkv",
    )


def pair_sum_kernel(mine, got, *refs):
    outs, (mine_s, got_s, sum_s, sems) = refs[:4], refs[4:]
    mover = Mover(sems)
    loads = []
    for i in range(4):
        loads.append((mover.start(mine.at[i], mine_s.at[i]), mover.start(got.at[i], got_s.at[i])))
    stores = []
    for i in (3, 2, 1, 0):
        wait_all(loads[i])
        sum_s[i] = (mine_s[i].astype(F32) + got_s[i].astype(F32)).astype(BF)
        stores.append(mover.start(sum_s.at[i], outs[i]))
    wait_all(stores)


def pair_sum(mine, got):
    shape = mine.shape[1:]
    return call(
        pair_sum_kernel,
        (mine, got),
        [any_spec()] * 2,
        [(shape, BF)] * 4,
        [hbm_spec()] * 4,
        [pltpu.VMEM(mine.shape, BF)] * 3 + [pltpu.SemaphoreType.DMA((12,))],
        mine.size,
        6 * mine.size,
        "pair_sum",
    )


def last_sum_kernel(S, R, *refs):
    ins, (*moved, out_tile, stat_out), refs = refs[:4], refs[4:9], refs[9:]
    held, (sum_s, sems) = refs[:4], refs[4:]
    mover = Mover(sems)
    wait_all([mover.start(a, b) for a, b in zip(ins, held)])
    total = held[0][...].astype(F32)
    for ref in held[1:]:
        total = total + ref[...].astype(F32)
    sum_s[...] = total.astype(BF)
    stat_out[...] = total[4 * R : 4 * R + 8, 0 : stat_out.shape[1]]
    me = seq_place()
    stores = [mover.start(sum_s.at[pl.ds(3 * R, R)], out_tile)]
    for j in range(3):
        owner = me ^ j
        start = pl.multiple_of(lax.div(3 * owner + block_at(owner, j), S) * R, R)
        stores.append(mover.start(sum_s.at[pl.ds(start, R)], moved[j].at[pl.ds(0, R)]))
        stores.append(
            mover.start(sum_s.at[pl.ds(4 * R, EXTRA)], moved[j].at[pl.ds(R, EXTRA)])
        )
    wait_all(stores)


def last_sum(S, R, terms):
    rows, W = terms[0].shape
    return call(
        partial(last_sum_kernel, S, R),
        tuple(terms),
        [any_spec()] * 4,
        [((R + EXTRA, W), BF)] * 3 + [((R, W), BF), ((8, R), F32)],
        [hbm_spec()] * 4 + [vmem_spec()],
        [pltpu.VMEM((rows, W), BF)] * 5 + [pltpu.SemaphoreType.DMA((11,))],
        4 * rows * W,
        10 * rows * W,
        "last_sum",
    )


def flip(bits, size):
    return [(i, i ^ bits) for i in range(size)]


def add_low(*terms):
    total = terms[0].astype(F32)
    for term in terms[1:]:
        total = total + term.astype(F32)
    return total.astype(BF)


def gather_slots(own, S, me, turn):
    if S != 4:
        full = lax.all_gather(own, "seq")
        return [
            lax.dynamic_index_in_dim(full, me ^ slot, 0, keepdims=False) for slot in range(S)
        ]
    far = lax.ppermute(own, "seq", flip(3, S))
    return [own] + [lax.ppermute(own, "seq", flip(j, S)) for j in (1, 2)] + [far]


def slot_order(S, turn):
    return [[slot] for slot in range(S)]


def slot_shapes(S, turn, shape):
    return [((len(group), *shape), BF) for group in slot_order(S, turn)]


def scatter_slots(groups, S, me, turn):
    if S != 4:
        order = jnp.take(jnp.concatenate(groups), me ^ jnp.arange(S), axis=0)
        return [lax.psum_scatter(order, "seq", scatter_dimension=0, tiled=True)]
    return [groups[0]] + [lax.ppermute(groups[j], "seq", flip(j, S)) for j in (3, 1, 2)]


def swap_slots(pieces, S):
    return [pieces[0]] + [lax.ppermute(pieces[j], "seq", flip(j, S)) for j in range(1, S)]


def sum_everywhere(v, S, F):
    if S != 4 or F != 8:
        return lax.psum(v, ("seq", "fsdp"))
    v = v + lax.ppermute(v, "fsdp", flip(1, F))
    v = v + lax.ppermute(v, "seq", flip(1, S))
    v = v + lax.ppermute(v, "seq", flip(2, S))
    v = v + lax.ppermute(v, "fsdp", flip(2, F))
    return v + lax.ppermute(v, "fsdp", flip(4, F))


def gather_blocks(block, F, early=()):
    if F != 8:
        return [lax.all_gather(block, "fsdp")]
    near = lax.ppermute(block, "fsdp", flip(1, F))
    far = [lax.ppermute(block, "fsdp", flip(j, F)) for j in (2, 4, 6)]
    far = after(far, near, *early)
    rest = [lax.ppermute(piece, "fsdp", flip(1, F)) for piece in far]
    return [piece[None] for piece in (block, near, *far, *rest)]


def after(value, *others):
    return lax.optimization_barrier((value, others))[0]


def blocks_in(blocks, S, me):
    moved = []
    for j in range(3):
        pairs = [(s, (3 * s + j) % S) for s in range(S)]
        moved.append(lax.ppermute(blocks[j], "seq", pairs))
    stack = jnp.stack(moved)
    return [
        lax.dynamic_index_in_dim(stack, (me + S * t) % 3, 0, keepdims=False) for t in range(3)
    ]


def blocks_out_pairs(S, j):
    return [((3 * s + j) % S, s) for s in range(S)]


def blocks_out(stack, S, me):
    moved = []
    for j in range(3):
        t = ((j - me) * (S % 3)) % 3
        piece = lax.dynamic_index_in_dim(stack, t, 0, keepdims=False)
        moved.append(lax.ppermute(piece, "seq", blocks_out_pairs(S, j)))
    return jnp.concatenate(moved, axis=1)


def turn_pairs(S, F):
    each = F // S
    return [
        (s * F + f, (f // each) * F + (f % each) * S + s) for s in range(S) for f in range(F)
    ]


def shards(tokens, cotangent, prefix, qkv_weight, out_weight, up_weight, down_weight, norm_gains):
    S, F = lax.axis_size("seq"), lax.axis_size("fsdp")
    B, r, D = tokens.shape
    heads = D // HEAD // S
    W = D // S
    R = D // F
    H = up_weight.shape[1]
    tiles = H // W
    me = seq_place()
    place = lax.axis_index("fsdp").astype(jnp.int32)
    pairs = turn_pairs(S, F)

    down_late, out_late = down_weight, out_weight
    axes = ("seq", "fsdp")
    if in_plane(S, F):
        gain_rows = jnp.pad(norm_gains, ((0, EXTRA - 4), (0, 3 * W - R)))
        first_block = jnp.concatenate([qkv_weight, gain_rows])
        near_block = lax.ppermute(first_block, "fsdp", flip(1, F))
        far = [lax.ppermute(first_block, "fsdp", flip(j, F)) for j in (2, 4, 6)]
        core = place % 2
        other = lax.ppermute(down_late, "fsdp", flip(1, F))
        halves = jnp.concatenate([down_late, other]).reshape(4, 2 * R, W)
        sent = []
        for j in range(S):
            target = me ^ j
            index = jnp.where(target // 2 == core, 0, 2) + target % 2
            piece = lax.dynamic_index_in_dim(halves, index, 0, keepdims=False)
            up_tile = lax.dynamic_slice_in_dim(up_weight, target * W, W, 1)
            sent.append(jnp.concatenate([up_tile, piece, out_late]))
        came, far, near_block = lax.optimization_barrier((swap_slots(sent, S), far, near_block))
        ups = [message[:R] for message in came]
        out_tiles = [message[3 * R :] for message in came]
        near = (me % 2) ^ core == 0
        pieces = [
            jnp.where(near, came[2 * i][R : 3 * R], came[2 * i + 1][R : 3 * R])
            for i in range(2)
        ]
        downs = [piece[t * R : t * R + R] for piece in pieces for t in range(2)]
    else:
        ups = [up_weight]
        down_mine = lax.ppermute(down_late, axes, pairs)
        downs = [down_mine[i * R : i * R + R] for i in range(tiles)]
        out_tiles = gather_slots(out_late, S, me, 0)
    ff_mine = jnp.concatenate([*ups, *downs, *out_tiles], axis=1)
    if in_plane(S, F):
        rest = [lax.ppermute(piece, "fsdp", flip(1, F)) for piece in far]
        stacks = [piece[None] for piece in (first_block, near_block, *far, *rest)]
        one, two = deal_qkv(R, W, stacks)
        one = lax.ppermute(one, "seq", flip(1, S))
        two = lax.ppermute(two, "seq", flip(2, S))
        all_x = [gather_slots(tokens[:1], S, me, 0)]
        all_x += [gather_slots(after(tokens[b : b + 1], one, two), S, me, 0) for b in range(1, B)]
        stacks = [*stacks, one, two]
    else:
        blocks = [qkv_weight[:, j * W : j * W + W] for j in range(3)]
        all_x = [gather_slots(tokens[b : b + 1], S, me, 0) for b in range(B)]
        stacks = gather_blocks(jnp.concatenate(blocks_in(blocks, S, me)), F)
    if in_plane(S, F):
        pass
    ff_full = lax.all_gather(ff_mine, "fsdp", axis=0, tiled=True)
    gains = None
    if F != 8:
        gains = lax.all_gather(norm_gains, "fsdp", axis=1, tiled=True).astype(F32)
        gains = jnp.pad(gains, ((0, 4), (0, 0)))
    att_dims = (S, F, r, D, heads)
    ff_dims = (S, F, r, D, W, H)
    a_all, qkv_all, p_all, os, os_own = [], [], [], [], []
    for b in range(B):
        a, qkv, o, p, gains_full = attend(att_dims, b, prefix, gains, stacks, all_x[b])
        a_all.append(a)
        qkv_all.append(qkv)
        p_all.append(p)
        os_own.append(o)
        os.append(gather_slots(o, S, me, b))
    gains = gains_full
    b_all, u_own, h_own, g_all, gp_all, m_terms = [], [], [], [], [], []
    for b in range(B):
        res = feed(ff_dims, b, gains, ff_full, all_x[b], os[b])
        b_all.append(res[0])
        u_own.append(res[1])
        h_own.append(res[2])
        g_all.append(res[3])
        gp_all.append(res[4])
        m_terms.append(scatter_slots(list(res[5:]), S, me, b))
    y, stats, dms = None, [], []
    for b in range(B):
        y, dm, stat = finish(b, B, y, gains, u_own[b], h_own[b], cotangent[b], m_terms[b])
        stats.append(stat)
        dms.append(gather_slots(dm, S, me, b))
    dm_all, dz_all, h_terms = [], [], []
    for b in range(B):
        res = feed_back(ff_dims, b, ff_full, gp_all[b], dms[b])
        dm_all.append(res[0])
        dz_all.append(res[1])
        h_terms.append(scatter_slots(list(res[2:]), S, me, b))
    dhs, dus = [], []
    for b in range(B):
        dh, du, stat = middle(gains, u_own[b], h_own[b], cotangent[b], h_terms[b])
        dhs.append(dh)
        dus.append(gather_slots(du, S, me, b))
        stats.append(stat)
    dm_all = after(dm_all, h_terms[0])
    ff_part = feed_outer((S, F, D, W, H), b_all, dz_all, g_all, dm_all)
    ff_sum = lax.psum_scatter(ff_part, "fsdp", scatter_dimension=0, tiled=True)
    back_pairs = [(b, a) for a, b in pairs]
    if not in_plane(S, F):
        down_sum = jnp.concatenate(
            [ff_sum[:, H + i * W : H + i * W + W] for i in range(tiles)], axis=0
        )
        down_grad = lax.ppermute(down_sum, axes, back_pairs).astype(F32)
        up_grad = ff_sum[:, :H].astype(F32)
    dqkvs, x_terms = [], []
    for b in range(B):
        res = attend_back(
            att_dims, b, gains, ff_full, stacks, a_all[b], qkv_all[b], p_all[b], dus[b]
        )
        dqkvs.append(res[0])
        stats.append(res[1])
        x_terms.append(scatter_slots(list(res[2:]), S, me, b))
    grad_dims = (S, F, D, W)
    parts = after(out_grad(grad_dims, os_own, dus), dqkvs)
    parts = after(parts, x_terms[0])
    parts = qkv_grad(grad_dims, parts, stats, a_all, dqkvs)
    if F == 8 and S == 4:
        kept = pair_sum(parts[0], lax.ppermute(parts[1], "fsdp", flip(1, F)))
        ff_sum = after(ff_sum, kept)
        got = [lax.ppermute(kept[j], "fsdp", flip(2 * j, F)) for j in (3, 2, 1)]
        pieces = [ff_sum[:, H + i * W : H + i * W + W] for i in range(4)]
        sent = [
            jnp.concatenate([ff_sum[:, j * W : j * W + W], *pieces[j // 2 * 2 : j // 2 * 2 + 2]])
            for j in range(S)
        ]
        came = swap_slots(sent, S)
        got = after(got, came)
        whole = jnp.stack(came)[:, R:]
        away = jnp.stack(
            [
                lax.dynamic_index_in_dim(whole, me ^ (2 * (1 - place % 2) + k), 0, keepdims=False)
                for k in range(2)
            ]
        )
        up_grad, down_grad = feed_last(S, F, came, lax.ppermute(away, "fsdp", flip(1, F)))
        *moved, out_tile, stat = last_sum(S, R, [kept[0], *got])
        moved[1:] = [lax.ppermute(moved[j], "seq", flip(j, S)) for j in (1, 2)]
        missed = lax.ppermute(stat, "seq", flip(3, S))
        for piece in moved:
            missed = missed + piece[R : R + 8, :R].astype(F32)
        odd = me % 2 == 1
        ends = (moved[0][:R], moved[2][:R])
        qkv_own = jnp.concatenate(
            [jnp.where(odd, ends[1], ends[0]), moved[1][:R], jnp.where(odd, ends[0], ends[1])],
            axis=1,
        )
        gains_grad, squares = missed[:4], jnp.sum(missed[4:], axis=1)
    else:
        rest = lax.psum_scatter(parts[0], "fsdp", scatter_dimension=0, tiled=False)
        qkv_own = blocks_out(jnp.stack([rest[t * R : t * R + R] for t in range(3)]), S, me)
        out_tile = rest[3 * R : 4 * R]
        totals = lax.psum(sum(stats), ("seq", "fsdp"))
        gains_grad = lax.dynamic_slice_in_dim(totals[:4], place * R, R, 1)
        squares = jnp.sum(totals[4:], axis=1)
    input_grad = None
    for b in range(B):
        input_grad = last(b, B, input_grad, gains, tokens[b], dhs[b], x_terms[b])

    out_own = lax.ppermute(out_tile, ("seq", "fsdp"), back_pairs)
    entries = B * r * D * S * F
    stream_rms = jnp.sqrt(squares / entries)
    return (
        y,
        input_grad,
        qkv_own.astype(F32),
        out_own.astype(F32),
        up_grad,
        down_grad,
        gains_grad,
        stream_rms,
    )


def solution(mesh):
    in_specs = (
        P("fsdp", "seq", None),
        P("fsdp", "seq", None),
        P("fsdp"),
        P("fsdp", "seq"),
        P("fsdp", "seq"),
        P("fsdp", "seq"),
        P("fsdp", "seq"),
        P(None, "fsdp"),
    )
    out_specs = (
        P("fsdp", "seq", None),
        P("fsdp", "seq", None),
        P("fsdp", "seq"),
        P("fsdp", "seq"),
        P("fsdp", "seq"),
        P("fsdp", "seq"),
        P(None, "fsdp"),
        P(),
    )
    return jax.shard_map(shards, mesh=mesh, in_specs=in_specs, out_specs=out_specs, check_vma=False)
```

```python
import math
from functools import partial

import jax
import jax.numpy as jnp
from jax import lax
from jax.experimental import pallas as pl
from jax.experimental.pallas import tpu as pltpu
from jax.sharding import PartitionSpec as P

HEAD = 64
NORM_EPSILON = 1e-05
MASKED_SCORE = -1e30
VMEM_LIMIT = 48 * 1024 * 1024
BF = jnp.bfloat16
F32 = jnp.float32
BLOCK_ORDER = (0, 1, 2, 4, 6, 3, 5, 7)
EXTRA = 16
COST = 0.001


def dot_nn(a, b):
    return lax.dot_general(a, b, (((1,), (0,)), ((), ())), preferred_element_type=F32)


def dot_nt(a, b):
    return lax.dot_general(a, b, (((1,), (1,)), ((), ())), preferred_element_type=F32)


def dot_tn(a, b):
    return lax.dot_general(a, b, (((0,), (0,)), ((), ())), preferred_element_type=F32)


def norm_parts(v):
    centre = jnp.mean(v, axis=-1, keepdims=True)
    shifted = v - centre
    spread = jnp.mean(shifted * shifted, axis=-1, keepdims=True)
    scale = lax.rsqrt(spread + NORM_EPSILON)
    return shifted * scale, scale


def norm_back(grad_unit, unit, scale):
    first = jnp.mean(grad_unit, axis=-1, keepdims=True)
    second = jnp.mean(grad_unit * unit, axis=-1, keepdims=True)
    return scale * (grad_unit - first - unit * second)


def seq_place():
    return lax.axis_index("seq").astype(jnp.int32)


def block_places(F):
    if F != 8:
        return [jnp.int32(i) for i in range(F)]
    place = lax.axis_index("fsdp").astype(jnp.int32)
    return [place ^ i for i in BLOCK_ORDER]


class Mover:
    def __init__(self, sems):
        self.sems = sems
        self.used = 0

    def start(self, src, dst):
        copy = pltpu.make_async_copy(src, dst, self.sems.at[self.used])
        self.used += 1
        copy.start()
        return copy


def wait_all(copies):
    for copy in copies:
        copy.wait()


def load_rows(mover, pieces, target, me):
    r = pieces[0].shape[0]
    copies = []
    for slot, piece in enumerate(pieces):
        start = pl.multiple_of((me ^ slot) * r, r)
        copies.append(mover.start(piece, target.at[pl.ds(start, r)]))
    return copies


def store_rows(mover, source, outs, order, me):
    r = outs[0].shape[1]
    copies = []
    for group, out in zip(order, outs):
        for i, slot in enumerate(group):
            start = pl.multiple_of((me ^ slot) * r, r)
            copies.append(mover.start(source.at[pl.ds(start, r)], out.at[i]))
    return copies


def in_plane(S, F):
    return S == 4 and F == 8


def block_at(s, slot):
    if slot == 1:
        return jnp.int32(1)
    odd = lax.rem(s, 2)
    return 2 * odd if slot == 0 else 2 - 2 * odd


def load_qkv(mover, weights, target, me, S, F):
    places, copies = block_places(F), []
    rows, cols = target.shape[0] // F, target.shape[1] // 3
    if in_plane(S, F):
        stacks, moved = weights[:F], weights[F:]
        for slot in range(3):
            sender = me ^ slot
            at = block_at(sender, slot)
            part = lax.div(3 * sender + at, S)
            col = pl.ds(pl.multiple_of(part * cols, cols), cols)
            from_col = pl.ds(pl.multiple_of(at * cols, cols), cols)
            for i in range(F):
                row = pl.ds(pl.multiple_of(places[i] * rows, rows), rows)
                if slot == 0:
                    source = stacks[i].at[0, pl.ds(0, rows), from_col]
                else:
                    source = moved[slot - 1].at[i]
                copies.append(mover.start(source, target.at[row, col]))
        return copies
    stack = weights[0]
    for i in range(F):
        row = pl.ds(pl.multiple_of(places[i] * rows, rows), rows)
        for t in range(3):
            copies.append(
                mover.start(
                    stack.at[i, pl.ds(t * rows, rows)], target.at[row, pl.ds(t * cols, cols)]
                )
            )
    return copies


def load_gains(mover, stacks, target, F):
    places, copies = block_places(F), []
    width = target.shape[1] // F
    for i, stack in enumerate(stacks[:F]):
        start = pl.multiple_of(places[i] * width, width)
        last = stack.shape[1] - EXTRA
        copies.append(
            mover.start(
                stack.at[0, pl.ds(last, EXTRA), pl.ds(0, width)],
                target.at[:, pl.ds(start, width)],
            )
        )
    return copies


def any_spec():
    return pl.BlockSpec(memory_space=pl.ANY)


def hbm_spec():
    return pl.BlockSpec(memory_space=pltpu.HBM)


def smem_spec():
    return pl.BlockSpec(memory_space=pltpu.SMEM)


def vmem_spec():
    return pl.BlockSpec(memory_space=pltpu.VMEM)


def call(body, operands, in_specs, outs, out_specs, scratch, flops, bytes_accessed, name, aliases={}, limit=VMEM_LIMIT):
    return pl.pallas_call(
        body,
        out_shape=tuple(jax.ShapeDtypeStruct(shape, dtype) for shape, dtype in outs),
        in_specs=in_specs,
        out_specs=tuple(out_specs),
        scratch_shapes=scratch,
        input_output_aliases=aliases,
        compiler_params=pltpu.CompilerParams(vmem_limit_bytes=limit),
        cost_estimate=pl.CostEstimate(
            flops=int(flops * COST), bytes_accessed=int(bytes_accessed * COST), transcendentals=0
        ),
        name=name,
    )(*operands)


def attend_kernel(dims, count, turn, packed, prefix, *refs):
    S, F, r, D, heads = dims
    L, W = S * r, heads * HEAD
    if packed:
        gains_in = None
    else:
        gains_in, refs = refs[0], refs[1:]
    weights, pieces, refs = refs[:count], refs[count : count + S], refs[count + S :]
    a_out, qkv_out, o_out, p_out, gains_out, refs = *refs[:5], refs[5:]
    x_s, w_s, a_s, qkv_s, o_s, p_s, bias_s, raw_s, sems = refs
    me, limit_len = seq_place(), prefix[turn]
    mover = Mover(sems)
    gain_loads = load_gains(mover, weights, raw_s, F) if packed else []
    loads = load_rows(mover, [piece.at[0] for piece in pieces], x_s, me)
    weight_loads = load_qkv(mover, weights, w_s, me, S, F)
    tile = 128
    limit = L // 2
    for i in range(L // tile):
        shape = (tile, max((i + 1) * tile, limit))
        rows = i * tile + lax.broadcasted_iota(jnp.int32, shape, 0)
        cols = lax.broadcasted_iota(jnp.int32, shape, 1)
        seen = (cols <= rows) | (cols < limit_len)
        bias_s[i * tile : i * tile + tile, : shape[1]] = jnp.where(seen, 0.0, MASKED_SCORE)
    wait_all(gain_loads)
    gains_out[...] = raw_s[0:8, :].astype(F32) if packed else gains_in[...]
    wait_all(loads)
    for i in range(L // tile):
        rows = slice(i * tile, i * tile + tile)
        unit, scale = norm_parts(x_s[rows, :].astype(F32))
        a_s[rows, :] = (unit * gains_out[0:1, :]).astype(BF)
    stores = [mover.start(a_s, a_out)]
    wait_all(weight_loads)
    for c in range(3):
        cols = slice(c * W, c * W + W)
        qkv_s[:, cols] = dot_nn(a_s[...], w_s[:, cols]).astype(BF)
    stores.append(mover.start(qkv_s, qkv_out))
    lane = lax.broadcasted_iota(jnp.int32, (1, 128), 1)
    for pair in range(heads // 2):
        q2 = qkv_s[:, pair * 128 : pair * 128 + 128] * BF(HEAD**-0.5)
        k2 = qkv_s[:, W + pair * 128 : W + pair * 128 + 128]
        v2 = qkv_s[:, 2 * W + pair * 128 : 2 * W + pair * 128 + 128]
        keys, values = [], []
        for side in range(2):
            mine = (lane >= 64) if side else (lane < 64)
            keys.append(jnp.where(mine, k2, BF(0)))
            values.append(jnp.where(mine, v2, BF(0)))
        for i in range(L // tile):
            rows = slice(i * tile, i * tile + tile)
            span = max((i + 1) * tile, limit)
            total = None
            for side in range(2):
                scores = dot_nt(q2[rows], keys[side][:span]) + bias_s[rows, :span]
                top = jnp.max(scores, axis=-1, keepdims=True)
                weights_here = jnp.exp(scores - top)
                share = 1.0 / jnp.sum(weights_here, axis=-1, keepdims=True)
                probs = (weights_here * share).astype(BF)
                p_s[2 * pair + side, rows, :span] = probs
                part = dot_nn(probs, values[side][:span])
                total = part if total is None else total + part
            o_s[rows, pair * 128 : pair * 128 + 128] = total.astype(BF)
        for side in range(2):
            stores.append(mover.start(p_s.at[2 * pair + side], p_out.at[2 * pair + side]))
    stores.append(mover.start(o_s, o_out))
    wait_all(stores)


def attend(dims, turn, prefix, gains, weights, pieces):
    S, F, r, D, heads = dims
    L, W = S * r, heads * HEAD
    outs = [((L, D), BF), ((L, 3 * W), BF), ((L, W), BF), ((heads, L, L), BF), ((8, D), F32)]
    scratch = [
        pltpu.VMEM((L, D), BF),
        pltpu.VMEM((D, 3 * W), BF),
        pltpu.VMEM((L, D), BF),
        pltpu.VMEM((L, 3 * W), BF),
        pltpu.VMEM((L, W), BF),
        pltpu.VMEM((heads, L, L), BF),
        pltpu.VMEM((L, L), F32),
        pltpu.VMEM((EXTRA, D), BF),
        pltpu.SemaphoreType.DMA((S + 4 * F + heads + 3,)),
    ]
    flops = 2 * L * D * 3 * W + 4 * heads * L * L * HEAD * 4
    size = 2 * (2 * L * D + 3 * D * W + 4 * L * W + heads * L * L)
    packed = gains is None
    extra = [] if packed else [gains]
    return call(
        partial(attend_kernel, dims, len(weights), turn, packed),
        (prefix, *extra, *weights, *pieces),
        [smem_spec()]
        + [vmem_spec()] * len(extra)
        + [any_spec()] * (len(weights) + len(pieces)),
        outs,
        [hbm_spec()] * 4 + [vmem_spec()],
        scratch,
        flops,
        size,
        "attend",
    )


def attend_back_kernel(dims, count, order, gains_in, out_w, *refs):
    S, F, r, D, heads = dims
    n = len(order)
    L, W = S * r, heads * HEAD
    weights, refs = refs[:count], refs[count:]
    a_in, qkv, probs_in, pieces, refs = *refs[:3], refs[3 : 3 + S], refs[3 + S :]
    grad_out, stat_out, slots, refs = *refs[:2], refs[2 : 2 + n], refs[2 + n :]
    w_s, qkv_s, p_s, du_s, do_s, d_s, grad_s, part_s, a_s, out_s, gains, sems = refs
    me = seq_place()
    mover = Mover(sems)
    own = pl.ds(pl.multiple_of(me * W, W), W)
    loads = load_out(mover, out_w, out_s, own, me, S) + load_rows(mover, pieces, du_s, me)
    loads.append(mover.start(qkv, qkv_s))
    prob_loads = [mover.start(probs_in.at[h], p_s.at[h]) for h in range(heads)]
    late_loads = load_qkv(mover, weights, w_s, me, S, F)
    late_loads.append(mover.start(a_in, a_s))
    late_loads.append(mover.start(gains_in, gains))
    tile = 128
    limit = L // 2
    wait_all(loads)
    do_s[...] = dot_nt(du_s[...], out_s[...]).astype(BF)
    lane = lax.broadcasted_iota(jnp.int32, (1, 128), 1)
    for pair in range(heads // 2):
        cols = slice(pair * 128, pair * 128 + 128)
        q2 = qkv_s[:, cols] * BF(HEAD**-0.5)
        k2 = qkv_s[:, W + pair * 128 : W + pair * 128 + 128] * BF(HEAD**-0.5)
        v2 = qkv_s[:, 2 * W + pair * 128 : 2 * W + pair * 128 + 128]
        do2 = do_s[:, cols]
        queries, keys, values, grads = [], [], [], []
        for side in range(2):
            mine = (lane >= 64) if side else (lane < 64)
            queries.append(jnp.where(mine, q2, BF(0)))
            keys.append(jnp.where(mine, k2, BF(0)))
            values.append(jnp.where(mine, v2, BF(0)))
            grads.append(jnp.where(mine, do2, BF(0)))
            prob_loads[2 * pair + side].wait()
        for i in range(L // tile):
            rows = slice(i * tile, i * tile + tile)
            span = max((i + 1) * tile, limit)
            total = None
            for side in range(2):
                probs = p_s[2 * pair + side, rows, :span].astype(F32)
                grad_probs = dot_nt(do2[rows], values[side][:span])
                delta = jnp.sum(probs * grad_probs, axis=-1, keepdims=True)
                grad_scores = (probs * (grad_probs - delta)).astype(BF)
                d_s[side, rows, :span] = grad_scores
                part = dot_nn(grad_scores, keys[side][:span])
                total = part if total is None else total + part
            grad_s[rows, cols] = total.astype(BF)
        for j in range(L // tile):
            columns = slice(j * tile, j * tile + tile)
            low = 0 if (j * tile) < limit else j * tile
            total_k, total_v = None, None
            for side in range(2):
                part = dot_tn(d_s[side, low:, columns], queries[side][low:])
                total_k = part if total_k is None else total_k + part
                part = dot_tn(p_s[2 * pair + side, low:, columns], grads[side][low:])
                total_v = part if total_v is None else total_v + part
            grad_s[columns, W + pair * 128 : W + pair * 128 + 128] = total_k.astype(BF)
            grad_s[columns, 2 * W + pair * 128 : 2 * W + pair * 128 + 128] = total_v.astype(BF)
    stores = [mover.start(grad_s, grad_out)]
    wait_all(late_loads)
    wide = 256
    stat_out[...] = jnp.zeros_like(stat_out)

    for c in range(D // wide):
        cols = slice(c * wide, c * wide + wide)
        part = dot_nt(grad_s[...], w_s[cols, :])
        part_s[:, cols] = part.astype(BF)
        stat_out[0:1, cols] = column_sum(part * a_s[:, cols].astype(F32)) / gains[0:1, cols]
    stores += store_rows(mover, part_s, slots, order, me)
    wait_all(stores)


def attend_back(dims, turn, gains, out_w, weights, a, qkv, probs, pieces):
    S, F, r, D, heads = dims
    L, W = S * r, heads * HEAD
    outs = [((L, 3 * W), BF), ((8, D), F32)] + slot_shapes(S, turn, (r, D))
    blocks = 3 * F
    scratch = [
        pltpu.VMEM((D, 3 * W), BF),
        pltpu.VMEM((L, 3 * W), BF),
        pltpu.VMEM((heads, L, L), BF),
        pltpu.VMEM((L, D), BF),
        pltpu.VMEM((L, W), BF),
        pltpu.VMEM((2, L, L), BF),
        pltpu.VMEM((L, 3 * W), BF),
        pltpu.VMEM((L, D), BF),
        pltpu.VMEM((L, D), BF),
        pltpu.VMEM((W, D), BF),
        pltpu.VMEM((8, D), F32),
        pltpu.SemaphoreType.DMA((3 * S + heads + 5 + blocks,)),
    ]
    flops = 2 * L * D * 4 * W + 8 * heads * L * L * HEAD * 4
    size = 2 * (2 * L * D + 3 * D * W + 7 * L * W + heads * L * L)
    return call(
        partial(attend_back_kernel, dims, len(weights), slot_order(S, turn)),
        (gains, out_w, *weights, a, qkv, probs, *pieces),
        [any_spec()] * 2
        + [any_spec()] * (3 + len(weights) + len(pieces)),
        outs,
        [hbm_spec(), vmem_spec()] + [hbm_spec()] * (len(outs) - 2),
        scratch,
        flops,
        size,
        "attend_back",
    )


def load_out(mover, ff_w, target, rows, me, S):
    D = target.shape[1]
    W, base = D // S, ff_w.shape[1] - D
    copies = []
    for slot in range(S):
        start = pl.multiple_of((me ^ slot) * W, W)
        copies.append(
            mover.start(
                ff_w.at[rows, pl.ds(base + slot * W, W)], target.at[:, pl.ds(start, W)]
            )
        )
    return copies


def load_up(mover, ff_w, up_s, me, S, F):
    H = up_s.shape[1]
    if not in_plane(S, F):
        return [mover.start(ff_w.at[:, pl.ds(0, H)], up_s)]
    W, copies = H // S, []
    for slot in range(S):
        start = pl.multiple_of((me ^ slot) * W, W)
        copies.append(
            mover.start(ff_w.at[:, pl.ds(slot * W, W)], up_s.at[:, pl.ds(start, W)])
        )
    return copies


def down_places(D, H, me, S, F):
    W, R = D // S, D // F
    if in_plane(S, F):
        for f in range(F):
            for col in range(2):
                part = col ^ lax.div(me, 2)
                for t in range(2):
                    start = pl.multiple_of(H + (2 * part + t) * W, W)
                    yield (
                        (pl.ds(f * R, R), pl.ds(start, W)),
                        (pl.ds(f // 2 * 2 * R + t * R, R), pl.ds((f % 2 + 2 * col) * W, W)),
                    )
        return
    for f in range(F):
        for i in range(H // W):
            yield (
                (pl.ds(f * R, R), pl.ds(H + i * W, W)),
                (pl.ds(f // S * (R * (H // W)) + i * R, R), pl.ds(f % S * W, W)),
            )


def load_down(mover, ff_w, down_s, me, S, F):
    H, D = down_s.shape
    return [mover.start(ff_w.at[a], down_s.at[b]) for a, b in down_places(D, H, me, S, F)]


def feed_kernel(dims, order, turn, gains_in, ff_w, *refs):
    S, F, r, D, W, H = dims
    L, n = S * r, len(order)
    xs, os, refs = refs[:S], refs[S : 2 * S], refs[2 * S :]
    b_out, u_own, h_own, g_out, gp_out, slots, refs = *refs[:5], refs[5 : 5 + n], refs[5 + n :]
    x_s, o_s, out_s, u_s, h_s, up_s, down_s, b_s, g_s, gp_s, m_s, gains, sems = refs
    me = seq_place()
    mover = Mover(sems)
    loads = [mover.start(gains_in, gains)]
    for slot in range(S):
        start = pl.multiple_of((me ^ slot) * W, W)
        loads.append(mover.start(os[slot], o_s.at[:, pl.ds(start, W)]))
    loads += load_out(mover, ff_w, out_s, pl.ds(0, D), me, S)
    loads += load_rows(mover, [x.at[0] for x in xs], x_s, me)
    up_loads = load_up(mover, ff_w, up_s, me, S, F)
    down_loads = load_down(mover, ff_w, down_s, me, S, F)
    wide, tall = 256, 256
    wait_all(loads)
    for i in range(L // tall):
        rows = slice(i * tall, i * tall + tall)
        for c in range(D // wide):
            cols = slice(c * wide, c * wide + wide)
            u_s[rows, cols] = dot_nn(o_s[rows, :], out_s[:, cols])
        unit, scale = norm_parts(u_s[rows, :])
        h = x_s[rows, :].astype(F32) + unit * gains[1:2, :]
        h_s[rows, :] = h
        unit, scale = norm_parts(h)
        b_s[rows, :] = (unit * gains[2:3, :]).astype(BF)
    own = pl.ds(pl.multiple_of(me * r, r), r)
    stores = [
        mover.start(b_s, b_out),
        mover.start(u_s.at[own], u_own),
        mover.start(h_s.at[own], h_own),
    ]
    wait_all(up_loads)
    root = math.sqrt(2.0 / math.pi)
    for c in range(H // wide):
        cols = slice(c * wide, c * wide + wide)
        z = dot_nn(b_s[...], up_s[:, cols])
        square = z * z
        bent = jnp.tanh(z * (root + root * 0.044715 * square))
        side = 0.5 + 0.5 * bent
        g_s[:, cols] = (z * side).astype(BF)
        slope = z * (root + 3.0 * root * 0.044715 * square)
        gp_s[:, cols] = (side + (0.5 * slope) * (1.0 - bent * bent)).astype(BF)
    stores += [mover.start(g_s, g_out), mover.start(gp_s, gp_out)]
    wait_all(down_loads)
    for c in range(D // wide):
        cols = slice(c * wide, c * wide + wide)
        m_s[:, cols] = dot_nn(g_s[...], down_s[:, cols]).astype(BF)
    stores += store_rows(mover, m_s, slots, order, me)
    wait_all(stores)


def feed(dims, turn, gains, ff_w, xs, os):
    S, F, r, D, W, H = dims
    L = S * r
    outs = [((L, D), BF), ((r, D), F32), ((r, D), F32), ((L, H), BF), ((L, H), BF)]
    outs += slot_shapes(S, turn, (r, D))
    scratch = [
        pltpu.VMEM((L, D), BF),
        pltpu.VMEM((L, D), BF),
        pltpu.VMEM((D, D), BF),
        pltpu.VMEM((L, D), F32),
        pltpu.VMEM((L, D), F32),
        pltpu.VMEM((D, H), BF),
        pltpu.VMEM((H, D), BF),
        pltpu.VMEM((L, D), BF),
        pltpu.VMEM((L, H), BF),
        pltpu.VMEM((L, H), BF),
        pltpu.VMEM((L, D), BF),
        pltpu.VMEM((8, D), F32),
        pltpu.SemaphoreType.DMA((5 * S + F * (H // W) + 7,)),
    ]
    return call(
        partial(feed_kernel, dims, slot_order(S, turn), turn),
        (gains, ff_w, *xs, *os),
        [any_spec()] * (2 + 2 * S),
        outs,
        [hbm_spec()] * len(outs),
        scratch,
        2 * L * D * D + 4 * L * D * H,
        2 * (D * D + 2 * D * H + 5 * L * D + 2 * L * H),
        "feed",
        limit=56 * 1024 * 1024,
    )


def feed_back_kernel(dims, order, ff_w, gp, *refs):
    S, F, r, D, W, H = dims
    pieces, dm_out, dz_out, refs = refs[:S], *refs[S : S + 2], refs[S + 2 :]
    slots, refs = refs[: len(order)], refs[len(order) :]
    up_s, down_s, gp_s, dm_s, dz_s, part_s, sems = refs
    me = seq_place()
    mover = Mover(sems)
    loads = load_rows(mover, pieces, dm_s, me)
    down_loads = load_down(mover, ff_w, down_s, me, S, F)
    down_loads.append(mover.start(gp, gp_s))
    up_loads = load_up(mover, ff_w, up_s, me, S, F)
    wide = 256
    wait_all(loads)
    stores = [mover.start(dm_s, dm_out)]
    wait_all(down_loads)

    for c in range(H // wide):
        cols = slice(c * wide, c * wide + wide)
        grad = dot_nt(dm_s[...], down_s[cols, :])
        dz_s[:, cols] = (grad * gp_s[:, cols].astype(F32)).astype(BF)
    stores.append(mover.start(dz_s, dz_out))
    wait_all(up_loads)

    for c in range(D // wide):
        cols = slice(c * wide, c * wide + wide)
        part_s[:, cols] = dot_nt(dz_s[...], up_s[cols, :]).astype(BF)
    stores += store_rows(mover, part_s, slots, order, me)
    wait_all(stores)


def feed_back(dims, turn, ff_w, gp, pieces):
    S, F, r, D, W, H = dims
    L = S * r
    outs = [((L, D), BF), ((L, H), BF)] + slot_shapes(S, turn, (r, D))
    scratch = [
        pltpu.VMEM((D, H), BF),
        pltpu.VMEM((H, D), BF),
        pltpu.VMEM((L, H), BF),
        pltpu.VMEM((L, D), BF),
        pltpu.VMEM((L, H), BF),
        pltpu.VMEM((L, D), BF),
        pltpu.SemaphoreType.DMA((3 * S + F * (H // W) + 4,)),
    ]
    return call(
        partial(feed_back_kernel, dims, slot_order(S, turn)),
        (ff_w, gp, *pieces),
        [any_spec()] * (2 + S),
        outs,
        [hbm_spec()] * len(outs),
        scratch,
        4 * L * D * H,
        2 * (2 * D * H + 3 * L * D + 2 * L * H),
        "feed_back",
    )


def feed_outer_kernel(dims, count, *refs):
    S, F, D, W, H = dims
    ins, (out, *held, down_s, up_s, sems) = refs[: 4 * count], refs[4 * count :]
    me = seq_place()
    mover = Mover(sems)
    loads = [mover.start(a, b) for a, b in zip(ins, held)]
    g_rows, dm_rows = held[:count], held[count : 2 * count]
    b_rows, dz_rows = held[2 * count : 3 * count], held[3 * count :]
    wide = 256
    stores = []
    wait_all(loads[: 2 * count])
    for c in range(D // wide):
        total = None
        cols = slice(c * wide, c * wide + wide)
        for b in range(count):
            part = dot_tn(g_rows[b][...], dm_rows[b][:, cols])
            total = part if total is None else total + part
        down_s[:, cols] = total.astype(BF)
    stores += [
        mover.start(down_s.at[b], out.at[a]) for a, b in down_places(D, H, me, S, F)
    ]
    wait_all(loads[2 * count :])
    for c in range(H // wide):
        total = None
        cols = slice(c * wide, c * wide + wide)
        for b in range(count):
            part = dot_tn(b_rows[b][...], dz_rows[b][:, cols])
            total = part if total is None else total + part
        up_s[:, cols] = total.astype(BF)
        piece = pl.ds(c * wide, wide)
        target = piece
        if in_plane(S, F):
            target = pl.ds(pl.multiple_of((me ^ c) * wide, wide), wide)
        stores.append(mover.start(up_s.at[:, piece], out.at[:, target]))
    wait_all(stores)


def feed_outer(dims, b_rows, dz_rows, g_rows, dm_rows):
    S, F, D, W, H = dims
    count = len(b_rows)
    L = b_rows[0].shape[0]
    operands = (*g_rows, *dm_rows, *b_rows, *dz_rows)
    return call(
        partial(feed_outer_kernel, dims, count),
        operands,
        [any_spec()] * len(operands),
        [((D, 2 * H), BF)],
        [hbm_spec()],
        [pltpu.VMEM(x.shape, BF) for x in operands]
        + [
            pltpu.VMEM((H, D), BF),
            pltpu.VMEM((D, H), BF),
            pltpu.SemaphoreType.DMA((4 * count + F * (H // W) + H // 256,)),
        ],
        4 * count * L * D * H,
        2 * (count * 2 * L * (D + H) + 2 * D * H),
        "feed_outer",
    )[0]


def feed_last_kernel(S, F, *refs):
    came, got, (up_out, down_out, held, sems) = refs[:S], refs[S], refs[S + 1 :]
    me = seq_place()
    core = lax.rem(lax.axis_index("fsdp").astype(jnp.int32), 2)
    mover = Mover(sems)
    loads = [mover.start(a, held.at[j]) for j, a in enumerate(came)]
    R, W = up_out.shape[0], up_out.shape[1] // S
    wait_all(loads)
    for slot in range(S):
        start = pl.multiple_of((me ^ slot) * W, W)
        up_out[:, pl.ds(start, W)] = held[slot, 0:R, :].astype(F32)
    near = lax.rem(me, 2) == core
    for k in range(2):
        rows = slice(k * 2 * R, k * 2 * R + 2 * R)
        here = held[me ^ (2 * core + k), R : 3 * R, :]
        down_out[rows, :] = jnp.where(near, here, got[k]).astype(F32)


def feed_last(S, F, came, got):
    R, W = came[0].shape[0] // 3, came[0].shape[1]
    return call(
        partial(feed_last_kernel, S, F),
        (*came, got),
        [any_spec()] * S + [vmem_spec()],
        [((R, S * W), F32), ((4 * R, W), F32)],
        [vmem_spec()] * 2,
        [pltpu.VMEM((S, 3 * R, W), BF), pltpu.SemaphoreType.DMA((S,))],
        R * W * S,
        R * W * 40,
        "feed_last",
    )


def total_of(refs, rows):
    total = None
    for ref in refs:
        value = ref[0, rows, :].astype(F32)
        total = value if total is None else total + value
    return total


def column_sum(v):
    return jnp.sum(v, axis=0, keepdims=True)


def finish_kernel(turn, *refs):
    if turn:
        refs = refs[1:]
    count = (len(refs) - 6) // 2
    ins, (y_hbm, dm_hbm, stat_out), refs = refs[:count], refs[count : count + 3], refs[count + 3 :]
    held, (y_out, dm_out, sems) = refs[: len(ins)], refs[len(ins) :]
    mover = Mover(sems)
    wait_all([mover.start(a, b) for a, b in zip(ins, held)])
    gains, u_ref, h_ref, dy_ref, *terms = held
    half = dm_out.shape[0] // 2
    stats = [None] * 5
    for part in range(2):
        rows = slice(part * half, part * half + half)
        m = total_of(terms, rows)
        unit, scale = norm_parts(m)
        f = unit * gains[3:4, :]
        h = h_ref[rows, :]
        y = h + f
        y_out[rows, :] = y.astype(BF)
        dy = dy_ref[rows, :].astype(F32)
        dm = norm_back(dy * gains[3:4, :], unit, scale)
        dm_out[rows, :] = dm.astype(BF)
        if part == 1:
            stores = [mover.start(dm_out, dm_hbm), mover.start(y_out, y_hbm.at[turn])]
        second, unused = norm_parts(u_ref[rows, :])
        e = second * gains[1:2, :]
        values = [dy * unit, h * h, y * y, e * e, f * f]
        for index, value in enumerate(values):
            value = column_sum(value)
            stats[index] = value if part == 0 else stats[index] + value
    stat_out[...] = jnp.zeros_like(stat_out)
    for index in range(5):
        stat_out[3 + index : 4 + index, :] = stats[index]
    wait_all(stores)


def finish(turn, B, joined, gains, u, h, dy, terms):
    r, D = u.shape
    outs = [((B, r, D), BF), ((r, D), BF), ((8, D), F32)]
    operands = (gains, u, h, dy, *terms)
    first = [] if joined is None else [joined]
    return call(
        partial(finish_kernel, turn),
        (*first, *operands),
        [hbm_spec()] * len(first) + [any_spec()] * len(operands),
        outs,
        [hbm_spec(), hbm_spec(), vmem_spec()],
        [pltpu.VMEM(x.shape, x.dtype) for x in operands]
        + [pltpu.VMEM((r, D), BF)] * 2
        + [pltpu.SemaphoreType.DMA((len(operands) + 2,))],
        60 * r * D,
        r * D * 20,
        "finish",
        {0: 0} if first else {},
    )


def middle_kernel(*refs):
    count = (len(refs) - 6) // 2
    ins, (dh_out, du_hbm, stat_out), refs = refs[:count], refs[count : count + 3], refs[count + 3 :]
    held, (dh_s, du_out, sems) = refs[: len(ins)], refs[len(ins) :]
    mover = Mover(sems)
    wait_all([mover.start(a, b) for a, b in zip(ins, held)])
    gains, u_ref, h_ref, dy_ref, *terms = held
    r, D = u_ref.shape
    half = r // 2
    stats = [None] * 2
    for part in range(2):
        rows = slice(part * half, part * half + half)
        back = total_of(terms, rows)
        unit, scale = norm_parts(h_ref[rows, :])
        third = column_sum(back * unit)
        dh = dy_ref[rows, :].astype(F32) + norm_back(back * gains[2:3, :], unit, scale)
        dh_s[rows, :] = dh
        unit, scale = norm_parts(u_ref[rows, :])
        second = column_sum(dh * unit)
        du_out[rows, :] = norm_back(dh * gains[1:2, :], unit, scale).astype(BF)
        for index, value in enumerate((second, third)):
            stats[index] = value if part == 0 else stats[index] + value
    stores = [mover.start(du_out, du_hbm), mover.start(dh_s, dh_out)]
    stat_out[...] = jnp.zeros_like(stat_out)
    stat_out[1:2, :] = stats[0]
    stat_out[2:3, :] = stats[1]
    wait_all(stores)


def middle(gains, u, h, dy, terms):
    r, D = u.shape
    outs = [((r, D), F32), ((r, D), BF), ((8, D), F32)]
    operands = (gains, u, h, dy, *terms)
    return call(
        middle_kernel,
        operands,
        [any_spec()] * len(operands),
        outs,
        [hbm_spec(), hbm_spec(), vmem_spec()],
        [pltpu.VMEM(x.shape, x.dtype) for x in operands]
        + [
            pltpu.VMEM((r, D), F32),
            pltpu.VMEM((r, D), BF),
            pltpu.SemaphoreType.DMA((len(operands) + 2,)),
        ],
        60 * r * D,
        r * D * 24,
        "middle",
    )


def last_kernel(turn, *refs):
    if turn:
        refs = refs[1:]
    count = (len(refs) - 3) // 2
    ins, joined, held, (out, sems) = refs[:count], refs[count], refs[count + 1 : -2], refs[-2:]
    mover = Mover(sems)
    wait_all([mover.start(a, b) for a, b in zip(ins, held)])
    gains, x_ref, dh_ref, *terms = held
    r, D = x_ref.shape
    half = r // 2
    for part in range(2):
        rows = slice(part * half, part * half + half)
        back = total_of(terms, rows)
        unit, scale = norm_parts(x_ref[rows, :].astype(F32))
        grad = dh_ref[rows, :] + norm_back(back * gains[0:1, :], unit, scale)
        out[rows, :] = grad.astype(BF)
    mover.start(out, joined.at[turn]).wait()


def last(turn, B, joined, gains, x, dh, terms):
    r, D = x.shape
    operands = (gains, x, dh, *terms)
    first = [] if joined is None else [joined]
    return call(
        partial(last_kernel, turn),
        (*first, *operands),
        [hbm_spec()] * len(first) + [any_spec()] * len(operands),
        [((B, r, D), BF)],
        [hbm_spec()],
        [pltpu.VMEM(x.shape, x.dtype) for x in operands]
        + [pltpu.VMEM((r, D), BF), pltpu.SemaphoreType.DMA((len(operands) + 1,))],
        40 * r * D,
        r * D * 14,
        "last",
        {0: 0} if first else {},
    )[0]


def block_groups(F):
    return [[0, 2, 3, 4], [1, 5, 6, 7]] if F == 8 else [list(range(F))]


def out_grad_kernel(dims, count, *refs):
    S, F, D, W = dims
    groups = block_groups(F)
    ins, outs, refs = refs[: (1 + S) * count], refs[(1 + S) * count :], None
    outs, (*held, sum_s, sems) = outs[: len(groups)], outs[len(groups) :]
    mover = Mover(sems)
    o_rows, dus = held[:count], held[count:]
    loads = [mover.start(a, b) for a, b in zip(ins[:count], o_rows)]
    for b in range(count):
        pieces = ins[count + b * S : count + b * S + S]
        loads += load_rows(mover, pieces, dus[b], seq_place())
    R = D // F
    places = block_places(F)
    stores = []
    wait_all(loads)
    total = None
    for b in range(count):
        part = dot_tn(o_rows[b][...], dus[b][...])
        total = part if total is None else total + part
    sum_s[...] = total.astype(BF)
    for group, out in zip(groups, outs):
        for i, index in enumerate(group):
            row = pl.multiple_of(places[index] // S * R, R)
            col = pl.multiple_of(places[index] % S * W, W)
            stores.append(
                mover.start(
                    sum_s.at[pl.ds(row, R), pl.ds(col, W)], out.at[i, pl.ds(3 * R, R)]
                )
            )
    wait_all(stores)


def out_grad(dims, o_rows, dus):
    S, F, D, W = dims
    count = len(o_rows)
    L = o_rows[0].shape[0]
    groups = block_groups(F)
    operands = (*o_rows, *[piece for du in dus for piece in du])
    return call(
        partial(out_grad_kernel, dims, count),
        operands,
        [any_spec()] * len(operands),
        [((len(group), 4 * (D // F) + EXTRA, W), BF) for group in groups],
        [hbm_spec()] * len(groups),
        [pltpu.VMEM(x.shape, BF) for x in o_rows]
        + [pltpu.VMEM((L, D), BF)] * count
        + [pltpu.VMEM((W, D), BF), pltpu.SemaphoreType.DMA(((1 + S) * count + F,))],
        2 * count * L * D * W,
        2 * (count * L * (D + W) + D * W),
        "out_grad",
    )


def qkv_grad_kernel(dims, count, many, *refs):
    S, F, D, W = dims
    groups = block_groups(F)
    n = len(groups)
    stats, refs = refs[n : n + many], refs[n + many :]
    ins, refs = refs[: 2 * count], refs[2 * count :]
    outs, (*held, sum_s, stat_s, sems) = refs[:n], refs[n:]
    held_stats, held = held[:many], held[many:]
    mover = Mover(sems)
    early = [mover.start(a, b) for a, b in zip(stats, held_stats)]
    loads = [mover.start(a, b) for a, b in zip(ins, held)]
    a_rows, grads = held[:count], held[count:]
    R = D // F
    places = [pl.multiple_of(place * R, R) for place in block_places(F)]
    stores = []
    wait_all(early)
    if F == 8:
        total = held_stats[0][...]
        for other in held_stats[1:]:
            total = total + other[...]
        squares = total[4:8, 0:R]
        for i in range(1, F):
            squares = squares + total[4:8, i * R : i * R + R]
        joined = jnp.concatenate([total[0:4], jnp.concatenate([squares] * F, axis=1)], axis=0)
        stat_s[0:8, 0:D] = joined.astype(BF)
        stat_s[8:16, 0:D] = jnp.zeros_like(total).astype(BF)
        for group, out in zip(groups, outs):
            for i, index in enumerate(group):
                stores.append(
                    mover.start(
                        stat_s.at[:, pl.ds(places[index], R)],
                        out.at[i, pl.ds(4 * R, EXTRA), pl.ds(0, R)],
                    )
                )
    wait_all(loads)
    for t in range(3):
        cols = slice(t * W, t * W + W)
        total = None
        for b in range(count):
            part = dot_tn(a_rows[b][...], grads[b][:, cols])
            total = part if total is None else total + part
        sum_s[:, cols] = total.astype(BF)
        for group, out in zip(groups, outs):
            for i, index in enumerate(group):
                stores.append(
                    mover.start(
                        sum_s.at[pl.ds(places[index], R), pl.ds(t * W, W)],
                        out.at[i, pl.ds(t * R, R)],
                    )
                )
    wait_all(stores)


def qkv_grad(dims, parts, stats, a_rows, grads):
    S, F, D, W = dims
    count = len(a_rows)
    L = a_rows[0].shape[0]
    operands = (*parts, *stats, *a_rows, *grads)
    return pl.pallas_call(
        partial(qkv_grad_kernel, dims, count, len(stats)),
        out_shape=tuple(jax.ShapeDtypeStruct(part.shape, part.dtype) for part in parts),
        in_specs=[hbm_spec()] * len(parts) + [any_spec()] * (len(operands) - len(parts)),
        out_specs=tuple([hbm_spec()] * len(parts)),
        input_output_aliases={i: i for i in range(len(parts))},
        scratch_shapes=[pltpu.VMEM(x.shape, x.dtype) for x in (*stats, *a_rows, *grads)]
        + [
            pltpu.VMEM((D, 3 * W), BF),
            pltpu.VMEM((EXTRA, D), BF),
            pltpu.SemaphoreType.DMA((2 * count + len(stats) + 4 * F,)),
        ],
        compiler_params=pltpu.CompilerParams(vmem_limit_bytes=VMEM_LIMIT),
        name="qkv_grad",
    )(*operands)


def deal_qkv_kernel(F, *refs):
    stacks, (one, two, held, sems) = refs[:F], refs[F:]
    me = seq_place()
    rows, cols = one.shape[1], one.shape[2]
    mover = Mover(sems)
    outs = (one, two)
    loads = []
    for i in range(F):
        for slot in (1, 2):
            start = pl.multiple_of(block_at(me, slot) * cols, cols)
            source = stacks[i].at[0, pl.ds(0, rows), pl.ds(start, cols)]
            loads.append(mover.start(source, held.at[slot - 1, i]))
    wait_all(loads)
    wait_all([mover.start(held.at[j], outs[j]) for j in range(2)])


def deal_qkv(R, W, stacks):
    F = len(stacks)
    return call(
        partial(deal_qkv_kernel, F),
        tuple(stacks),
        [any_spec()] * F,
        [((F, R, W), BF)] * 2,
        [hbm_spec()] * 2,
        [pltpu.VMEM((2, F, R, W), BF), pltpu.SemaphoreType.DMA((2 * F + 2,))],
        0,
        8 * F * R * W,
        "deal_qkv",
    )


def pair_sum_kernel(mine, got, *refs):
    outs, (mine_s, got_s, sum_s, sems) = refs[:4], refs[4:]
    mover = Mover(sems)
    loads = []
    for i in range(4):
        loads.append((mover.start(mine.at[i], mine_s.at[i]), mover.start(got.at[i], got_s.at[i])))
    stores = []
    for i in (3, 2, 1, 0):
        wait_all(loads[i])
        sum_s[i] = (mine_s[i].astype(F32) + got_s[i].astype(F32)).astype(BF)
        stores.append(mover.start(sum_s.at[i], outs[i]))
    wait_all(stores)


def pair_sum(mine, got):
    shape = mine.shape[1:]
    return call(
        pair_sum_kernel,
        (mine, got),
        [any_spec()] * 2,
        [(shape, BF)] * 4,
        [hbm_spec()] * 4,
        [pltpu.VMEM(mine.shape, BF)] * 3 + [pltpu.SemaphoreType.DMA((12,))],
        mine.size,
        6 * mine.size,
        "pair_sum",
    )


def last_sum_kernel(S, R, *refs):
    ins, (*moved, out_tile, stat_out), refs = refs[:4], refs[4:9], refs[9:]
    held, (sum_s, sems) = refs[:4], refs[4:]
    mover = Mover(sems)
    wait_all([mover.start(a, b) for a, b in zip(ins, held)])
    total = held[0][...].astype(F32)
    for ref in held[1:]:
        total = total + ref[...].astype(F32)
    sum_s[...] = total.astype(BF)
    stat_out[...] = total[4 * R : 4 * R + 8, 0 : stat_out.shape[1]]
    me = seq_place()
    stores = [mover.start(sum_s.at[pl.ds(3 * R, R)], out_tile)]
    for j in range(3):
        owner = me ^ j
        start = pl.multiple_of(lax.div(3 * owner + block_at(owner, j), S) * R, R)
        stores.append(mover.start(sum_s.at[pl.ds(start, R)], moved[j].at[pl.ds(0, R)]))
        stores.append(
            mover.start(sum_s.at[pl.ds(4 * R, EXTRA)], moved[j].at[pl.ds(R, EXTRA)])
        )
    wait_all(stores)


def last_sum(S, R, terms):
    rows, W = terms[0].shape
    return call(
        partial(last_sum_kernel, S, R),
        tuple(terms),
        [any_spec()] * 4,
        [((R + EXTRA, W), BF)] * 3 + [((R, W), BF), ((8, R), F32)],
        [hbm_spec()] * 4 + [vmem_spec()],
        [pltpu.VMEM((rows, W), BF)] * 5 + [pltpu.SemaphoreType.DMA((11,))],
        4 * rows * W,
        10 * rows * W,
        "last_sum",
    )


def flip(bits, size):
    return [(i, i ^ bits) for i in range(size)]


def add_low(*terms):
    total = terms[0].astype(F32)
    for term in terms[1:]:
        total = total + term.astype(F32)
    return total.astype(BF)


def gather_slots(own, S, me, turn):
    if S != 4:
        full = lax.all_gather(own, "seq")
        return [
            lax.dynamic_index_in_dim(full, me ^ slot, 0, keepdims=False) for slot in range(S)
        ]
    far = lax.ppermute(own, "seq", flip(3, S))
    return [own] + [lax.ppermute(own, "seq", flip(j, S)) for j in (1, 2)] + [far]


def slot_order(S, turn):
    return [[slot] for slot in range(S)]


def slot_shapes(S, turn, shape):
    return [((len(group), *shape), BF) for group in slot_order(S, turn)]


def scatter_slots(groups, S, me, turn):
    if S != 4:
        order = jnp.take(jnp.concatenate(groups), me ^ jnp.arange(S), axis=0)
        return [lax.psum_scatter(order, "seq", scatter_dimension=0, tiled=True)]
    return [groups[0]] + [lax.ppermute(groups[j], "seq", flip(j, S)) for j in (3, 1, 2)]


def swap_slots(pieces, S):
    return [pieces[0]] + [lax.ppermute(pieces[j], "seq", flip(j, S)) for j in range(1, S)]


def sum_everywhere(v, S, F):
    if S != 4 or F != 8:
        return lax.psum(v, ("seq", "fsdp"))
    v = v + lax.ppermute(v, "fsdp", flip(1, F))
    v = v + lax.ppermute(v, "seq", flip(1, S))
    v = v + lax.ppermute(v, "seq", flip(2, S))
    v = v + lax.ppermute(v, "fsdp", flip(2, F))
    return v + lax.ppermute(v, "fsdp", flip(4, F))


def gather_blocks(block, F, early=()):
    if F != 8:
        return [lax.all_gather(block, "fsdp")]
    near = lax.ppermute(block, "fsdp", flip(1, F))
    far = [lax.ppermute(block, "fsdp", flip(j, F)) for j in (2, 4, 6)]
    far = after(far, near, *early)
    rest = [lax.ppermute(piece, "fsdp", flip(1, F)) for piece in far]
    return [piece[None] for piece in (block, near, *far, *rest)]


def after(value, *others):
    return lax.optimization_barrier((value, others))[0]


def blocks_in(blocks, S, me):
    moved = []
    for j in range(3):
        pairs = [(s, (3 * s + j) % S) for s in range(S)]
        moved.append(lax.ppermute(blocks[j], "seq", pairs))
    stack = jnp.stack(moved)
    return [
        lax.dynamic_index_in_dim(stack, (me + S * t) % 3, 0, keepdims=False) for t in range(3)
    ]


def blocks_out_pairs(S, j):
    return [((3 * s + j) % S, s) for s in range(S)]


def blocks_out(stack, S, me):
    moved = []
    for j in range(3):
        t = ((j - me) * (S % 3)) % 3
        piece = lax.dynamic_index_in_dim(stack, t, 0, keepdims=False)
        moved.append(lax.ppermute(piece, "seq", blocks_out_pairs(S, j)))
    return jnp.concatenate(moved, axis=1)


def turn_pairs(S, F):
    each = F // S
    return [
        (s * F + f, (f // each) * F + (f % each) * S + s) for s in range(S) for f in range(F)
    ]


def shards(tokens, cotangent, prefix, qkv_weight, out_weight, up_weight, down_weight, norm_gains):
    S, F = lax.axis_size("seq"), lax.axis_size("fsdp")
    B, r, D = tokens.shape
    heads = D // HEAD // S
    W = D // S
    R = D // F
    H = up_weight.shape[1]
    tiles = H // W
    me = seq_place()
    place = lax.axis_index("fsdp").astype(jnp.int32)
    pairs = turn_pairs(S, F)

    down_late, out_late = down_weight, out_weight
    axes = ("seq", "fsdp")
    if in_plane(S, F):
        gain_rows = jnp.pad(norm_gains, ((0, EXTRA - 4), (0, 3 * W - R)))
        first_block = jnp.concatenate([qkv_weight, gain_rows])
        near_block = lax.ppermute(first_block, "fsdp", flip(1, F))
        far = [lax.ppermute(first_block, "fsdp", flip(j, F)) for j in (2, 4, 6)]
        core = place % 2
        other = lax.ppermute(down_late, "fsdp", flip(1, F))
        halves = jnp.concatenate([down_late, other]).reshape(4, 2 * R, W)
        sent = []
        for j in range(S):
            target = me ^ j
            index = jnp.where(target // 2 == core, 0, 2) + target % 2
            piece = lax.dynamic_index_in_dim(halves, index, 0, keepdims=False)
            up_tile = lax.dynamic_slice_in_dim(up_weight, target * W, W, 1)
            sent.append(jnp.concatenate([up_tile, piece, out_late]))
        came, far, near_block = lax.optimization_barrier((swap_slots(sent, S), far, near_block))
        ups = [message[:R] for message in came]
        out_tiles = [message[3 * R :] for message in came]
        near = (me % 2) ^ core == 0
        pieces = [
            jnp.where(near, came[2 * i][R : 3 * R], came[2 * i + 1][R : 3 * R])
            for i in range(2)
        ]
        downs = [piece[t * R : t * R + R] for piece in pieces for t in range(2)]
    else:
        ups = [up_weight]
        down_mine = lax.ppermute(down_late, axes, pairs)
        downs = [down_mine[i * R : i * R + R] for i in range(tiles)]
        out_tiles = gather_slots(out_late, S, me, 0)
    ff_mine = jnp.concatenate([*ups, *downs, *out_tiles], axis=1)
    if in_plane(S, F):
        rest = [lax.ppermute(piece, "fsdp", flip(1, F)) for piece in far]
        stacks = [piece[None] for piece in (first_block, near_block, *far, *rest)]
        one, two = deal_qkv(R, W, stacks)
        one = lax.ppermute(one, "seq", flip(1, S))
        two = lax.ppermute(two, "seq", flip(2, S))
        all_x = [gather_slots(tokens[:1], S, me, 0)]
        all_x += [gather_slots(after(tokens[b : b + 1], one, two), S, me, 0) for b in range(1, B)]
        stacks = [*stacks, one, two]
    else:
        blocks = [qkv_weight[:, j * W : j * W + W] for j in range(3)]
        all_x = [gather_slots(tokens[b : b + 1], S, me, 0) for b in range(B)]
        stacks = gather_blocks(jnp.concatenate(blocks_in(blocks, S, me)), F)
    if in_plane(S, F):
        pass
    ff_full = lax.all_gather(ff_mine, "fsdp", axis=0, tiled=True)
    gains = None
    if F != 8:
        gains = lax.all_gather(norm_gains, "fsdp", axis=1, tiled=True).astype(F32)
        gains = jnp.pad(gains, ((0, 4), (0, 0)))
    att_dims = (S, F, r, D, heads)
    ff_dims = (S, F, r, D, W, H)
    a_all, qkv_all, p_all, os, os_own = [], [], [], [], []
    for b in range(B):
        a, qkv, o, p, gains_full = attend(att_dims, b, prefix, gains, stacks, all_x[b])
        a_all.append(a)
        qkv_all.append(qkv)
        p_all.append(p)
        os_own.append(o)
        os.append(gather_slots(o, S, me, b))
    gains = gains_full
    b_all, u_own, h_own, g_all, gp_all, m_terms = [], [], [], [], [], []
    for b in range(B):
        res = feed(ff_dims, b, gains, ff_full, all_x[b], os[b])
        b_all.append(res[0])
        u_own.append(res[1])
        h_own.append(res[2])
        g_all.append(res[3])
        gp_all.append(res[4])
        m_terms.append(scatter_slots(list(res[5:]), S, me, b))
    y, stats, dms = None, [], []
    for b in range(B):
        y, dm, stat = finish(b, B, y, gains, u_own[b], h_own[b], cotangent[b], m_terms[b])
        stats.append(stat)
        dms.append(gather_slots(dm, S, me, b))
    dm_all, dz_all, h_terms = [], [], []
    for b in range(B):
        res = feed_back(ff_dims, b, ff_full, gp_all[b], dms[b])
        dm_all.append(res[0])
        dz_all.append(res[1])
        h_terms.append(scatter_slots(list(res[2:]), S, me, b))
    dhs, dus = [], []
    for b in range(B):
        dh, du, stat = middle(gains, u_own[b], h_own[b], cotangent[b], h_terms[b])
        dhs.append(dh)
        dus.append(gather_slots(du, S, me, b))
        stats.append(stat)
    dm_all = after(dm_all, h_terms[0])
    ff_part = feed_outer((S, F, D, W, H), b_all, dz_all, g_all, dm_all)
    ff_sum = lax.psum_scatter(ff_part, "fsdp", scatter_dimension=0, tiled=True)
    back_pairs = [(b, a) for a, b in pairs]
    if not in_plane(S, F):
        down_sum = jnp.concatenate(
            [ff_sum[:, H + i * W : H + i * W + W] for i in range(tiles)], axis=0
        )
        down_grad = lax.ppermute(down_sum, axes, back_pairs).astype(F32)
        up_grad = ff_sum[:, :H].astype(F32)
    dqkvs, x_terms = [], []
    for b in range(B):
        res = attend_back(
            att_dims, b, gains, ff_full, stacks, a_all[b], qkv_all[b], p_all[b], dus[b]
        )
        dqkvs.append(res[0])
        stats.append(res[1])
        x_terms.append(scatter_slots(list(res[2:]), S, me, b))
    grad_dims = (S, F, D, W)
    parts = after(out_grad(grad_dims, os_own, dus), dqkvs)
    parts = after(parts, x_terms[0])
    parts = qkv_grad(grad_dims, parts, stats, a_all, dqkvs)
    if F == 8 and S == 4:
        kept = pair_sum(parts[0], lax.ppermute(parts[1], "fsdp", flip(1, F)))
        ff_sum = after(ff_sum, kept)
        got = [lax.ppermute(kept[j], "fsdp", flip(2 * j, F)) for j in (3, 2, 1)]
        pieces = [ff_sum[:, H + i * W : H + i * W + W] for i in range(4)]
        sent = [
            jnp.concatenate([ff_sum[:, j * W : j * W + W], *pieces[j // 2 * 2 : j // 2 * 2 + 2]])
            for j in range(S)
        ]
        came = swap_slots(sent, S)
        got = after(got, came)
        whole = jnp.stack(came)[:, R:]
        away = jnp.stack(
            [
                lax.dynamic_index_in_dim(whole, me ^ (2 * (1 - place % 2) + k), 0, keepdims=False)
                for k in range(2)
            ]
        )
        up_grad, down_grad = feed_last(S, F, came, lax.ppermute(away, "fsdp", flip(1, F)))
        *moved, out_tile, stat = last_sum(S, R, [kept[0], *got])
        moved[1:] = [lax.ppermute(moved[j], "seq", flip(j, S)) for j in (1, 2)]
        missed = lax.ppermute(stat, "seq", flip(3, S))
        for piece in moved:
            missed = missed + piece[R : R + 8, :R].astype(F32)
        odd = me % 2 == 1
        ends = (moved[0][:R], moved[2][:R])
        qkv_own = jnp.concatenate(
            [jnp.where(odd, ends[1], ends[0]), moved[1][:R], jnp.where(odd, ends[0], ends[1])],
            axis=1,
        )
        gains_grad, squares = missed[:4], jnp.sum(missed[4:], axis=1)
    else:
        rest = lax.psum_scatter(parts[0], "fsdp", scatter_dimension=0, tiled=False)
        qkv_own = blocks_out(jnp.stack([rest[t * R : t * R + R] for t in range(3)]), S, me)
        out_tile = rest[3 * R : 4 * R]
        totals = lax.psum(sum(stats), ("seq", "fsdp"))
        gains_grad = lax.dynamic_slice_in_dim(totals[:4], place * R, R, 1)
        squares = jnp.sum(totals[4:], axis=1)
    input_grad = None
    for b in range(B):
        input_grad = last(b, B, input_grad, gains, tokens[b], dhs[b], x_terms[b])

    out_own = lax.ppermute(out_tile, ("seq", "fsdp"), back_pairs)
    entries = B * r * D * S * F
    stream_rms = jnp.sqrt(squares / entries)
    return (
        y,
        input_grad,
        qkv_own.astype(F32),
        out_own.astype(F32),
        up_grad,
        down_grad,
        gains_grad,
        stream_rms,
    )


def solution(mesh):
    in_specs = (
        P("fsdp", "seq", None),
        P("fsdp", "seq", None),
        P("fsdp"),
        P("fsdp", "seq"),
        P("fsdp", "seq"),
        P("fsdp", "seq"),
        P("fsdp", "seq"),
        P(None, "fsdp"),
    )
    out_specs = (
        P("fsdp", "seq", None),
        P("fsdp", "seq", None),
        P("fsdp", "seq"),
        P("fsdp", "seq"),
        P("fsdp", "seq"),
        P("fsdp", "seq"),
        P(None, "fsdp"),
        P(),
    )
    return jax.shard_map(shards, mesh=mesh, in_specs=in_specs, out_specs=out_specs, check_vma=False)
```

```python
import math
from functools import partial

import jax
import jax.numpy as jnp
from jax import lax
from jax.experimental import pallas as pl
from jax.experimental.pallas import tpu as pltpu
from jax.sharding import PartitionSpec as P

HEAD = 64
NORM_EPSILON = 1e-05
MASKED_SCORE = -1e30
VMEM_LIMIT = 48 * 1024 * 1024
BF = jnp.bfloat16
F32 = jnp.float32
BLOCK_ORDER = (0, 1, 2, 4, 6, 3, 5, 7)
EXTRA = 16
COST = 0.001


def dot_nn(a, b):
    return lax.dot_general(a, b, (((1,), (0,)), ((), ())), preferred_element_type=F32)


def dot_nt(a, b):
    return lax.dot_general(a, b, (((1,), (1,)), ((), ())), preferred_element_type=F32)


def dot_tn(a, b):
    return lax.dot_general(a, b, (((0,), (0,)), ((), ())), preferred_element_type=F32)


def norm_parts(v):
    centre = jnp.mean(v, axis=-1, keepdims=True)
    shifted = v - centre
    spread = jnp.mean(shifted * shifted, axis=-1, keepdims=True)
    scale = lax.rsqrt(spread + NORM_EPSILON)
    return shifted * scale, scale


def norm_back(grad_unit, unit, scale):
    first = jnp.mean(grad_unit, axis=-1, keepdims=True)
    second = jnp.mean(grad_unit * unit, axis=-1, keepdims=True)
    return scale * (grad_unit - first - unit * second)


def seq_place():
    return lax.axis_index("seq").astype(jnp.int32)


def block_places(F):
    if F != 8:
        return [jnp.int32(i) for i in range(F)]
    place = lax.axis_index("fsdp").astype(jnp.int32)
    return [place ^ i for i in BLOCK_ORDER]


class Mover:
    def __init__(self, sems):
        self.sems = sems
        self.used = 0

    def start(self, src, dst):
        copy = pltpu.make_async_copy(src, dst, self.sems.at[self.used])
        self.used += 1
        copy.start()
        return copy


def wait_all(copies):
    for copy in copies:
        copy.wait()


def load_rows(mover, pieces, target, me):
    r = pieces[0].shape[0]
    copies = []
    for slot, piece in enumerate(pieces):
        start = pl.multiple_of((me ^ slot) * r, r)
        copies.append(mover.start(piece, target.at[pl.ds(start, r)]))
    return copies


def store_rows(mover, source, outs, order, me):
    r = outs[0].shape[1]
    copies = []
    for group, out in zip(order, outs):
        for i, slot in enumerate(group):
            start = pl.multiple_of((me ^ slot) * r, r)
            copies.append(mover.start(source.at[pl.ds(start, r)], out.at[i]))
    return copies


def in_plane(S, F):
    return S == 4 and F == 8


def block_at(s, slot):
    if slot == 1:
        return jnp.int32(1)
    odd = lax.rem(s, 2)
    return 2 * odd if slot == 0 else 2 - 2 * odd


def load_qkv(mover, weights, target, me, S, F):
    places, copies = block_places(F), []
    rows, cols = target.shape[0] // F, target.shape[1] // 3
    if in_plane(S, F):
        stacks, moved = weights[:F], weights[F:]
        for slot in range(3):
            sender = me ^ slot
            at = block_at(sender, slot)
            part = lax.div(3 * sender + at, S)
            col = pl.ds(pl.multiple_of(part * cols, cols), cols)
            from_col = pl.ds(pl.multiple_of(at * cols, cols), cols)
            for i in range(F):
                row = pl.ds(pl.multiple_of(places[i] * rows, rows), rows)
                if slot == 0:
                    source = stacks[i].at[0, pl.ds(0, rows), from_col]
                else:
                    source = moved[slot - 1].at[i]
                copies.append(mover.start(source, target.at[row, col]))
        return copies
    stack = weights[0]
    for i in range(F):
        row = pl.ds(pl.multiple_of(places[i] * rows, rows), rows)
        for t in range(3):
            copies.append(
                mover.start(
                    stack.at[i, pl.ds(t * rows, rows)], target.at[row, pl.ds(t * cols, cols)]
                )
            )
    return copies


def load_gains(mover, stacks, target, F):
    places, copies = block_places(F), []
    width = target.shape[1] // F
    for i, stack in enumerate(stacks[:F]):
        start = pl.multiple_of(places[i] * width, width)
        last = stack.shape[1] - EXTRA
        copies.append(
            mover.start(
                stack.at[0, pl.ds(last, EXTRA), pl.ds(0, width)],
                target.at[:, pl.ds(start, width)],
            )
        )
    return copies


def any_spec():
    return pl.BlockSpec(memory_space=pl.ANY)


def hbm_spec():
    return pl.BlockSpec(memory_space=pltpu.HBM)


def smem_spec():
    return pl.BlockSpec(memory_space=pltpu.SMEM)


def vmem_spec():
    return pl.BlockSpec(memory_space=pltpu.VMEM)


def call(body, operands, in_specs, outs, out_specs, scratch, flops, bytes_accessed, name, aliases={}, limit=VMEM_LIMIT):
    return pl.pallas_call(
        body,
        out_shape=tuple(jax.ShapeDtypeStruct(shape, dtype) for shape, dtype in outs),
        in_specs=in_specs,
        out_specs=tuple(out_specs),
        scratch_shapes=scratch,
        input_output_aliases=aliases,
        compiler_params=pltpu.CompilerParams(vmem_limit_bytes=limit),
        cost_estimate=pl.CostEstimate(
            flops=int(flops * COST), bytes_accessed=int(bytes_accessed * COST), transcendentals=0
        ),
        name=name,
    )(*operands)


def attend_kernel(dims, count, turn, packed, prefix, *refs):
    S, F, r, D, heads = dims
    L, W = S * r, heads * HEAD
    if packed:
        gains_in = None
    else:
        gains_in, refs = refs[0], refs[1:]
    weights, pieces, refs = refs[:count], refs[count : count + S], refs[count + S :]
    a_out, qkv_out, o_out, p_out, gains_out, refs = *refs[:5], refs[5:]
    x_s, w_s, a_s, qkv_s, o_s, p_s, bias_s, raw_s, sems = refs
    me, limit_len = seq_place(), prefix[turn]
    mover = Mover(sems)
    gain_loads = load_gains(mover, weights, raw_s, F) if packed else []
    loads = load_rows(mover, [piece.at[0] for piece in pieces], x_s, me)
    weight_loads = load_qkv(mover, weights, w_s, me, S, F)
    tile = 128
    limit = L // 2
    for i in range(L // tile):
        shape = (tile, max((i + 1) * tile, limit))
        rows = i * tile + lax.broadcasted_iota(jnp.int32, shape, 0)
        cols = lax.broadcasted_iota(jnp.int32, shape, 1)
        seen = (cols <= rows) | (cols < limit_len)
        bias_s[i * tile : i * tile + tile, : shape[1]] = jnp.where(seen, 0.0, MASKED_SCORE)
    wait_all(gain_loads)
    gains_out[...] = raw_s[0:8, :].astype(F32) if packed else gains_in[...]
    wait_all(loads)
    for i in range(L // tile):
        rows = slice(i * tile, i * tile + tile)
        unit, scale = norm_parts(x_s[rows, :].astype(F32))
        a_s[rows, :] = (unit * gains_out[0:1, :]).astype(BF)
    stores = [mover.start(a_s, a_out)]
    wait_all(weight_loads)
    for c in range(3):
        cols = slice(c * W, c * W + W)
        qkv_s[:, cols] = dot_nn(a_s[...], w_s[:, cols]).astype(BF)
    stores.append(mover.start(qkv_s, qkv_out))
    lane = lax.broadcasted_iota(jnp.int32, (1, 128), 1)
    for pair in range(heads // 2):
        q2 = qkv_s[:, pair * 128 : pair * 128 + 128] * BF(HEAD**-0.5)
        k2 = qkv_s[:, W + pair * 128 : W + pair * 128 + 128]
        v2 = qkv_s[:, 2 * W + pair * 128 : 2 * W + pair * 128 + 128]
        keys, values = [], []
        for side in range(2):
            mine = (lane >= 64) if side else (lane < 64)
            keys.append(jnp.where(mine, k2, BF(0)))
            values.append(jnp.where(mine, v2, BF(0)))
        for i in range(L // tile):
            rows = slice(i * tile, i * tile + tile)
            span = max((i + 1) * tile, limit)
            total = None
            for side in range(2):
                scores = dot_nt(q2[rows], keys[side][:span]) + bias_s[rows, :span]
                top = jnp.max(scores, axis=-1, keepdims=True)
                weights_here = jnp.exp(scores - top)
                share = 1.0 / jnp.sum(weights_here, axis=-1, keepdims=True)
                probs = (weights_here * share).astype(BF)
                p_s[2 * pair + side, rows, :span] = probs
                part = dot_nn(probs, values[side][:span])
                total = part if total is None else total + part
            o_s[rows, pair * 128 : pair * 128 + 128] = total.astype(BF)
        for side in range(2):
            stores.append(mover.start(p_s.at[2 * pair + side], p_out.at[2 * pair + side]))
    stores.append(mover.start(o_s, o_out))
    wait_all(stores)


def attend(dims, turn, prefix, gains, weights, pieces):
    S, F, r, D, heads = dims
    L, W = S * r, heads * HEAD
    outs = [((L, D), BF), ((L, 3 * W), BF), ((L, W), BF), ((heads, L, L), BF), ((8, D), F32)]
    scratch = [
        pltpu.VMEM((L, D), BF),
        pltpu.VMEM((D, 3 * W), BF),
        pltpu.VMEM((L, D), BF),
        pltpu.VMEM((L, 3 * W), BF),
        pltpu.VMEM((L, W), BF),
        pltpu.VMEM((heads, L, L), BF),
        pltpu.VMEM((L, L), F32),
        pltpu.VMEM((EXTRA, D), BF),
        pltpu.SemaphoreType.DMA((S + 4 * F + heads + 3,)),
    ]
    flops = 2 * L * D * 3 * W + 4 * heads * L * L * HEAD * 4
    size = 2 * (2 * L * D + 3 * D * W + 4 * L * W + heads * L * L)
    packed = gains is None
    extra = [] if packed else [gains]
    return call(
        partial(attend_kernel, dims, len(weights), turn, packed),
        (prefix, *extra, *weights, *pieces),
        [smem_spec()]
        + [vmem_spec()] * len(extra)
        + [any_spec()] * (len(weights) + len(pieces)),
        outs,
        [hbm_spec()] * 4 + [vmem_spec()],
        scratch,
        flops,
        size,
        "attend",
        limit=56 * 1024 * 1024,
    )


def attend_back_kernel(dims, count, order, gains_in, out_w, *refs):
    S, F, r, D, heads = dims
    n = len(order)
    L, W = S * r, heads * HEAD
    weights, refs = refs[:count], refs[count:]
    a_in, qkv, probs_in, pieces, refs = *refs[:3], refs[3 : 3 + S], refs[3 + S :]
    grad_out, stat_out, slots, refs = *refs[:2], refs[2 : 2 + n], refs[2 + n :]
    w_s, qkv_s, p_s, du_s, do_s, d_s, grad_s, part_s, a_s, out_s, gains, sems = refs
    me = seq_place()
    mover = Mover(sems)
    own = pl.ds(pl.multiple_of(me * W, W), W)
    loads = load_out(mover, out_w, out_s, own, me, S) + load_rows(mover, pieces, du_s, me)
    loads.append(mover.start(qkv, qkv_s))
    prob_loads = [mover.start(probs_in.at[h], p_s.at[h]) for h in range(heads)]
    late_loads = load_qkv(mover, weights, w_s, me, S, F)
    late_loads.append(mover.start(a_in, a_s))
    late_loads.append(mover.start(gains_in, gains))
    tile = 128
    limit = L // 2
    wait_all(loads)
    do_s[...] = dot_nt(du_s[...], out_s[...]).astype(BF)
    lane = lax.broadcasted_iota(jnp.int32, (1, 128), 1)
    for pair in range(heads // 2):
        cols = slice(pair * 128, pair * 128 + 128)
        q2 = qkv_s[:, cols] * BF(HEAD**-0.5)
        k2 = qkv_s[:, W + pair * 128 : W + pair * 128 + 128] * BF(HEAD**-0.5)
        v2 = qkv_s[:, 2 * W + pair * 128 : 2 * W + pair * 128 + 128]
        do2 = do_s[:, cols]
        queries, keys, values, grads = [], [], [], []
        for side in range(2):
            mine = (lane >= 64) if side else (lane < 64)
            queries.append(jnp.where(mine, q2, BF(0)))
            keys.append(jnp.where(mine, k2, BF(0)))
            values.append(jnp.where(mine, v2, BF(0)))
            grads.append(jnp.where(mine, do2, BF(0)))
            prob_loads[2 * pair + side].wait()
        for i in range(L // tile):
            rows = slice(i * tile, i * tile + tile)
            span = max((i + 1) * tile, limit)
            total = None
            for side in range(2):
                probs = p_s[2 * pair + side, rows, :span].astype(F32)
                grad_probs = dot_nt(do2[rows], values[side][:span])
                delta = jnp.sum(probs * grad_probs, axis=-1, keepdims=True)
                grad_scores = (probs * (grad_probs - delta)).astype(BF)
                d_s[side, rows, :span] = grad_scores
                part = dot_nn(grad_scores, keys[side][:span])
                total = part if total is None else total + part
            grad_s[rows, cols] = total.astype(BF)
        for j in range(L // tile):
            columns = slice(j * tile, j * tile + tile)
            low = 0 if (j * tile) < limit else j * tile
            total_k, total_v = None, None
            for side in range(2):
                part = dot_tn(d_s[side, low:, columns], queries[side][low:])
                total_k = part if total_k is None else total_k + part
                part = dot_tn(p_s[2 * pair + side, low:, columns], grads[side][low:])
                total_v = part if total_v is None else total_v + part
            grad_s[columns, W + pair * 128 : W + pair * 128 + 128] = total_k.astype(BF)
            grad_s[columns, 2 * W + pair * 128 : 2 * W + pair * 128 + 128] = total_v.astype(BF)
    stores = [mover.start(grad_s, grad_out)]
    wait_all(late_loads)
    wide = 256
    stat_out[...] = jnp.zeros_like(stat_out)

    for c in range(D // wide):
        cols = slice(c * wide, c * wide + wide)
        part = dot_nt(grad_s[...], w_s[cols, :])
        part_s[:, cols] = part.astype(BF)
        stat_out[0:1, cols] = column_sum(part * a_s[:, cols].astype(F32)) / gains[0:1, cols]
    stores += store_rows(mover, part_s, slots, order, me)
    wait_all(stores)


def attend_back(dims, turn, gains, out_w, weights, a, qkv, probs, pieces):
    S, F, r, D, heads = dims
    L, W = S * r, heads * HEAD
    outs = [((L, 3 * W), BF), ((8, D), F32)] + slot_shapes(S, turn, (r, D))
    blocks = 3 * F
    scratch = [
        pltpu.VMEM((D, 3 * W), BF),
        pltpu.VMEM((L, 3 * W), BF),
        pltpu.VMEM((heads, L, L), BF),
        pltpu.VMEM((L, D), BF),
        pltpu.VMEM((L, W), BF),
        pltpu.VMEM((2, L, L), BF),
        pltpu.VMEM((L, 3 * W), BF),
        pltpu.VMEM((L, D), BF),
        pltpu.VMEM((L, D), BF),
        pltpu.VMEM((W, D), BF),
        pltpu.VMEM((8, D), F32),
        pltpu.SemaphoreType.DMA((3 * S + heads + 5 + blocks,)),
    ]
    flops = 2 * L * D * 4 * W + 8 * heads * L * L * HEAD * 4
    size = 2 * (2 * L * D + 3 * D * W + 7 * L * W + heads * L * L)
    return call(
        partial(attend_back_kernel, dims, len(weights), slot_order(S, turn)),
        (gains, out_w, *weights, a, qkv, probs, *pieces),
        [any_spec()] * 2
        + [any_spec()] * (3 + len(weights) + len(pieces)),
        outs,
        [hbm_spec(), vmem_spec()] + [hbm_spec()] * (len(outs) - 2),
        scratch,
        flops,
        size,
        "attend_back",
    )


def load_out(mover, ff_w, target, rows, me, S):
    D = target.shape[1]
    W, base = D // S, ff_w.shape[1] - D
    copies = []
    for slot in range(S):
        start = pl.multiple_of((me ^ slot) * W, W)
        copies.append(
            mover.start(
                ff_w.at[rows, pl.ds(base + slot * W, W)], target.at[:, pl.ds(start, W)]
            )
        )
    return copies


def load_up(mover, ff_w, up_s, me, S, F):
    H = up_s.shape[1]
    if not in_plane(S, F):
        return [mover.start(ff_w.at[:, pl.ds(0, H)], up_s)]
    W, copies = H // S, []
    for slot in range(S):
        start = pl.multiple_of((me ^ slot) * W, W)
        copies.append(
            mover.start(ff_w.at[:, pl.ds(slot * W, W)], up_s.at[:, pl.ds(start, W)])
        )
    return copies


def down_places(D, H, me, S, F):
    W, R = D // S, D // F
    if in_plane(S, F):
        for f in range(F):
            for col in range(2):
                part = col ^ lax.div(me, 2)
                for t in range(2):
                    start = pl.multiple_of(H + (2 * part + t) * W, W)
                    yield (
                        (pl.ds(f * R, R), pl.ds(start, W)),
                        (pl.ds(f // 2 * 2 * R + t * R, R), pl.ds((f % 2 + 2 * col) * W, W)),
                    )
        return
    for f in range(F):
        for i in range(H // W):
            yield (
                (pl.ds(f * R, R), pl.ds(H + i * W, W)),
                (pl.ds(f // S * (R * (H // W)) + i * R, R), pl.ds(f % S * W, W)),
            )


def load_down(mover, ff_w, down_s, me, S, F):
    H, D = down_s.shape
    return [mover.start(ff_w.at[a], down_s.at[b]) for a, b in down_places(D, H, me, S, F)]


def feed_kernel(dims, order, turn, gains_in, ff_w, *refs):
    S, F, r, D, W, H = dims
    L, n = S * r, len(order)
    xs, os, refs = refs[:S], refs[S : 2 * S], refs[2 * S :]
    b_out, u_own, h_own, g_out, gp_out, slots, refs = *refs[:5], refs[5 : 5 + n], refs[5 + n :]
    x_s, o_s, out_s, u_s, h_s, up_s, down_s, b_s, g_s, gp_s, m_s, gains, sems = refs
    me = seq_place()
    mover = Mover(sems)
    loads = [mover.start(gains_in, gains)]
    for slot in range(S):
        start = pl.multiple_of((me ^ slot) * W, W)
        loads.append(mover.start(os[slot], o_s.at[:, pl.ds(start, W)]))
    loads += load_out(mover, ff_w, out_s, pl.ds(0, D), me, S)
    loads += load_rows(mover, [x.at[0] for x in xs], x_s, me)
    up_loads = load_up(mover, ff_w, up_s, me, S, F)
    down_loads = load_down(mover, ff_w, down_s, me, S, F)
    wide, tall = 256, 256
    wait_all(loads)
    for i in range(L // tall):
        rows = slice(i * tall, i * tall + tall)
        for c in range(D // wide):
            cols = slice(c * wide, c * wide + wide)
            u_s[rows, cols] = dot_nn(o_s[rows, :], out_s[:, cols])
        unit, scale = norm_parts(u_s[rows, :])
        h = x_s[rows, :].astype(F32) + unit * gains[1:2, :]
        h_s[rows, :] = h
        unit, scale = norm_parts(h)
        b_s[rows, :] = (unit * gains[2:3, :]).astype(BF)
    own = pl.ds(pl.multiple_of(me * r, r), r)
    stores = [
        mover.start(b_s, b_out),
        mover.start(u_s.at[own], u_own),
        mover.start(h_s.at[own], h_own),
    ]
    wait_all(up_loads)
    root = math.sqrt(2.0 / math.pi)
    for c in range(H // wide):
        cols = slice(c * wide, c * wide + wide)
        z = dot_nn(b_s[...], up_s[:, cols])
        square = z * z
        bent = jnp.tanh(z * (root + root * 0.044715 * square))
        side = 0.5 + 0.5 * bent
        g_s[:, cols] = (z * side).astype(BF)
        slope = z * (root + 3.0 * root * 0.044715 * square)
        gp_s[:, cols] = (side + (0.5 * slope) * (1.0 - bent * bent)).astype(BF)
    stores += [mover.start(g_s, g_out), mover.start(gp_s, gp_out)]
    wait_all(down_loads)
    for c in range(D // wide):
        cols = slice(c * wide, c * wide + wide)
        m_s[:, cols] = dot_nn(g_s[...], down_s[:, cols]).astype(BF)
    stores += store_rows(mover, m_s, slots, order, me)
    wait_all(stores)


def feed(dims, turn, gains, ff_w, xs, os):
    S, F, r, D, W, H = dims
    L = S * r
    outs = [((L, D), BF), ((r, D), F32), ((r, D), F32), ((L, H), BF), ((L, H), BF)]
    outs += slot_shapes(S, turn, (r, D))
    scratch = [
        pltpu.VMEM((L, D), BF),
        pltpu.VMEM((L, D), BF),
        pltpu.VMEM((D, D), BF),
        pltpu.VMEM((L, D), F32),
        pltpu.VMEM((L, D), F32),
        pltpu.VMEM((D, H), BF),
        pltpu.VMEM((H, D), BF),
        pltpu.VMEM((L, D), BF),
        pltpu.VMEM((L, H), BF),
        pltpu.VMEM((L, H), BF),
        pltpu.VMEM((L, D), BF),
        pltpu.VMEM((8, D), F32),
        pltpu.SemaphoreType.DMA((5 * S + F * (H // W) + 7,)),
    ]
    return call(
        partial(feed_kernel, dims, slot_order(S, turn), turn),
        (gains, ff_w, *xs, *os),
        [any_spec()] * (2 + 2 * S),
        outs,
        [hbm_spec()] * len(outs),
        scratch,
        2 * L * D * D + 4 * L * D * H,
        2 * (D * D + 2 * D * H + 5 * L * D + 2 * L * H),
        "feed",
        limit=56 * 1024 * 1024,
    )


def feed_back_kernel(dims, order, ff_w, gp, *refs):
    S, F, r, D, W, H = dims
    pieces, dm_out, dz_out, refs = refs[:S], *refs[S : S + 2], refs[S + 2 :]
    slots, refs = refs[: len(order)], refs[len(order) :]
    up_s, down_s, gp_s, dm_s, dz_s, part_s, sems = refs
    me = seq_place()
    mover = Mover(sems)
    loads = load_rows(mover, pieces, dm_s, me)
    down_loads = load_down(mover, ff_w, down_s, me, S, F)
    down_loads.append(mover.start(gp, gp_s))
    up_loads = load_up(mover, ff_w, up_s, me, S, F)
    wide = 256
    wait_all(loads)
    stores = [mover.start(dm_s, dm_out)]
    wait_all(down_loads)

    for c in range(H // wide):
        cols = slice(c * wide, c * wide + wide)
        grad = dot_nt(dm_s[...], down_s[cols, :])
        dz_s[:, cols] = (grad * gp_s[:, cols].astype(F32)).astype(BF)
    stores.append(mover.start(dz_s, dz_out))
    wait_all(up_loads)

    for c in range(D // wide):
        cols = slice(c * wide, c * wide + wide)
        part_s[:, cols] = dot_nt(dz_s[...], up_s[cols, :]).astype(BF)
    stores += store_rows(mover, part_s, slots, order, me)
    wait_all(stores)


def feed_back(dims, turn, ff_w, gp, pieces):
    S, F, r, D, W, H = dims
    L = S * r
    outs = [((L, D), BF), ((L, H), BF)] + slot_shapes(S, turn, (r, D))
    scratch = [
        pltpu.VMEM((D, H), BF),
        pltpu.VMEM((H, D), BF),
        pltpu.VMEM((L, H), BF),
        pltpu.VMEM((L, D), BF),
        pltpu.VMEM((L, H), BF),
        pltpu.VMEM((L, D), BF),
        pltpu.SemaphoreType.DMA((3 * S + F * (H // W) + 4,)),
    ]
    return call(
        partial(feed_back_kernel, dims, slot_order(S, turn)),
        (ff_w, gp, *pieces),
        [any_spec()] * (2 + S),
        outs,
        [hbm_spec()] * len(outs),
        scratch,
        4 * L * D * H,
        2 * (2 * D * H + 3 * L * D + 2 * L * H),
        "feed_back",
    )


def feed_outer_kernel(dims, count, *refs):
    S, F, D, W, H = dims
    ins, (out, *held, down_s, up_s, sems) = refs[: 4 * count], refs[4 * count :]
    me = seq_place()
    mover = Mover(sems)
    loads = [mover.start(a, b) for a, b in zip(ins, held)]
    g_rows, dm_rows = held[:count], held[count : 2 * count]
    b_rows, dz_rows = held[2 * count : 3 * count], held[3 * count :]
    wide = 256
    stores = []
    wait_all(loads[: 2 * count])
    for c in range(D // wide):
        total = None
        cols = slice(c * wide, c * wide + wide)
        for b in range(count):
            part = dot_tn(g_rows[b][...], dm_rows[b][:, cols])
            total = part if total is None else total + part
        down_s[:, cols] = total.astype(BF)
    stores += [
        mover.start(down_s.at[b], out.at[a]) for a, b in down_places(D, H, me, S, F)
    ]
    wait_all(loads[2 * count :])
    for c in range(H // wide):
        total = None
        cols = slice(c * wide, c * wide + wide)
        for b in range(count):
            part = dot_tn(b_rows[b][...], dz_rows[b][:, cols])
            total = part if total is None else total + part
        up_s[:, cols] = total.astype(BF)
        piece = pl.ds(c * wide, wide)
        target = piece
        if in_plane(S, F):
            target = pl.ds(pl.multiple_of((me ^ c) * wide, wide), wide)
        stores.append(mover.start(up_s.at[:, piece], out.at[:, target]))
    wait_all(stores)


def feed_outer(dims, b_rows, dz_rows, g_rows, dm_rows):
    S, F, D, W, H = dims
    count = len(b_rows)
    L = b_rows[0].shape[0]
    operands = (*g_rows, *dm_rows, *b_rows, *dz_rows)
    return call(
        partial(feed_outer_kernel, dims, count),
        operands,
        [any_spec()] * len(operands),
        [((D, 2 * H), BF)],
        [hbm_spec()],
        [pltpu.VMEM(x.shape, BF) for x in operands]
        + [
            pltpu.VMEM((H, D), BF),
            pltpu.VMEM((D, H), BF),
            pltpu.SemaphoreType.DMA((4 * count + F * (H // W) + H // 256,)),
        ],
        4 * count * L * D * H,
        2 * (count * 2 * L * (D + H) + 2 * D * H),
        "feed_outer",
    )[0]


def feed_last_kernel(S, F, *refs):
    came, got, (up_out, down_out, held, sems) = refs[:S], refs[S], refs[S + 1 :]
    me = seq_place()
    core = lax.rem(lax.axis_index("fsdp").astype(jnp.int32), 2)
    mover = Mover(sems)
    loads = [mover.start(a, held.at[j]) for j, a in enumerate(came)]
    R, W = up_out.shape[0], up_out.shape[1] // S
    wait_all(loads)
    for slot in range(S):
        start = pl.multiple_of((me ^ slot) * W, W)
        up_out[:, pl.ds(start, W)] = held[slot, 0:R, :].astype(F32)
    near = lax.rem(me, 2) == core
    for k in range(2):
        rows = slice(k * 2 * R, k * 2 * R + 2 * R)
        here = held[me ^ (2 * core + k), R : 3 * R, :]
        down_out[rows, :] = jnp.where(near, here, got[k]).astype(F32)


def feed_last(S, F, came, got):
    R, W = came[0].shape[0] // 3, came[0].shape[1]
    return call(
        partial(feed_last_kernel, S, F),
        (*came, got),
        [any_spec()] * S + [vmem_spec()],
        [((R, S * W), F32), ((4 * R, W), F32)],
        [vmem_spec()] * 2,
        [pltpu.VMEM((S, 3 * R, W), BF), pltpu.SemaphoreType.DMA((S,))],
        R * W * S,
        R * W * 40,
        "feed_last",
    )


def total_of(refs, rows):
    total = None
    for ref in refs:
        value = ref[0, rows, :].astype(F32)
        total = value if total is None else total + value
    return total


def column_sum(v):
    return jnp.sum(v, axis=0, keepdims=True)


def finish_kernel(turn, *refs):
    if turn:
        refs = refs[1:]
    count = (len(refs) - 6) // 2
    ins, (y_hbm, dm_hbm, stat_out), refs = refs[:count], refs[count : count + 3], refs[count + 3 :]
    held, (y_out, dm_out, sems) = refs[: len(ins)], refs[len(ins) :]
    mover = Mover(sems)
    wait_all([mover.start(a, b) for a, b in zip(ins, held)])
    gains, u_ref, h_ref, dy_ref, *terms = held
    half = dm_out.shape[0] // 2
    stats = [None] * 5
    for part in range(2):
        rows = slice(part * half, part * half + half)
        m = total_of(terms, rows)
        unit, scale = norm_parts(m)
        f = unit * gains[3:4, :]
        h = h_ref[rows, :]
        y = h + f
        y_out[rows, :] = y.astype(BF)
        dy = dy_ref[rows, :].astype(F32)
        dm = norm_back(dy * gains[3:4, :], unit, scale)
        dm_out[rows, :] = dm.astype(BF)
        if part == 1:
            stores = [mover.start(dm_out, dm_hbm), mover.start(y_out, y_hbm.at[turn])]
        second, unused = norm_parts(u_ref[rows, :])
        e = second * gains[1:2, :]
        values = [dy * unit, h * h, y * y, e * e, f * f]
        for index, value in enumerate(values):
            value = column_sum(value)
            stats[index] = value if part == 0 else stats[index] + value
    stat_out[...] = jnp.zeros_like(stat_out)
    for index in range(5):
        stat_out[3 + index : 4 + index, :] = stats[index]
    wait_all(stores)


def finish(turn, B, joined, gains, u, h, dy, terms):
    r, D = u.shape
    outs = [((B, r, D), BF), ((r, D), BF), ((8, D), F32)]
    operands = (gains, u, h, dy, *terms)
    first = [] if joined is None else [joined]
    return call(
        partial(finish_kernel, turn),
        (*first, *operands),
        [hbm_spec()] * len(first) + [any_spec()] * len(operands),
        outs,
        [hbm_spec(), hbm_spec(), vmem_spec()],
        [pltpu.VMEM(x.shape, x.dtype) for x in operands]
        + [pltpu.VMEM((r, D), BF)] * 2
        + [pltpu.SemaphoreType.DMA((len(operands) + 2,))],
        60 * r * D,
        r * D * 20,
        "finish",
        {0: 0} if first else {},
    )


def middle_kernel(*refs):
    count = (len(refs) - 6) // 2
    ins, (dh_out, du_hbm, stat_out), refs = refs[:count], refs[count : count + 3], refs[count + 3 :]
    held, (dh_s, du_out, sems) = refs[: len(ins)], refs[len(ins) :]
    mover = Mover(sems)
    wait_all([mover.start(a, b) for a, b in zip(ins, held)])
    gains, u_ref, h_ref, dy_ref, *terms = held
    r, D = u_ref.shape
    half = r // 2
    stats = [None] * 2
    for part in range(2):
        rows = slice(part * half, part * half + half)
        back = total_of(terms, rows)
        unit, scale = norm_parts(h_ref[rows, :])
        third = column_sum(back * unit)
        dh = dy_ref[rows, :].astype(F32) + norm_back(back * gains[2:3, :], unit, scale)
        dh_s[rows, :] = dh
        unit, scale = norm_parts(u_ref[rows, :])
        second = column_sum(dh * unit)
        du_out[rows, :] = norm_back(dh * gains[1:2, :], unit, scale).astype(BF)
        for index, value in enumerate((second, third)):
            stats[index] = value if part == 0 else stats[index] + value
    stores = [mover.start(du_out, du_hbm), mover.start(dh_s, dh_out)]
    stat_out[...] = jnp.zeros_like(stat_out)
    stat_out[1:2, :] = stats[0]
    stat_out[2:3, :] = stats[1]
    wait_all(stores)


def middle(gains, u, h, dy, terms):
    r, D = u.shape
    outs = [((r, D), F32), ((r, D), BF), ((8, D), F32)]
    operands = (gains, u, h, dy, *terms)
    return call(
        middle_kernel,
        operands,
        [any_spec()] * len(operands),
        outs,
        [hbm_spec(), hbm_spec(), vmem_spec()],
        [pltpu.VMEM(x.shape, x.dtype) for x in operands]
        + [
            pltpu.VMEM((r, D), F32),
            pltpu.VMEM((r, D), BF),
            pltpu.SemaphoreType.DMA((len(operands) + 2,)),
        ],
        60 * r * D,
        r * D * 24,
        "middle",
    )


def last_kernel(turn, *refs):
    if turn:
        refs = refs[1:]
    count = (len(refs) - 3) // 2
    ins, joined, held, (out, sems) = refs[:count], refs[count], refs[count + 1 : -2], refs[-2:]
    mover = Mover(sems)
    wait_all([mover.start(a, b) for a, b in zip(ins, held)])
    gains, x_ref, dh_ref, *terms = held
    r, D = x_ref.shape
    half = r // 2
    for part in range(2):
        rows = slice(part * half, part * half + half)
        back = total_of(terms, rows)
        unit, scale = norm_parts(x_ref[rows, :].astype(F32))
        grad = dh_ref[rows, :] + norm_back(back * gains[0:1, :], unit, scale)
        out[rows, :] = grad.astype(BF)
    mover.start(out, joined.at[turn]).wait()


def last(turn, B, joined, gains, x, dh, terms):
    r, D = x.shape
    operands = (gains, x, dh, *terms)
    first = [] if joined is None else [joined]
    return call(
        partial(last_kernel, turn),
        (*first, *operands),
        [hbm_spec()] * len(first) + [any_spec()] * len(operands),
        [((B, r, D), BF)],
        [hbm_spec()],
        [pltpu.VMEM(x.shape, x.dtype) for x in operands]
        + [pltpu.VMEM((r, D), BF), pltpu.SemaphoreType.DMA((len(operands) + 1,))],
        40 * r * D,
        r * D * 14,
        "last",
        {0: 0} if first else {},
    )[0]


def block_groups(F):
    return [[0, 2, 3, 4], [1, 5, 6, 7]] if F == 8 else [list(range(F))]


def out_grad_kernel(dims, count, *refs):
    S, F, D, W = dims
    groups = block_groups(F)
    ins, outs, refs = refs[: (1 + S) * count], refs[(1 + S) * count :], None
    outs, (*held, sum_s, sems) = outs[: len(groups)], outs[len(groups) :]
    mover = Mover(sems)
    o_rows, dus = held[:count], held[count:]
    loads = [mover.start(a, b) for a, b in zip(ins[:count], o_rows)]
    for b in range(count):
        pieces = ins[count + b * S : count + b * S + S]
        loads += load_rows(mover, pieces, dus[b], seq_place())
    R = D // F
    places = block_places(F)
    stores = []
    wait_all(loads)
    total = None
    for b in range(count):
        part = dot_tn(o_rows[b][...], dus[b][...])
        total = part if total is None else total + part
    sum_s[...] = total.astype(BF)
    for group, out in zip(groups, outs):
        for i, index in enumerate(group):
            row = pl.multiple_of(places[index] // S * R, R)
            col = pl.multiple_of(places[index] % S * W, W)
            stores.append(
                mover.start(
                    sum_s.at[pl.ds(row, R), pl.ds(col, W)], out.at[i, pl.ds(3 * R, R)]
                )
            )
    wait_all(stores)


def out_grad(dims, o_rows, dus):
    S, F, D, W = dims
    count = len(o_rows)
    L = o_rows[0].shape[0]
    groups = block_groups(F)
    operands = (*o_rows, *[piece for du in dus for piece in du])
    return call(
        partial(out_grad_kernel, dims, count),
        operands,
        [any_spec()] * len(operands),
        [((len(group), 4 * (D // F) + EXTRA, W), BF) for group in groups],
        [hbm_spec()] * len(groups),
        [pltpu.VMEM(x.shape, BF) for x in o_rows]
        + [pltpu.VMEM((L, D), BF)] * count
        + [pltpu.VMEM((W, D), BF), pltpu.SemaphoreType.DMA(((1 + S) * count + F,))],
        2 * count * L * D * W,
        2 * (count * L * (D + W) + D * W),
        "out_grad",
    )


def qkv_grad_kernel(dims, count, many, *refs):
    S, F, D, W = dims
    groups = block_groups(F)
    n = len(groups)
    stats, refs = refs[n : n + many], refs[n + many :]
    ins, refs = refs[: 2 * count], refs[2 * count :]
    outs, (*held, sum_s, stat_s, sems) = refs[:n], refs[n:]
    held_stats, held = held[:many], held[many:]
    mover = Mover(sems)
    early = [mover.start(a, b) for a, b in zip(stats, held_stats)]
    loads = [mover.start(a, b) for a, b in zip(ins, held)]
    a_rows, grads = held[:count], held[count:]
    R = D // F
    places = [pl.multiple_of(place * R, R) for place in block_places(F)]
    stores = []
    wait_all(early)
    if F == 8:
        total = held_stats[0][...]
        for other in held_stats[1:]:
            total = total + other[...]
        squares = total[4:8, 0:R]
        for i in range(1, F):
            squares = squares + total[4:8, i * R : i * R + R]
        joined = jnp.concatenate([total[0:4], jnp.concatenate([squares] * F, axis=1)], axis=0)
        stat_s[0:8, 0:D] = joined.astype(BF)
        stat_s[8:16, 0:D] = jnp.zeros_like(total).astype(BF)
        for group, out in zip(groups, outs):
            for i, index in enumerate(group):
                stores.append(
                    mover.start(
                        stat_s.at[:, pl.ds(places[index], R)],
                        out.at[i, pl.ds(4 * R, EXTRA), pl.ds(0, R)],
                    )
                )
    wait_all(loads)
    for t in range(3):
        cols = slice(t * W, t * W + W)
        total = None
        for b in range(count):
            part = dot_tn(a_rows[b][...], grads[b][:, cols])
            total = part if total is None else total + part
        sum_s[:, cols] = total.astype(BF)
        for group, out in zip(groups, outs):
            for i, index in enumerate(group):
                stores.append(
                    mover.start(
                        sum_s.at[pl.ds(places[index], R), pl.ds(t * W, W)],
                        out.at[i, pl.ds(t * R, R)],
                    )
                )
    wait_all(stores)


def qkv_grad(dims, parts, stats, a_rows, grads):
    S, F, D, W = dims
    count = len(a_rows)
    L = a_rows[0].shape[0]
    operands = (*parts, *stats, *a_rows, *grads)
    return pl.pallas_call(
        partial(qkv_grad_kernel, dims, count, len(stats)),
        out_shape=tuple(jax.ShapeDtypeStruct(part.shape, part.dtype) for part in parts),
        in_specs=[hbm_spec()] * len(parts) + [any_spec()] * (len(operands) - len(parts)),
        out_specs=tuple([hbm_spec()] * len(parts)),
        input_output_aliases={i: i for i in range(len(parts))},
        scratch_shapes=[pltpu.VMEM(x.shape, x.dtype) for x in (*stats, *a_rows, *grads)]
        + [
            pltpu.VMEM((D, 3 * W), BF),
            pltpu.VMEM((EXTRA, D), BF),
            pltpu.SemaphoreType.DMA((2 * count + len(stats) + 4 * F,)),
        ],
        compiler_params=pltpu.CompilerParams(vmem_limit_bytes=VMEM_LIMIT),
        name="qkv_grad",
    )(*operands)


def deal_qkv_kernel(F, *refs):
    stacks, (one, two, held, sems) = refs[:F], refs[F:]
    me = seq_place()
    rows, cols = one.shape[1], one.shape[2]
    mover = Mover(sems)
    outs = (one, two)
    loads = []
    for i in range(F):
        for slot in (1, 2):
            start = pl.multiple_of(block_at(me, slot) * cols, cols)
            source = stacks[i].at[0, pl.ds(0, rows), pl.ds(start, cols)]
            loads.append(mover.start(source, held.at[slot - 1, i]))
    wait_all(loads)
    wait_all([mover.start(held.at[j], outs[j]) for j in range(2)])


def deal_qkv(R, W, stacks):
    F = len(stacks)
    return call(
        partial(deal_qkv_kernel, F),
        tuple(stacks),
        [any_spec()] * F,
        [((F, R, W), BF)] * 2,
        [hbm_spec()] * 2,
        [pltpu.VMEM((2, F, R, W), BF), pltpu.SemaphoreType.DMA((2 * F + 2,))],
        0,
        8 * F * R * W,
        "deal_qkv",
    )


def pair_sum_kernel(mine, got, *refs):
    outs, (mine_s, got_s, sum_s, sems) = refs[:4], refs[4:]
    mover = Mover(sems)
    loads = []
    for i in range(4):
        loads.append((mover.start(mine.at[i], mine_s.at[i]), mover.start(got.at[i], got_s.at[i])))
    stores = []
    for i in (3, 2, 1, 0):
        wait_all(loads[i])
        sum_s[i] = (mine_s[i].astype(F32) + got_s[i].astype(F32)).astype(BF)
        stores.append(mover.start(sum_s.at[i], outs[i]))
    wait_all(stores)


def pair_sum(mine, got):
    shape = mine.shape[1:]
    return call(
        pair_sum_kernel,
        (mine, got),
        [any_spec()] * 2,
        [(shape, BF)] * 4,
        [hbm_spec()] * 4,
        [pltpu.VMEM(mine.shape, BF)] * 3 + [pltpu.SemaphoreType.DMA((12,))],
        mine.size,
        6 * mine.size,
        "pair_sum",
    )


def last_sum_kernel(S, R, *refs):
    ins, (*moved, out_tile, stat_out), refs = refs[:4], refs[4:9], refs[9:]
    held, (sum_s, sems) = refs[:4], refs[4:]
    mover = Mover(sems)
    wait_all([mover.start(a, b) for a, b in zip(ins, held)])
    total = held[0][...].astype(F32)
    for ref in held[1:]:
        total = total + ref[...].astype(F32)
    sum_s[...] = total.astype(BF)
    stat_out[...] = total[4 * R : 4 * R + 8, 0 : stat_out.shape[1]]
    me = seq_place()
    stores = [mover.start(sum_s.at[pl.ds(3 * R, R)], out_tile)]
    for j in range(3):
        owner = me ^ j
        start = pl.multiple_of(lax.div(3 * owner + block_at(owner, j), S) * R, R)
        stores.append(mover.start(sum_s.at[pl.ds(start, R)], moved[j].at[pl.ds(0, R)]))
        stores.append(
            mover.start(sum_s.at[pl.ds(4 * R, EXTRA)], moved[j].at[pl.ds(R, EXTRA)])
        )
    wait_all(stores)


def last_sum(S, R, terms):
    rows, W = terms[0].shape
    return call(
        partial(last_sum_kernel, S, R),
        tuple(terms),
        [any_spec()] * 4,
        [((R + EXTRA, W), BF)] * 3 + [((R, W), BF), ((8, R), F32)],
        [hbm_spec()] * 4 + [vmem_spec()],
        [pltpu.VMEM((rows, W), BF)] * 5 + [pltpu.SemaphoreType.DMA((11,))],
        4 * rows * W,
        10 * rows * W,
        "last_sum",
    )


def flip(bits, size):
    return [(i, i ^ bits) for i in range(size)]


def add_low(*terms):
    total = terms[0].astype(F32)
    for term in terms[1:]:
        total = total + term.astype(F32)
    return total.astype(BF)


def gather_slots(own, S, me, turn):
    if S != 4:
        full = lax.all_gather(own, "seq")
        return [
            lax.dynamic_index_in_dim(full, me ^ slot, 0, keepdims=False) for slot in range(S)
        ]
    far = lax.ppermute(own, "seq", flip(3, S))
    return [own] + [lax.ppermute(own, "seq", flip(j, S)) for j in (1, 2)] + [far]


def slot_order(S, turn):
    return [[slot] for slot in range(S)]


def slot_shapes(S, turn, shape):
    return [((len(group), *shape), BF) for group in slot_order(S, turn)]


def scatter_slots(groups, S, me, turn):
    if S != 4:
        order = jnp.take(jnp.concatenate(groups), me ^ jnp.arange(S), axis=0)
        return [lax.psum_scatter(order, "seq", scatter_dimension=0, tiled=True)]
    return [groups[0]] + [lax.ppermute(groups[j], "seq", flip(j, S)) for j in (3, 1, 2)]


def swap_slots(pieces, S):
    return [pieces[0]] + [lax.ppermute(pieces[j], "seq", flip(j, S)) for j in range(1, S)]


def sum_everywhere(v, S, F):
    if S != 4 or F != 8:
        return lax.psum(v, ("seq", "fsdp"))
    v = v + lax.ppermute(v, "fsdp", flip(1, F))
    v = v + lax.ppermute(v, "seq", flip(1, S))
    v = v + lax.ppermute(v, "seq", flip(2, S))
    v = v + lax.ppermute(v, "fsdp", flip(2, F))
    return v + lax.ppermute(v, "fsdp", flip(4, F))


def gather_blocks(block, F, early=()):
    if F != 8:
        return [lax.all_gather(block, "fsdp")]
    near = lax.ppermute(block, "fsdp", flip(1, F))
    far = [lax.ppermute(block, "fsdp", flip(j, F)) for j in (2, 4, 6)]
    far = after(far, near, *early)
    rest = [lax.ppermute(piece, "fsdp", flip(1, F)) for piece in far]
    return [piece[None] for piece in (block, near, *far, *rest)]


def after(value, *others):
    return lax.optimization_barrier((value, others))[0]


def blocks_in(blocks, S, me):
    moved = []
    for j in range(3):
        pairs = [(s, (3 * s + j) % S) for s in range(S)]
        moved.append(lax.ppermute(blocks[j], "seq", pairs))
    stack = jnp.stack(moved)
    return [
        lax.dynamic_index_in_dim(stack, (me + S * t) % 3, 0, keepdims=False) for t in range(3)
    ]


def blocks_out_pairs(S, j):
    return [((3 * s + j) % S, s) for s in range(S)]


def blocks_out(stack, S, me):
    moved = []
    for j in range(3):
        t = ((j - me) * (S % 3)) % 3
        piece = lax.dynamic_index_in_dim(stack, t, 0, keepdims=False)
        moved.append(lax.ppermute(piece, "seq", blocks_out_pairs(S, j)))
    return jnp.concatenate(moved, axis=1)


def turn_pairs(S, F):
    each = F // S
    return [
        (s * F + f, (f // each) * F + (f % each) * S + s) for s in range(S) for f in range(F)
    ]


def shards(tokens, cotangent, prefix, qkv_weight, out_weight, up_weight, down_weight, norm_gains):
    S, F = lax.axis_size("seq"), lax.axis_size("fsdp")
    B, r, D = tokens.shape
    heads = D // HEAD // S
    W = D // S
    R = D // F
    H = up_weight.shape[1]
    tiles = H // W
    me = seq_place()
    place = lax.axis_index("fsdp").astype(jnp.int32)
    pairs = turn_pairs(S, F)

    down_late, out_late = down_weight, out_weight
    axes = ("seq", "fsdp")
    if in_plane(S, F):
        gain_rows = jnp.pad(norm_gains, ((0, EXTRA - 4), (0, 3 * W - R)))
        first_block = jnp.concatenate([qkv_weight, gain_rows])
        near_block = lax.ppermute(first_block, "fsdp", flip(1, F))
        far = [lax.ppermute(first_block, "fsdp", flip(j, F)) for j in (2, 4, 6)]
        core = place % 2
        other = lax.ppermute(down_late, "fsdp", flip(1, F))
        halves = jnp.concatenate([down_late, other]).reshape(4, 2 * R, W)
        sent = []
        for j in range(S):
            target = me ^ j
            index = jnp.where(target // 2 == core, 0, 2) + target % 2
            piece = lax.dynamic_index_in_dim(halves, index, 0, keepdims=False)
            up_tile = lax.dynamic_slice_in_dim(up_weight, target * W, W, 1)
            sent.append(jnp.concatenate([up_tile, piece, out_late]))
        came, far, near_block = lax.optimization_barrier((swap_slots(sent, S), far, near_block))
        ups = [message[:R] for message in came]
        out_tiles = [message[3 * R :] for message in came]
        near = (me % 2) ^ core == 0
        pieces = [
            jnp.where(near, came[2 * i][R : 3 * R], came[2 * i + 1][R : 3 * R])
            for i in range(2)
        ]
        downs = [piece[t * R : t * R + R] for piece in pieces for t in range(2)]
    else:
        ups = [up_weight]
        down_mine = lax.ppermute(down_late, axes, pairs)
        downs = [down_mine[i * R : i * R + R] for i in range(tiles)]
        out_tiles = gather_slots(out_late, S, me, 0)
    ff_mine = jnp.concatenate([*ups, *downs, *out_tiles], axis=1)
    if in_plane(S, F):
        rest = [lax.ppermute(piece, "fsdp", flip(1, F)) for piece in far]
        stacks = [piece[None] for piece in (first_block, near_block, *far, *rest)]
        one, two = deal_qkv(R, W, stacks)
        one = lax.ppermute(one, "seq", flip(1, S))
        two = lax.ppermute(two, "seq", flip(2, S))
        all_x = [gather_slots(tokens[:1], S, me, 0)]
        all_x += [gather_slots(after(tokens[b : b + 1], one, two), S, me, 0) for b in range(1, B)]
        stacks = [*stacks, one, two]
    else:
        blocks = [qkv_weight[:, j * W : j * W + W] for j in range(3)]
        all_x = [gather_slots(tokens[b : b + 1], S, me, 0) for b in range(B)]
        stacks = gather_blocks(jnp.concatenate(blocks_in(blocks, S, me)), F)
    if in_plane(S, F):
        pass
    ff_full = lax.all_gather(ff_mine, "fsdp", axis=0, tiled=True)
    gains = None
    if F != 8:
        gains = lax.all_gather(norm_gains, "fsdp", axis=1, tiled=True).astype(F32)
        gains = jnp.pad(gains, ((0, 4), (0, 0)))
    att_dims = (S, F, r, D, heads)
    ff_dims = (S, F, r, D, W, H)
    a_all, qkv_all, p_all, os, os_own = [], [], [], [], []
    for b in range(B):
        a, qkv, o, p, gains_full = attend(att_dims, b, prefix, gains, stacks, all_x[b])
        a_all.append(a)
        qkv_all.append(qkv)
        p_all.append(p)
        os_own.append(o)
        os.append(gather_slots(o, S, me, b))
    gains = gains_full
    b_all, u_own, h_own, g_all, gp_all, m_terms = [], [], [], [], [], []
    for b in range(B):
        res = feed(ff_dims, b, gains, ff_full, all_x[b], os[b])
        b_all.append(res[0])
        u_own.append(res[1])
        h_own.append(res[2])
        g_all.append(res[3])
        gp_all.append(res[4])
        m_terms.append(scatter_slots(list(res[5:]), S, me, b))
    y, stats, dms = None, [], []
    for b in range(B):
        y, dm, stat = finish(b, B, y, gains, u_own[b], h_own[b], cotangent[b], m_terms[b])
        stats.append(stat)
        dms.append(gather_slots(dm, S, me, b))
    dm_all, dz_all, h_terms = [], [], []
    for b in range(B):
        res = feed_back(ff_dims, b, ff_full, gp_all[b], dms[b])
        dm_all.append(res[0])
        dz_all.append(res[1])
        h_terms.append(scatter_slots(list(res[2:]), S, me, b))
    dhs, dus = [], []
    for b in range(B):
        dh, du, stat = middle(gains, u_own[b], h_own[b], cotangent[b], h_terms[b])
        dhs.append(dh)
        dus.append(gather_slots(du, S, me, b))
        stats.append(stat)
    dm_all = after(dm_all, h_terms[0])
    ff_part = feed_outer((S, F, D, W, H), b_all, dz_all, g_all, dm_all)
    ff_sum = lax.psum_scatter(ff_part, "fsdp", scatter_dimension=0, tiled=True)
    back_pairs = [(b, a) for a, b in pairs]
    if not in_plane(S, F):
        down_sum = jnp.concatenate(
            [ff_sum[:, H + i * W : H + i * W + W] for i in range(tiles)], axis=0
        )
        down_grad = lax.ppermute(down_sum, axes, back_pairs).astype(F32)
        up_grad = ff_sum[:, :H].astype(F32)
    dqkvs, x_terms = [], []
    for b in range(B):
        res = attend_back(
            att_dims, b, gains, ff_full, stacks, a_all[b], qkv_all[b], p_all[b], dus[b]
        )
        dqkvs.append(res[0])
        stats.append(res[1])
        x_terms.append(scatter_slots(list(res[2:]), S, me, b))
    grad_dims = (S, F, D, W)
    parts = after(out_grad(grad_dims, os_own, dus), dqkvs)
    parts = after(parts, x_terms[0])
    parts = qkv_grad(grad_dims, parts, stats, a_all, dqkvs)
    if F == 8 and S == 4:
        kept = pair_sum(parts[0], lax.ppermute(parts[1], "fsdp", flip(1, F)))
        ff_sum = after(ff_sum, kept)
        got = [lax.ppermute(kept[j], "fsdp", flip(2 * j, F)) for j in (3, 2, 1)]
        pieces = [ff_sum[:, H + i * W : H + i * W + W] for i in range(4)]
        sent = [
            jnp.concatenate([ff_sum[:, j * W : j * W + W], *pieces[j // 2 * 2 : j // 2 * 2 + 2]])
            for j in range(S)
        ]
        came = swap_slots(sent, S)
        got = after(got, came)
        whole = jnp.stack(came)[:, R:]
        away = jnp.stack(
            [
                lax.dynamic_index_in_dim(whole, me ^ (2 * (1 - place % 2) + k), 0, keepdims=False)
                for k in range(2)
            ]
        )
        up_grad, down_grad = feed_last(S, F, came, lax.ppermute(away, "fsdp", flip(1, F)))
        *moved, out_tile, stat = last_sum(S, R, [kept[0], *got])
        moved[1:] = [lax.ppermute(moved[j], "seq", flip(j, S)) for j in (1, 2)]
        missed = lax.ppermute(stat, "seq", flip(3, S))
        for piece in moved:
            missed = missed + piece[R : R + 8, :R].astype(F32)
        odd = me % 2 == 1
        ends = (moved[0][:R], moved[2][:R])
        qkv_own = jnp.concatenate(
            [jnp.where(odd, ends[1], ends[0]), moved[1][:R], jnp.where(odd, ends[0], ends[1])],
            axis=1,
        )
        gains_grad, squares = missed[:4], jnp.sum(missed[4:], axis=1)
    else:
        rest = lax.psum_scatter(parts[0], "fsdp", scatter_dimension=0, tiled=False)
        qkv_own = blocks_out(jnp.stack([rest[t * R : t * R + R] for t in range(3)]), S, me)
        out_tile = rest[3 * R : 4 * R]
        totals = lax.psum(sum(stats), ("seq", "fsdp"))
        gains_grad = lax.dynamic_slice_in_dim(totals[:4], place * R, R, 1)
        squares = jnp.sum(totals[4:], axis=1)
    input_grad = None
    for b in range(B):
        input_grad = last(b, B, input_grad, gains, tokens[b], dhs[b], x_terms[b])

    out_own = lax.ppermute(out_tile, ("seq", "fsdp"), back_pairs)
    entries = B * r * D * S * F
    stream_rms = jnp.sqrt(squares / entries)
    return (
        y,
        input_grad,
        qkv_own.astype(F32),
        out_own.astype(F32),
        up_grad,
        down_grad,
        gains_grad,
        stream_rms,
    )


def solution(mesh):
    in_specs = (
        P("fsdp", "seq", None),
        P("fsdp", "seq", None),
        P("fsdp"),
        P("fsdp", "seq"),
        P("fsdp", "seq"),
        P("fsdp", "seq"),
        P("fsdp", "seq"),
        P(None, "fsdp"),
    )
    out_specs = (
        P("fsdp", "seq", None),
        P("fsdp", "seq", None),
        P("fsdp", "seq"),
        P("fsdp", "seq"),
        P("fsdp", "seq"),
        P("fsdp", "seq"),
        P(None, "fsdp"),
        P(),
    )
    return jax.shard_map(shards, mesh=mesh, in_specs=in_specs, out_specs=out_specs, check_vma=False)
```
